32 devices in a mesh: dp: 16 (over z, y, core), tensor: 2 (over x).
Axes of the slice: x: 2, y: 2, z: 4, core: 2. Of those that a mesh axis runs over, the one named last changes fastest.
Arguments:
- tokens: bfloat16 [32, 512, 768], P('dp', 'tensor')
- prob_masks: int32 [2, 32, 12, 512, 40], P(None, 'dp', 'tensor'), may hold values from 0 to 8191, as said below
- branch_masks: int32 [2, 2, 32, 512, 52], P(None, None, 'dp', 'tensor'), may hold values from 0 to 32767, as said below
- attn_weight: float32 [768, 3, 768], P('dp', None, 'tensor'), may hold values from -0.21875 to 0.21875
- attn_first: float32 [768, 3, 768], P('dp', None, 'tensor'), may hold values from -3.0517578e-05 to 3.0517578e-05
- attn_second: float32 [768, 3, 768], P('dp', None, 'tensor'), may hold values from 1.159668e-12 to 1.8615722e-11
- out_weight: float32 [768, 768], P('tensor', 'dp'), may hold values from -0.4375 to 0.4375
- out_first: float32 [768, 768], P('tensor', 'dp'), may hold values from -3.0517578e-05 to 3.0517578e-05
- out_second: float32 [768, 768], P('tensor', 'dp'), may hold values from 1.159668e-12 to 1.8615722e-11
- up_weight: float32 [768, 3072], P('dp', 'tensor'), may hold values from -0.21875 to 0.21875
- up_first: float32 [768, 3072], P('dp', 'tensor'), may hold values from -3.0517578e-05 to 3.0517578e-05
- up_second: float32 [768, 3072], P('dp', 'tensor'), may hold values from 1.159668e-12 to 1.8615722e-11
- down_weight: float32 [3072, 768], P('tensor', 'dp'), may hold values from -0.109375 to 0.109375
- down_first: float32 [3072, 768], P('tensor', 'dp'), may hold values from -3.0517578e-05 to 3.0517578e-05
- down_second: float32 [3072, 768], P('tensor', 'dp'), may hold values from 1.159668e-12 to 1.8615722e-11
- gains: float32 [2, 768], replicated, may hold values from 0.5 to 1.5
- gains_first: float32 [2, 768], replicated, may hold values from -0.00012207031 to 0.00012207031
- gains_second: float32 [2, 768], replicated, may hold values from 1.8615722e-11 to 2.9907227e-10
- shifts: float32 [6, 768], replicated, may hold values from -1.25 to 1.25
- shifts_first: float32 [6, 768], replicated, may hold values from -0.00012207031 to 0.00012207031
- shifts_second: float32 [6, 768], replicated, may hold values from 1.8615722e-11 to 2.9907227e-10
- hidden_bias: float32 [3072], replicated, may hold values from -1.25 to 1.25
- hidden_first: float32 [3072], replicated, may hold values from -0.00012207031 to 0.00012207031
- hidden_second: float32 [3072], replicated, may hold values from 1.8615722e-11 to 2.9907227e-10
Outputs:
- loss: float32 [], replicated
- grad_tokens: float32 [32, 512, 768], P('dp', 'tensor')
- new_attn: float32 [768, 3, 768], P('dp', None, 'tensor')
- new_attn_first: float32 [768, 3, 768], P('dp', None, 'tensor')
- new_attn_second: float32 [768, 3, 768], P('dp', None, 'tensor')
- new_out: float32 [768, 768], P('tensor', 'dp')
- new_out_first: float32 [768, 768], P('tensor', 'dp')
- new_out_second: float32 [768, 768], P('tensor', 'dp')
- new_up: float32 [768, 3072], P('dp', 'tensor')
- new_up_first: float32 [768, 3072], P('dp', 'tensor')
- new_up_second: float32 [768, 3072], P('dp', 'tensor')
- new_down: float32 [3072, 768], P('tensor', 'dp')
- new_down_first: float32 [3072, 768], P('tensor', 'dp')
- new_down_second: float32 [3072, 768], P('tensor', 'dp')
- new_gains: float32 [2, 768], replicated
- new_gains_first: float32 [2, 768], replicated
- new_gains_second: float32 [2, 768], replicated
- new_shifts: float32 [6, 768], replicated
- new_shifts_first: float32 [6, 768], replicated
- new_shifts_second: float32 [6, 768], replicated
- new_hidden: float32 [3072], replicated
- new_hidden_first: float32 [3072], replicated
- new_hidden_second: float32 [3072], replicated
The draws below stay inside these ranges and needn't reach their ends.
Inputs may be any that keep to these rules, and one draw needn't show every extreme that they name: `prob_masks`: each word holds 13 keep bits for 13 consecutive keys, bit b of word w for key 13 w + b; bits for keys at 512 or past are zero. `branch_masks`: each word holds 15 keep bits for 15 consecutive features, bit b of word w for feature 15 w + b; bits for features at 768 or past are zero.
All inputs are finite; a program needn't handle non-finite values.
Results may differ from the reference program's by a relative error of at most 0.009.
Values may be sent and summed in bfloat16 or wider, within the bound.
No kernel may reach another device: no remote copies, remote signals or barrier semaphores. Data moves between devices by JAX's collectives and lax.ppermute only.
A program may use at most 192 MiB of HBM per device.

```python
import math
import jax
import jax.numpy as jnp
from jax import lax

D = 768
HEADS = 12
HD = 64
FF = 3072
LEN = 512
STEP = 10
SEQS = 32
KW = 40
BW = 52
LOSS_SCALE = 1048576


def draw_tokens(key, part):
    common = jax.random.normal(jax.random.fold_in(key, 11), (LEN, D), jnp.float32)
    noise = 0.6 * jax.random.normal(key, (SEQS, LEN, D), jnp.float32)
    return (common[None] + noise).astype(jnp.bfloat16)


def packed_keep(key, leading, width_in, word_count, word_bits):
    raw = jax.random.randint(key, leading + (word_count, word_bits), 0, 10)
    places = jnp.arange(word_count * word_bits, dtype=jnp.int32).reshape(word_count, word_bits)
    alive = jnp.logical_and(raw < 9, places < width_in).astype(jnp.int32)
    powers = jnp.left_shift(jnp.int32(1), jnp.arange(word_bits, dtype=jnp.int32))
    return jnp.sum(alive * powers, axis=-1).astype(jnp.int32)


def draw_prob_masks(key, part):
    blocks = lax.map(lambda index: packed_keep(jax.random.fold_in(key, index), (2, HEADS, LEN), LEN, KW, 13), jnp.arange(SEQS, dtype=jnp.int32))
    return jnp.moveaxis(blocks, 0, 1)


def draw_branch_masks(key, part):
    blocks = lax.map(lambda index: packed_keep(jax.random.fold_in(key, index), (2, 2, LEN), D, BW, 15), jnp.arange(SEQS, dtype=jnp.int32))
    return jnp.moveaxis(blocks, 0, 2)


def levels(own_key, dims, cuts, smallest, largest):
    def one(dim, parts):
        draws = jax.random.uniform(jax.random.fold_in(jax.random.fold_in(own_key, 6), dim), (parts,), jnp.float32, smallest / len(cuts), largest / len(cuts))
        return jnp.repeat(jnp.exp(draws), dims[dim] // parts).reshape((-1,) + (1,) * (len(dims) - dim - 1))

    loudness = one(*cuts[0])
    for cut in cuts[1:]:
        loudness = loudness * one(*cut)
    return loudness


def scatter_about(rng, shape, scale, reach, pieces=(), held_as=jnp.bfloat16):
    values = scale * jax.random.normal(rng, shape, jnp.float32)
    if pieces:
        values = values * levels(rng, shape, pieces, -0.22, 0.18)
    return jnp.clip(values, -reach, reach).astype(held_as)


def setup_inputs(seed: int = 0) -> dict:
    streams_of = jax.random.split(jax.random.key(seed), 25)
    tokens = draw_tokens(jax.random.fold_in(streams_of[24], 71), 0)
    prob_masks = draw_prob_masks(jax.random.fold_in(streams_of[24], 71), 0)
    branch_masks = draw_branch_masks(jax.random.fold_in(streams_of[24], 71), 0)
    attn_weight = scatter_about(streams_of[3], (D, 3, D), D ** -0.5, 0.21875, ((0, 16), (2, 2)), jnp.float32)
    attn_first = scatter_about(streams_of[4], (D, 3, D), (0.00097 / (2 * SEQS * LEN) ** 0.5), 3.0517578125e-05, ((0, 16), (2, 2)), jnp.float32)
    attn_second = jnp.clip(jnp.exp(math.log(1.861572181127702e-11) - 2.7758728 * jax.random.uniform(streams_of[5], (D, 3, D), jnp.float32) ** levels(streams_of[5], (D, 3, D), ((0, 16), (2, 2)), -0.2, 0.2)), 1.1596679562811407e-12, 1.861572181127702e-11)
    out_weight = scatter_about(streams_of[6], (D, D), (D // 4) ** -0.5, 0.4375, ((0, 2), (1, 16)), jnp.float32)
    out_first = scatter_about(streams_of[7], (D, D), (0.00097 / (2 * SEQS * LEN) ** 0.5), 3.0517578125e-05, ((0, 2), (1, 16)), jnp.float32)
    out_second = jnp.clip(jnp.exp(math.log(1.861572181127702e-11) - 2.7758728 * jax.random.uniform(streams_of[8], (D, D), jnp.float32) ** levels(streams_of[8], (D, D), ((0, 2), (1, 16)), -0.2, 0.2)), 1.1596679562811407e-12, 1.861572181127702e-11)
    up_weight = scatter_about(streams_of[9], (D, FF), D ** -0.5, 0.21875, ((0, 16), (1, 2)), jnp.float32)
    up_first = scatter_about(streams_of[10], (D, FF), (0.00097 / (2 * SEQS * LEN) ** 0.5), 3.0517578125e-05, ((0, 16), (1, 2)), jnp.float32)
    up_second = jnp.clip(jnp.exp(math.log(1.861572181127702e-11) - 2.7758728 * jax.random.uniform(streams_of[11], (D, FF), jnp.float32) ** levels(streams_of[11], (D, FF), ((0, 16), (1, 2)), -0.2, 0.2)), 1.1596679562811407e-12, 1.861572181127702e-11)
    down_weight = scatter_about(streams_of[12], (FF, D), FF ** -0.5, 0.109375, ((0, 2), (1, 16)), jnp.float32)
    down_first = scatter_about(streams_of[13], (FF, D), (0.00097 / (2 * SEQS * LEN) ** 0.5), 3.0517578125e-05, ((0, 2), (1, 16)), jnp.float32)
    down_second = jnp.clip(jnp.exp(math.log(1.861572181127702e-11) - 2.7758728 * jax.random.uniform(streams_of[14], (FF, D), jnp.float32) ** levels(streams_of[14], (FF, D), ((0, 2), (1, 16)), -0.2, 0.2)), 1.1596679562811407e-12, 1.861572181127702e-11)
    gains = jnp.clip(1.0 + 0.1 * jax.random.normal(streams_of[15], (2, D), jnp.float32), 0.5, 1.5)
    gains_first = scatter_about(streams_of[16], (2, D), (0.0039 / (2 * SEQS * LEN) ** 0.5), 0.00012207031, (), jnp.float32)
    gains_second = jnp.clip(jnp.exp(jax.random.uniform(streams_of[17], (2, D), jnp.float32, math.log(1.861572181127702e-11), math.log(2.990722669515833e-10))), 1.861572181127702e-11, 2.990722669515833e-10)
    shifts = scatter_about(streams_of[18], (6, D), 0.2, 1.25, (), jnp.float32)
    shifts_first = scatter_about(streams_of[19], (6, D), (0.0039 / (2 * SEQS * LEN) ** 0.5), 0.00012207031, (), jnp.float32)
    shifts_second = jnp.clip(jnp.exp(jax.random.uniform(streams_of[20], (6, D), jnp.float32, math.log(1.861572181127702e-11), math.log(2.990722669515833e-10))), 1.861572181127702e-11, 2.990722669515833e-10)
    hidden_bias = scatter_about(streams_of[21], (FF,), 0.2, 1.25, (), jnp.float32)
    hidden_first = scatter_about(streams_of[22], (FF,), (0.0039 / (2 * SEQS * LEN) ** 0.5), 0.00012207031, (), jnp.float32)
    hidden_second = jnp.clip(jnp.exp(jax.random.uniform(streams_of[23], (FF,), jnp.float32, math.log(1.861572181127702e-11), math.log(2.990722669515833e-10))), 1.861572181127702e-11, 2.990722669515833e-10)
    return dict(tokens=tokens, prob_masks=prob_masks, branch_masks=branch_masks, attn_weight=attn_weight, attn_first=attn_first, attn_second=attn_second, out_weight=out_weight, out_first=out_first, out_second=out_second, up_weight=up_weight, up_first=up_first, up_second=up_second, down_weight=down_weight, down_first=down_first, down_second=down_second, gains=gains, gains_first=gains_first, gains_second=gains_second, shifts=shifts, shifts_first=shifts_first, shifts_second=shifts_second, hidden_bias=hidden_bias, hidden_first=hidden_first, hidden_second=hidden_second)


@jax.custom_vjp
def low(v):
    return lax.optimization_barrier(v.astype(jnp.bfloat16)).astype(jnp.float32)

@jax.custom_vjp
def low_back(v):
    return v

def low_keep(v):
    return (low(v), None)

def low_pass(kept, grad):
    return (grad,)

def back_keep(v):
    return (v, None)

def back_low(kept, grad):
    return (low(grad),)
low.defvjp(low_keep, low_pass)
low_back.defvjp(back_keep, back_low)

def unpack(packed, length, word_bits):
    places = jnp.arange(word_bits, dtype=jnp.int32)
    bit_flags = jnp.bitwise_and(jnp.right_shift(packed[..., None], places), 1)
    bit_flags = bit_flags.reshape(packed.shape[:-1] + (packed.shape[-1] * word_bits,))
    return bit_flags[..., :length].astype(jnp.float32) * (1.0 / 0.9)

def layer_norm(values_in, gain_row, shift_row):
    center = values_in - lax.optimization_barrier(jnp.mean(values_in, axis=-1, keepdims=True))
    spread = lax.optimization_barrier(jnp.mean(center * center, axis=-1, keepdims=True))
    return center * lax.rsqrt(spread + 1e-12) * gain_row + shift_row

def contrastive(pooled):
    unit_rows = pooled * lax.rsqrt(lax.optimization_barrier(jnp.sum(pooled * pooled, axis=-1, keepdims=True)) + 1e-06)
    logits = jnp.dot(unit_rows[0], unit_rows[1].T, precision=lax.Precision.HIGHEST) * 20.0
    return jnp.mean(jax.nn.logsumexp(logits, axis=1) - jnp.diagonal(logits))

def hdot(left_side, right_side):
    return jnp.dot(left_side, right_side, precision=lax.Precision.HIGHEST)

def adam_direction(weight, gradient, first_moment, second, decay_rate):
    new_first = 0.9 * first_moment + 0.1 * gradient
    new_second = 0.999 * second + 0.001 * gradient * gradient
    first_hat = new_first / (1.0 - 0.9 ** STEP)
    second_hat = new_second / (1.0 - 0.999 ** STEP)
    update = first_hat / (jnp.sqrt(second_hat) + 1e-06) + decay_rate * weight
    return (new_first, new_second, update)

def reference(tokens, prob_masks, branch_masks, attn_weight, attn_first, attn_second, out_weight, out_first, out_second, up_weight, up_first, up_second, down_weight, down_first, down_second, gains, gains_first, gains_second, shifts, shifts_first, shifts_second, hidden_bias, hidden_first, hidden_second):
    token_rows = tokens.astype(jnp.float32)
    mask_words = jnp.moveaxis(prob_masks, 1, 0)
    branch_words = jnp.moveaxis(branch_masks, 2, 0)

    def forward(token_rows, attn_weight, out_weight, up_weight, down_weight, gains, shifts, hidden_bias):
        attn_matrix = low(attn_weight).reshape(D, 3 * D)
        out_matrix = low(out_weight)
        up_matrix = low(up_weight)
        down_matrix = low(down_weight)
        qkv_bias = jnp.stack([shifts[0], jnp.zeros((D,), jnp.float32), shifts[1]])

        def one_sequence(sequence_items):
            seq_rows, prob_words, branch = sequence_items
            projected = hdot(seq_rows, attn_matrix).reshape(LEN, 3, D) + qkv_bias
            projected = low_back(low(projected))
            queries = projected[:, 0].reshape(LEN, HEADS, HD)
            key_rows = projected[:, 1].reshape(LEN, HEADS, HD)
            values = projected[:, 2].reshape(LEN, HEADS, HD)
            scores = low_back(jnp.einsum('qhd,khd->hqk', queries, key_rows, precision=lax.Precision.HIGHEST) * 0.125)
            attn_probs = jax.nn.softmax(scores, axis=-1)
            pooled = []
            for view_index in range(2):
                weighted = low(attn_probs * unpack(prob_words[view_index], LEN, 13))
                context = jnp.einsum('hqk,khd->qhd', weighted, values, precision=lax.Precision.HIGHEST)
                context = low_back(low(context)).reshape(LEN, D)
                attn_out = low_back(hdot(context, out_matrix) + shifts[2])
                normed = layer_norm(seq_rows + attn_out * unpack(branch[0, view_index], D, 15), gains[0], shifts[3])
                hidden_pre = low_back(hdot(low(normed), up_matrix) + hidden_bias)
                active = low(jax.nn.gelu(hidden_pre, approximate=False))
                ffn_out = low_back(hdot(active, down_matrix) + shifts[4])
                output = layer_norm(normed + ffn_out * unpack(branch[1, view_index], D, 15), gains[1], shifts[5])
                pooled.append(lax.optimization_barrier(jnp.mean(output, axis=0)))
            return jnp.stack(pooled)
        pooled_all = lax.map(jax.checkpoint(one_sequence), (token_rows, mask_words, branch_words))
        return contrastive(jnp.moveaxis(pooled_all, 0, 1)) * jnp.float32(LOSS_SCALE)
    scaled, backward = jax.vjp(forward, token_rows, attn_weight, out_weight, up_weight, down_weight, gains, shifts, hidden_bias)
    gradients = backward(jnp.float32(1.0))
    loss_value = scaled / jnp.float32(LOSS_SCALE)
    inverse = 1.0 / jnp.float32(LOSS_SCALE)

    def matrix_step(weight, gradient, first_moment, second, axes):
        new_first, new_second, update = adam_direction(weight, gradient * inverse, first_moment, second, 0.01)
        trust_ratio = jnp.sqrt(lax.optimization_barrier(jnp.sum(weight * weight, axis=axes, keepdims=True))) / jnp.sqrt(lax.optimization_barrier(jnp.sum(update * update, axis=axes, keepdims=True)))
        return (weight - 0.25 * trust_ratio * update, new_first, new_second)

    def small_step(weight, gradient, first_moment, second):
        new_first, new_second, update = adam_direction(weight, gradient * inverse, first_moment, second, 0.0)
        trust_ratio = jnp.sqrt(lax.optimization_barrier(jnp.sum(weight * weight, axis=-1, keepdims=True))) / jnp.sqrt(lax.optimization_barrier(jnp.sum(update * update, axis=-1, keepdims=True)))
        return (weight - 0.25 * trust_ratio * update, new_first, new_second)
    new_attn, new_attn_first, new_attn_second = matrix_step(attn_weight, gradients[1], attn_first, attn_second, (0, 2))
    new_out, new_out_first, new_out_second = matrix_step(out_weight, gradients[2], out_first, out_second, (0, 1))
    new_up, new_up_first, new_up_second = matrix_step(up_weight, gradients[3], up_first, up_second, (0, 1))
    new_down, new_down_first, new_down_second = matrix_step(down_weight, gradients[4], down_first, down_second, (0, 1))
    new_gains, new_gains_first, new_gains_second = small_step(gains, gradients[5], gains_first, gains_second)
    new_shifts, new_shifts_first, new_shifts_second = small_step(shifts, gradients[6], shifts_first, shifts_second)
    new_hidden, new_hidden_first, new_hidden_second = small_step(hidden_bias, gradients[7], hidden_first, hidden_second)
    return (loss_value, gradients[0], new_attn, new_attn_first, new_attn_second, new_out, new_out_first, new_out_second, new_up, new_up_first, new_up_second, new_down, new_down_first, new_down_second, new_gains, new_gains_first, new_gains_second, new_shifts, new_shifts_first, new_shifts_second, new_hidden, new_hidden_first, new_hidden_second)
```

```python
import functools

import jax
import jax.numpy as jnp
import numpy as np
from jax import lax
from jax.experimental import pallas as pl
from jax.experimental.pallas import tpu as pltpu
from jax.sharding import PartitionSpec as P

HD = 64
STEP = 10
KEEP_SCALE = 1.0 / 0.9
PROB_BITS = 13
BRANCH_BITS = 15
LOW_BITS = 7
BF = jnp.bfloat16
F32 = jnp.float32
EXACT = lax.Precision.HIGHEST
VMEM_LIMIT = 56 << 20


def dot(left, right, left_dim, right_dim, precision=None):
    return lax.dot_general(
        left,
        right,
        (((left_dim,), (right_dim,)), ((), ())),
        preferred_element_type=F32,
        precision=precision,
    )


def swap_dp(value, distance):
    count = lax.axis_size("dp")
    return lax.ppermute(value, "dp", [(i, i ^ distance) for i in range(count)])


def swap_tensor(value):
    return lax.ppermute(value, "tensor", [(0, 1), (1, 0)])


def bit_groups(count):
    bits = count.bit_length() - 1
    groups, top = [], bits
    while top - 2 >= 2:
        groups.append((top - 2, top - 1))
        top -= 2
    while top > 0:
        groups.append((top - 1,))
        top -= 1
    return groups


def distances(group):
    out = [0]
    for bit in group:
        out = out + [o | (1 << bit) for o in out]
    return out


def gathered_order(count):
    order = [0]
    for group in bit_groups(count):
        order = [o | step for step in distances(group) for o in order]
    return order


def joined_kernel(spans, *refs):
    count = len(refs) - 1 - len(spans)
    pieces, out_refs, arrived = refs[:count], refs[count:-1], refs[-1]
    copies, start = [], 0
    for index, piece in enumerate(pieces):
        rows = piece.shape[0]
        for place, (first, last) in enumerate(spans):
            copies.append(
                pltpu.make_async_copy(
                    piece.at[:, pl.ds(first, last - first)],
                    out_refs[place].at[pl.ds(start, rows)],
                    arrived.at[index, place],
                )
            )
        start += rows
    for copy in copies:
        copy.start()
    for copy in copies:
        copy.wait()


def joined(pieces, spans=None):
    rows = sum(piece.shape[0] for piece in pieces)
    columns = pieces[0].shape[1]
    parts = spans or ((0, columns),)
    if any(piece.shape[0] % 16 for piece in pieces):
        whole = jnp.concatenate(pieces, axis=0)
        return [whole[:, first:last] for first, last in parts] if spans else whole
    out = pl.pallas_call(
        functools.partial(joined_kernel, parts),
        in_specs=[pl.BlockSpec(memory_space=pl.ANY)] * len(pieces),
        out_specs=[pl.BlockSpec(memory_space=pltpu.VMEM)] * len(parts),
        out_shape=[
            jax.ShapeDtypeStruct((rows, last - first), pieces[0].dtype) for first, last in parts
        ],
        scratch_shapes=[pltpu.SemaphoreType.DMA((len(pieces), len(parts)))],
        compiler_params=pltpu.CompilerParams(vmem_limit_bytes=VMEM_LIMIT),
        name="joined",
    )(*pieces)
    return out if spans else out[0]


def picked_kernel(places_ref, blocks_ref, own_ref, other_ref, arrived):
    count = own_ref.shape[0]
    copies = []
    for half, out_ref in enumerate((own_ref, other_ref)):
        for index in range(count):
            copies.append(
                pltpu.make_async_copy(
                    blocks_ref.at[places_ref[half, index]],
                    out_ref.at[index],
                    arrived.at[half, index],
                )
            )
    for copy in copies:
        copy.start()
    for copy in copies:
        copy.wait()


def picked(blocks, places):
    _, rows, columns = blocks.shape
    count = places.shape[1]
    if rows % 16:
        return [blocks[places[half]].reshape(count * rows, columns) for half in range(2)]
    out = pl.pallas_call(
        picked_kernel,
        in_specs=[
            pl.BlockSpec(memory_space=pltpu.SMEM),
            pl.BlockSpec(memory_space=pl.ANY),
        ],
        out_specs=[pl.BlockSpec(memory_space=pltpu.VMEM)] * 2,
        out_shape=[jax.ShapeDtypeStruct((count, rows, columns), blocks.dtype)] * 2,
        scratch_shapes=[pltpu.SemaphoreType.DMA((2, count))],
        compiler_params=pltpu.CompilerParams(vmem_limit_bytes=VMEM_LIMIT),
        name="picked",
    )(places, blocks)
    return [half.reshape(count * rows, columns) for half in out]


def tie(value, *others):
    return lax.optimization_barrier((value,) + others)[0]


def together(*values):
    return lax.optimization_barrier(values)


def upper_groups():
    return bit_groups(lax.axis_size("dp"))[:-2]


def gather_upper(block):
    for group in upper_groups():
        block = joined([block] + [swap_dp(block, s) for s in distances(group)[1:]])
    return block


def gather_sides(mine, corner_by_tensor):
    beside = swap_dp(mine, 2)
    across = swap_tensor(mine)
    corner = swap_tensor(beside) if corner_by_tensor else swap_dp(across, 2)
    return (mine, beside), (across, corner)


def gather_core(quarters, spans=None):
    near, far = quarters
    return joined([near, far, swap_dp(near, 1), swap_dp(far, 1)], spans)


def reduce_upper(parts):
    for group in reversed(upper_groups()):
        steps = distances(group)
        rows = parts[0].shape[0] // len(steps)
        kept = [part[:rows].astype(F32) for part in parts]
        for index, step in enumerate(steps[1:], 1):
            sent = sum(part[index * rows : (index + 1) * rows].astype(F32) for part in parts)
            kept.append(swap_dp(sent.astype(BF), step))
        parts = kept
    return sum(part.astype(F32) for part in parts)


def added(*parts):
    return sum(part.astype(F32) for part in parts)


def slices_summed(values):
    count = lax.axis_size("dp") * lax.axis_size("tensor")
    values = jnp.pad(values, (0, -values.size % (128 * count)))
    spread = values.reshape(count, -1, 128)
    return jnp.sum(lax.all_to_all(spread, ("dp", "tensor"), 0, 0, tiled=True), axis=0).reshape(-1)


def everyones(value):
    count = lax.axis_size("dp") * lax.axis_size("tensor")
    spread = jnp.broadcast_to(value[None], (count,) + value.shape)
    return lax.all_to_all(spread, ("dp", "tensor"), 0, 0, tiled=True)


def selector(places, words, word_bits):
    out = np.zeros((places, 2 * words), np.float32)
    for place in range(places):
        word, bit = divmod(place, word_bits)
        if bit < LOW_BITS:
            out[place, word] = 2.0**-bit
        else:
            out[place, words + word] = 2.0 ** (LOW_BITS - bit)
    return out


def split_words(words):
    words = words.astype(jnp.int32)
    low = jnp.bitwise_and(words, (1 << LOW_BITS) - 1)
    high = jnp.right_shift(words, LOW_BITS)
    return jnp.concatenate([low.astype(F32), high.astype(F32)], axis=0).astype(BF)


def units_bit(values):
    return jnp.bitwise_and(values.astype(jnp.int32), 1).astype(F32).astype(BF)


def prob_keep_kernel(select_ref, words_ref, keep_ref):
    for view in range(2):
        keep_ref[view, 0] = units_bit(
            dot(select_ref[...], split_words(words_ref[view, 0]), 1, 0)
        )


def prob_keep(words, length):
    _, heads, rows, _ = words.shape
    select = jnp.asarray(selector(length, rows, PROB_BITS), BF)
    return pl.pallas_call(
        prob_keep_kernel,
        grid=(heads,),
        in_specs=[
            pl.BlockSpec(select.shape, lambda h: (0, 0)),
            pl.BlockSpec((2, 1, rows, length), lambda h: (0, h, 0, 0)),
        ],
        out_specs=pl.BlockSpec((2, 1, length, length), lambda h: (0, h, 0, 0)),
        out_shape=jax.ShapeDtypeStruct((2, heads, length, length), BF),
        compiler_params=pltpu.CompilerParams(vmem_limit_bytes=VMEM_LIMIT),
        name="prob_keep",
    )(select, words)


def branch_keep_kernel(select_ref, words_ref, keep_ref):
    keep_ref[0, 0] = units_bit(dot(split_words(words_ref[0, 0]), select_ref[...], 0, 0))


def branch_keep(words, select):
    _, _, rows, length = words.shape
    width = select.shape[1]
    return pl.pallas_call(
        branch_keep_kernel,
        grid=(2, 2),
        in_specs=[
            pl.BlockSpec(select.shape, lambda b, v: (0, 0)),
            pl.BlockSpec((1, 1, rows, length), lambda b, v: (b, v, 0, 0)),
        ],
        out_specs=pl.BlockSpec((1, 1, length, width), lambda b, v: (b, v, 0, 0)),
        out_shape=jax.ShapeDtypeStruct((2, 2, length, width), BF),
        compiler_params=pltpu.CompilerParams(vmem_limit_bytes=VMEM_LIMIT),
        name="branch_keep",
    )(select, words)


def head_lanes(shape, head):
    lane = lax.broadcasted_iota(jnp.int32, shape, 1)
    return jnp.logical_and(lane >= head * HD, lane < (head + 1) * HD)


def attend_kernel(chunk, q_ref, k_ref, v_ref, keep_ref, context_ref, logsum_ref, turned):
    length = q_ref.shape[0]
    queries = q_ref[...] * BF(0.125)
    key_rows = k_ref[...]
    values_turned = v_ref[...].T
    for head in range(2):
        own = jnp.where(head_lanes(queries.shape, head), queries, BF(0))
        span = slice(head * HD, (head + 1) * HD)
        for start in range(0, length, chunk):
            part = slice(start, start + chunk)
            scores = dot(key_rows, own[part], 1, 1)
            peak = jnp.max(scores, axis=0, keepdims=True)
            powers = jnp.exp(scores - peak)
            total = jnp.sum(powers, axis=0, keepdims=True)
            weighted = (powers * (KEEP_SCALE / total)).astype(BF)
            logsum_ref[head, :, part] = peak + jnp.log(total * (1.0 / KEEP_SCALE))
            for view in range(2):
                kept = weighted * keep_ref[view, head, :, part]
                turned[view, span, part] = dot(values_turned[span], kept, 1, 0).astype(BF)
    for view in range(2):
        context_ref[view] = turned[view].T


def attend(qkv, keep, chunk):
    length = qkv.shape[0]
    heads = keep.shape[1]
    pairs = heads // 2

    def part(p):
        return pl.BlockSpec((length, 2 * HD), lambda h: (0, p * pairs + h))

    return pl.pallas_call(
        functools.partial(attend_kernel, chunk),
        grid=(pairs,),
        in_specs=[
            part(0),
            part(1),
            part(2),
            pl.BlockSpec((2, 2, length, length), lambda h: (0, h, 0, 0)),
        ],
        out_specs=[
            pl.BlockSpec((2, length, 2 * HD), lambda h: (0, 0, h)),
            pl.BlockSpec((2, 1, length), lambda h: (h, 0, 0)),
        ],
        out_shape=[
            jax.ShapeDtypeStruct((2, length, heads * HD), BF),
            jax.ShapeDtypeStruct((heads, 1, length), F32),
        ],
        scratch_shapes=[pltpu.VMEM((2, 2 * HD, length), BF)],
        compiler_params=pltpu.CompilerParams(vmem_limit_bytes=VMEM_LIMIT),
        name="attend",
    )(qkv, qkv, qkv, keep)


def attend_back_kernel(
    chunk,
    q_ref,
    k_ref,
    v_ref,
    keep_ref,
    logsum_ref,
    context_ref,
    grad_ref,
    out_ref,
    turned,
    grad_keys,
    grad_values,
):
    length = q_ref.shape[0]
    width = 2 * HD
    pairs = pl.num_programs(0)
    queries = q_ref[...] * BF(0.125)
    key_rows = k_ref[...]
    values = v_ref[...]
    keys_turned = key_rows.T
    grads = [grad_ref[0], grad_ref[1]]
    product = sum(
        grads[view].astype(F32) * context_ref[view].astype(F32) for view in range(2)
    ).T
    for head in range(2):
        span = slice(head * HD, (head + 1) * HD)
        mine = head_lanes(queries.shape, head)
        own = jnp.where(mine, queries, BF(0))
        own_grads = [jnp.where(mine, grad, BF(0)) for grad in grads]
        inner = jnp.sum(product[span], axis=0, keepdims=True) * (1.0 / KEEP_SCALE)
        total_keys, total_values = None, None
        for start in range(0, length, chunk):
            part = slice(start, start + chunk)
            scores = dot(key_rows, own[part], 1, 1)
            scaled = jnp.exp(scores - logsum_ref[head, :, part])
            weighted = scaled.astype(BF)
            change = None
            for view in range(2):
                keep = keep_ref[view, head, :, part]
                more = dot(weighted * keep, grads[view][part], 1, 0)
                total_values = more if total_values is None else total_values + more
                term = dot(values, own_grads[view][part], 1, 1) * keep.astype(F32)
                change = term if change is None else change + term
            grad_scores = (scaled * (change - inner[:, part])).astype(BF)
            more = dot(grad_scores, queries[part], 1, 0)
            total_keys = more if total_keys is None else total_keys + more
            turned[span, part] = (dot(keys_turned[span], grad_scores, 1, 0) * 0.125).astype(BF)
        if head == 0:
            grad_keys[...] = total_keys
            grad_values[...] = total_values
        else:
            grad_keys[...] = jnp.where(mine, total_keys, grad_keys[...])
            grad_values[...] = jnp.where(mine, total_values, grad_values[...])
    pair = pl.program_id(0)

    def columns(p):
        return pl.ds(pl.multiple_of((p * pairs + pair) * width, width), width)

    out_ref[:, columns(0)] = turned[...].T
    out_ref[:, columns(1)] = grad_keys[...].astype(BF)
    out_ref[:, columns(2)] = grad_values[...].astype(BF)


def attend_back(qkv, keep, logsum, context, grad_context, chunk):
    length = qkv.shape[0]
    heads = keep.shape[1]
    pairs = heads // 2

    def part(p):
        return pl.BlockSpec((length, 2 * HD), lambda h: (0, p * pairs + h))

    sides = pl.BlockSpec((2, length, 2 * HD), lambda h: (0, 0, h))
    return pl.pallas_call(
        functools.partial(attend_back_kernel, chunk),
        grid=(pairs,),
        in_specs=[
            part(0),
            part(1),
            part(2),
            pl.BlockSpec((2, 2, length, length), lambda h: (0, h, 0, 0)),
            pl.BlockSpec((2, 1, length), lambda h: (h, 0, 0)),
            sides,
            sides,
        ],
        out_specs=pl.BlockSpec(qkv.shape, lambda h: (0, 0)),
        out_shape=jax.ShapeDtypeStruct(qkv.shape, BF),
        scratch_shapes=[
            pltpu.VMEM((2 * HD, length), BF),
            pltpu.VMEM((length, 2 * HD), F32),
            pltpu.VMEM((length, 2 * HD), F32),
        ],
        compiler_params=pltpu.CompilerParams(vmem_limit_bytes=VMEM_LIMIT),
        name="attend_back",
    )(qkv, qkv, qkv, keep, logsum, context, grad_context)


GAIN_ONE, GAIN_TWO, OUT_BIAS, SHIFT_ONE, DOWN_BIAS, SHIFT_TWO = range(6)
ROWS = 128
COLUMNS = 256


def rows_block(width):
    return pl.BlockSpec((2, ROWS, width), lambda i: (0, i, 0))


def constant_block(shape):
    return pl.BlockSpec(shape, lambda i: (0,) * len(shape), pipeline_mode=pl.Buffered(1))


def flat(values):
    return values.reshape(values.shape[0] * values.shape[1], values.shape[2])


def norm_parts(values):
    center = values - jnp.mean(values, axis=-1, keepdims=True)
    spread = jnp.mean(center * center, axis=-1, keepdims=True)
    inverse = lax.rsqrt(spread + 1e-12)
    return center * inverse, inverse


def norm_back(grad, unit, inverse, gain):
    scaled = grad * gain
    mean = jnp.mean(scaled, axis=-1, keepdims=True)
    along = jnp.mean(scaled * unit, axis=-1, keepdims=True)
    return inverse * (scaled - mean - unit * along)


def kept(keep_ref):
    return flat(keep_ref[...]).astype(F32) * KEEP_SCALE


def first_norm_kernel(
    vectors_ref, own_ref, other_ref, own_out, other_out, token_ref, keep_ref, unit_ref, inverse_ref
):
    attn_out = dot(flat(own_ref[...]), own_out[...], 1, 1) + dot(
        flat(other_ref[...]), other_out[...], 1, 1
    )
    change = (attn_out + vectors_ref[OUT_BIAS : OUT_BIAS + 1]) * kept(keep_ref)
    token = token_ref[...].astype(F32)
    unit, inverse = norm_parts(change.reshape(unit_ref.shape) + token[None])
    unit_ref[...] = unit
    inverse_ref[...] = inverse


def first_norm(vectors, contexts, outs, token, keep):
    _, length, width = keep.shape
    local = contexts[0].shape[2]
    return pl.pallas_call(
        first_norm_kernel,
        grid=(length // ROWS,),
        in_specs=[constant_block(vectors.shape)]
        + [rows_block(local)] * 2
        + [constant_block(outs[0].shape)] * 2
        + [pl.BlockSpec((ROWS, width), lambda i: (i, 0)), rows_block(width)],
        out_specs=[rows_block(width), rows_block(1)],
        out_shape=[
            jax.ShapeDtypeStruct((2, length, width), F32),
            jax.ShapeDtypeStruct((2, length, 1), F32),
        ],
        compiler_params=pltpu.CompilerParams(vmem_limit_bytes=VMEM_LIMIT),
        name="first_norm",
    )(vectors, *contexts, *outs, token, keep)


def hidden_kernel(
    vectors_ref,
    bias_ref,
    unit_ref,
    keep_ref,
    up_own,
    up_other,
    down_own,
    down_other,
    low_ref,
    active_own,
    active_other,
    slope_ref,
    unit_two_ref,
    inverse_two_ref,
    sum_ref,
):
    vector = lambda row: vectors_ref[row : row + 1]
    normed = flat(unit_ref[...]) * vector(GAIN_ONE) + vector(SHIFT_ONE)
    low = normed.astype(BF)
    low_ref[...] = low.reshape(low_ref.shape)
    hidden = up_own.shape[1]
    step = min(COLUMNS, hidden)
    total = vector(DOWN_BIAS)
    for half, (up, down, active_ref) in enumerate(
        ((up_own, down_own, active_own), (up_other, down_other, active_other))
    ):
        for start in range(0, hidden, step):
            part = slice(start, start + step)
            pre = dot(low, up[:, part], 1, 0) + bias_ref[half : half + 1, part]
            cumulative = 0.5 + 0.5 * lax.erf(pre * (0.5**0.5))
            density = jnp.exp(-0.5 * pre * pre) * (1.0 / (2.0 * np.pi) ** 0.5)
            active = (pre * cumulative).astype(BF)
            slope = (cumulative + pre * density).astype(BF)
            active_ref[:, :, part] = active.reshape(2, ROWS, step)
            slope_ref[:, :, half * hidden + start : half * hidden + start + step] = slope.reshape(
                2, ROWS, step
            )
            total = total + dot(active, down[:, part], 1, 1)
    unit, inverse = norm_parts((normed + total * kept(keep_ref)).reshape(unit_two_ref.shape))
    unit_two_ref[...] = unit
    inverse_two_ref[...] = inverse
    added_rows = jnp.sum(unit, axis=1)

    @pl.when(pl.program_id(0) == 0)
    def _():
        sum_ref[...] = added_rows

    @pl.when(pl.program_id(0) > 0)
    def _():
        sum_ref[...] += added_rows


def hidden_units(vectors, bias, unit, keep, ups, downs):
    _, length, width = keep.shape
    hidden = ups[0].shape[1]
    return pl.pallas_call(
        hidden_kernel,
        grid=(length // ROWS,),
        in_specs=[
            constant_block(vectors.shape),
            constant_block(bias.shape),
            rows_block(width),
            rows_block(width),
        ]
        + [constant_block(ups[0].shape)] * 4,
        out_specs=[
            rows_block(width),
            rows_block(hidden),
            rows_block(hidden),
            rows_block(2 * hidden),
            rows_block(width),
            rows_block(1),
            pl.BlockSpec((2, width), lambda i: (0, 0)),
        ],
        out_shape=[
            jax.ShapeDtypeStruct((2, length, width), BF),
            jax.ShapeDtypeStruct((2, length, hidden), BF),
            jax.ShapeDtypeStruct((2, length, hidden), BF),
            jax.ShapeDtypeStruct((2, length, 2 * hidden), BF),
            jax.ShapeDtypeStruct((2, length, width), F32),
            jax.ShapeDtypeStruct((2, length, 1), F32),
            jax.ShapeDtypeStruct((2, width), F32),
        ],
        compiler_params=pltpu.CompilerParams(vmem_limit_bytes=VMEM_LIMIT),
        name="hidden_units",
    )(vectors, bias, unit, keep, *ups, *downs)


def second_back_kernel(
    vectors_ref, rows_ref, unit_ref, inverse_ref, keep_ref, second_ref, low_ref
):
    grad = norm_back(
        rows_ref[...][:, None, :],
        unit_ref[...],
        inverse_ref[...],
        vectors_ref[GAIN_TWO : GAIN_TWO + 1],
    )
    second_ref[...] = grad
    low_ref[...] = (grad * (keep_ref[...].astype(F32) * KEEP_SCALE)).astype(BF)


def second_back(vectors, rows, unit, inverse, keep):
    _, length, width = keep.shape
    return pl.pallas_call(
        second_back_kernel,
        grid=(length // ROWS,),
        in_specs=[
            constant_block(vectors.shape),
            constant_block(rows.shape),
            rows_block(width),
            rows_block(1),
            rows_block(width),
        ],
        out_specs=[rows_block(width)] * 2,
        out_shape=[
            jax.ShapeDtypeStruct(keep.shape, F32),
            jax.ShapeDtypeStruct(keep.shape, BF),
        ],
        compiler_params=pltpu.CompilerParams(vmem_limit_bytes=VMEM_LIMIT),
        name="second_back",
    )(vectors, rows, unit, inverse, keep)


def hidden_back_kernel(
    vectors_ref,
    grad_ref,
    slope_ref,
    second_ref,
    unit_ref,
    inverse_ref,
    keep_ref,
    up_own,
    up_other,
    down_own,
    down_other,
    hidden_own,
    hidden_other,
    attn_ref,
    first_ref,
    sums_ref,
    hidden_sums_ref,
):
    @pl.when(pl.program_id(0) == 0)
    def _():
        sums_ref[...] = jnp.zeros_like(sums_ref)
        hidden_sums_ref[...] = jnp.zeros_like(hidden_sums_ref)

    grad = flat(grad_ref[...])
    hidden = up_own.shape[1]
    step = min(COLUMNS, hidden)
    back = flat(second_ref[...])
    for half, (up, down, hidden_ref) in enumerate(
        ((up_own, down_own, hidden_own), (up_other, down_other, hidden_other))
    ):
        for start in range(0, hidden, step):
            part = slice(start, start + step)
            slope = flat(
                slope_ref[:, :, half * hidden + start : half * hidden + start + step]
            ).astype(F32)
            grad_hidden = (dot(grad, down[:, part], 1, 0) * slope).astype(BF)
            hidden_ref[:, :, part] = grad_hidden.reshape(2, ROWS, step)
            hidden_sums_ref[half : half + 1, part] += jnp.sum(
                grad_hidden.astype(F32), axis=0, keepdims=True
            )
            back = back + dot(grad_hidden, up[:, part], 1, 1)
    unit = flat(unit_ref[...])
    grad_first = norm_back(
        back, unit, flat(inverse_ref[...]), vectors_ref[GAIN_ONE : GAIN_ONE + 1]
    )
    grad_attn = (grad_first * kept(keep_ref)).astype(BF)
    attn_ref[...] = grad_attn.reshape(attn_ref.shape)
    first_ref[...] = grad_first[:ROWS] + grad_first[ROWS:]
    for row, values in enumerate(
        (back * unit, back, grad_attn.astype(F32), grad.astype(F32))
    ):
        sums_ref[row : row + 1] += jnp.sum(values, axis=0, keepdims=True)


def hidden_back(vectors, grad, slope, second, unit, inverse, keep, ups, downs):
    _, length, width = keep.shape
    hidden = ups[0].shape[1]
    return pl.pallas_call(
        hidden_back_kernel,
        grid=(length // ROWS,),
        in_specs=[
            constant_block(vectors.shape),
            rows_block(width),
            rows_block(2 * hidden),
            rows_block(width),
            rows_block(width),
            rows_block(1),
            rows_block(width),
        ]
        + [constant_block(ups[0].shape)] * 4,
        out_specs=[
            rows_block(hidden),
            rows_block(hidden),
            rows_block(width),
            pl.BlockSpec((ROWS, width), lambda i: (i, 0)),
            pl.BlockSpec((4, width), lambda i: (0, 0)),
            pl.BlockSpec((2, hidden), lambda i: (0, 0)),
        ],
        out_shape=[
            jax.ShapeDtypeStruct((2, length, hidden), BF),
            jax.ShapeDtypeStruct((2, length, hidden), BF),
            jax.ShapeDtypeStruct((2, length, width), BF),
            jax.ShapeDtypeStruct((length, width), F32),
            jax.ShapeDtypeStruct((4, width), F32),
            jax.ShapeDtypeStruct((2, hidden), F32),
        ],
        compiler_params=pltpu.CompilerParams(vmem_limit_bytes=VMEM_LIMIT),
        name="hidden_back",
    )(vectors, grad, slope, second, unit, inverse, keep, *ups, *downs)


def loss_kernel(rows_ref, place_ref, loss_ref, grad_ref, *, scale):
    first, second = rows_ref[0], rows_ref[1]
    count = first.shape[0]
    inverse = [
        lax.rsqrt(jnp.sum(rows * rows, axis=-1, keepdims=True) + 1e-06) for rows in (first, second)
    ]
    units = [first * inverse[0], second * inverse[1]]
    logits = dot(units[0], units[1], 1, 1, EXACT) * 20.0
    peak = jnp.max(logits, axis=1, keepdims=True)
    powers = jnp.exp(logits - peak)
    total = jnp.sum(powers, axis=1, keepdims=True)
    row = lax.broadcasted_iota(jnp.int32, logits.shape, 0)
    column = lax.broadcasted_iota(jnp.int32, logits.shape, 1)
    on_diagonal = row == column
    losses = (
        peak
        + jnp.log(total)
        - jnp.sum(jnp.where(on_diagonal, logits, 0.0), axis=1, keepdims=True)
    )
    loss_ref[...] = jnp.sum(losses, axis=0, keepdims=True) * (1.0 / count)
    grad_logits = (powers / total - jnp.where(on_diagonal, 1.0, 0.0)) * (20.0 * scale / count)
    grad_units = [
        dot(grad_logits, units[1], 1, 0, EXACT),
        dot(grad_logits, units[0], 0, 0, EXACT),
    ]
    mine = lax.broadcasted_iota(jnp.int32, first.shape, 0) == place_ref[0]
    for view in range(2):
        along = jnp.sum(units[view] * grad_units[view], axis=-1, keepdims=True)
        grad_rows = (grad_units[view] - units[view] * along) * inverse[view]
        grad_ref[view : view + 1] = jnp.sum(
            jnp.where(mine, grad_rows, 0.0), axis=0, keepdims=True
        )


def loss_and_grad(rows, place, scale):
    width = rows.shape[-1]
    return pl.pallas_call(
        functools.partial(loss_kernel, scale=scale),
        in_specs=[
            pl.BlockSpec(memory_space=pltpu.VMEM),
            pl.BlockSpec(memory_space=pltpu.SMEM),
        ],
        out_shape=[
            jax.ShapeDtypeStruct((1, 1), F32),
            jax.ShapeDtypeStruct((2, width), F32),
        ],
        compiler_params=pltpu.CompilerParams(vmem_limit_bytes=VMEM_LIMIT),
        name="contrast",
    )(rows, place)


def adam_direction(weight, gradient, first_moment, second, decay_rate):
    new_first = 0.9 * first_moment + 0.1 * gradient
    new_second = 0.999 * second + 0.001 * gradient * gradient
    first_hat = new_first / (1.0 - 0.9**STEP)
    second_hat = new_second / (1.0 - 0.999**STEP)
    update = first_hat / (jnp.sqrt(second_hat) + 1e-06) + decay_rate * weight
    return (new_first, new_second, update)


LANES = 128
SQUARES = {"attn": 0, "out": 3, "up": 4, "down": 5}
MATRICES = 6


def in_lane(lane, value):
    lanes = lax.broadcasted_iota(jnp.int32, (1, LANES), 1)
    return jnp.where(lanes == lane, value, 0.0)


def pieces_of(matrix_ref):
    if len(matrix_ref.shape) == 3:
        return [(part,) for part in range(matrix_ref.shape[0])]
    return [(slice(None),)]


def adam_kernel(names, scale, *refs):
    count = len(names)
    ins, before_ref = refs[: 4 * count], refs[4 * count]
    outs, sums_ref = refs[4 * count + 1 : -1], refs[-1]
    sums = before_ref[...]
    for place, name in enumerate(names):
        weight_ref, grad_ref, first_ref, second_ref = ins[4 * place : 4 * place + 4]
        out_refs = outs[3 * place : 3 * place + 3]
        for part, where in enumerate(pieces_of(weight_ref)):
            weight = weight_ref[where]
            columns = weight.shape[-1]
            grad = grad_ref[:, part * columns : (part + 1) * columns] * scale
            results = adam_direction(weight, grad, first_ref[where], second_ref[where], 0.01)
            for out_ref, result in zip(out_refs, results):
                out_ref[where] = result
            lane = SQUARES[name] + part
            sums = sums + in_lane(lane, jnp.sum(weight * weight))
            sums = sums + in_lane(lane + MATRICES, jnp.sum(results[2] * results[2]))
    sums_ref[...] = sums


def adam(names, matrices, before, scale):
    args = [array for matrix in matrices for array in matrix]
    shapes = [
        jax.ShapeDtypeStruct(matrix[0].shape, F32) for matrix in matrices for _ in range(3)
    ] + [jax.ShapeDtypeStruct(before.shape, F32)]
    out = pl.pallas_call(
        functools.partial(adam_kernel, names, scale),
        out_shape=shapes,
        compiler_params=pltpu.CompilerParams(vmem_limit_bytes=VMEM_LIMIT),
        name="adam",
    )(*args, before)
    return [out[3 * i : 3 * i + 3] for i in range(len(names))], out[-1]


def apply_kernel(names, *refs):
    count = len(names)
    sums_ref, pairs, outs = refs[0], refs[1 : 1 + 2 * count], refs[1 + 2 * count :]
    sums = jnp.sum(sums_ref[...], axis=0, keepdims=True)
    roots = jnp.sqrt(sums)
    for place, name in enumerate(names):
        weight_ref, update_ref = pairs[2 * place : 2 * place + 2]
        for part, where in enumerate(pieces_of(weight_ref)):
            lane = SQUARES[name] + part
            ratio = roots[:, lane : lane + 1] / roots[:, lane + MATRICES : lane + MATRICES + 1]
            outs[place][where] = weight_ref[where] - 0.25 * ratio * update_ref[where]


def apply_updates(names, sums, pairs):
    return pl.pallas_call(
        functools.partial(apply_kernel, names),
        out_shape=[jax.ShapeDtypeStruct(weight.shape, F32) for weight, _ in pairs],
        compiler_params=pltpu.CompilerParams(vmem_limit_bytes=VMEM_LIMIT),
        name="apply_updates",
    )(sums, *(array for pair in pairs for array in pair))


def small_step(weight, gradient, first_moment, second):
    new_first, new_second, update = adam_direction(weight, gradient, first_moment, second, 0.0)
    trust_ratio = jnp.sqrt(jnp.sum(weight * weight, axis=-1, keepdims=True)) / jnp.sqrt(
        jnp.sum(update * update, axis=-1, keepdims=True)
    )
    return (weight - 0.25 * trust_ratio * update, new_first, new_second)


def shards(
    tokens,
    prob_masks,
    branch_masks,
    attn_weight,
    attn_first,
    attn_second,
    out_weight,
    out_first,
    out_second,
    up_weight,
    up_first,
    up_second,
    down_weight,
    down_first,
    down_second,
    gains,
    gains_first,
    gains_second,
    shifts,
    shifts_first,
    shifts_second,
    hidden_bias,
    hidden_first,
    hidden_second,
):
    tensor_count = lax.axis_size("tensor")
    tensor_rank = lax.axis_index("tensor")
    data_count = lax.axis_size("dp")
    data_rank = lax.axis_index("dp")
    seq_local, half_len, width = tokens.shape
    assert tensor_count == 2 and seq_local == 2
    seq_len = half_len * tensor_count
    heads_local = prob_masks.shape[2]
    local_width = heads_local * HD
    hidden_local = up_weight.shape[1]
    rows_local = width // data_count
    scale_loss = 64.0 * data_count * seq_local * seq_len
    chunk = min(256, seq_len)
    is_first = tensor_rank == 0

    def in_order(mine, others, axis):
        return jnp.where(
            is_first,
            jnp.concatenate([mine, others], axis=axis),
            jnp.concatenate([others, mine], axis=axis),
        )

    def of_rank(whole, axis, length):
        mine = lax.dynamic_slice_in_dim(whole, tensor_rank * length, length, axis)
        others = lax.dynamic_slice_in_dim(whole, (1 - tensor_rank) * length, length, axis)
        return mine, others

    own_tokens, send_tokens = of_rank(tokens, 0, 1)
    words = jnp.pad(
        jnp.swapaxes(prob_masks.astype(jnp.int16), 3, 4),
        ((0, 0), (0, 0), (0, 0), (0, -prob_masks.shape[4] % 16), (0, 0)),
    )
    own_words, send_words = of_rank(words, 1, 1)
    branch_words = jnp.pad(
        jnp.swapaxes(branch_masks.astype(jnp.int16), 3, 4),
        ((0, 0), (0, 0), (0, 0), (0, -branch_masks.shape[4] % 16), (0, 0)),
    )
    own_branch, send_branch = of_rank(branch_words, 2, 1)

    order = jnp.asarray(np.array(gathered_order(data_count), np.int32))
    owner = jnp.bitwise_xor(order, data_rank)
    feature = (owner[:, None] * rows_local + jnp.arange(rows_local, dtype=jnp.int32)).reshape(-1)
    places = lax.broadcasted_iota(jnp.int32, (width, width), 0)
    to_own = (places == feature[None, :]).astype(F32)
    to_own_low = to_own.astype(BF)

    attn_block = attn_weight.astype(BF).reshape(rows_local, 3 * local_width)
    out_block = out_weight.astype(BF).T
    up_block = up_weight.astype(BF)
    down_block = down_weight.astype(BF).T
    device_count = data_count * tensor_count
    down_blocks = lax.all_gather(down_block, ("dp", "tensor"), axis=0, tiled=False)
    branch_rows_padded = branch_words.shape[3]
    word = feature // BRANCH_BITS
    bit = feature % BRANCH_BITS
    high = bit >= LOW_BITS
    row = jnp.where(high, word + branch_rows_padded, word)
    power = jnp.exp2(-jnp.where(high, bit - LOW_BITS, bit).astype(F32))
    branch_select = jnp.where(
        lax.broadcasted_iota(jnp.int32, (2 * branch_rows_padded, width), 0) == row[None, :],
        power[None, :],
        0.0,
    ).astype(BF)

    bias_q = of_rank(shifts[0], 0, local_width)
    bias_v = of_rank(shifts[1], 0, local_width)

    def project(half, rows, matrix):
        bias = jnp.concatenate([bias_q[half], jnp.zeros_like(bias_q[half]), bias_v[half]])
        return (dot(rows, matrix, 1, 0) + bias).astype(BF)

    token_other, other_words = swap_tensor(send_tokens), swap_tensor(send_words)
    attn_quarter = gather_upper(attn_block)
    attn_beside, attn_across = swap_dp(attn_quarter, 2), swap_tensor(attn_quarter)
    wide_block = tie(jnp.concatenate([out_block, up_block], axis=1), attn_quarter)
    wide_quarter = gather_upper(wide_block)
    own_keep = prob_keep(tie(own_words[:, 0], attn_quarter), seq_len)
    token_rows = in_order(own_tokens[0], token_other[0], 0)
    token_own = dot(token_rows, to_own_low, 1, 0).astype(BF)
    attn_beside, attn_across, wide_quarter, own_keep, token_own, other_words = together(
        attn_beside, attn_across, wide_quarter, own_keep, token_own, other_words
    )
    attn_corner = swap_dp(attn_across, 2)
    wide_across = swap_tensor(wide_quarter)
    wide_beside = swap_dp(wide_quarter, 2)
    attn_near = gather_core((attn_quarter, attn_beside))
    qkv_own = project(0, token_own, attn_near)
    attended = attend(qkv_own, own_keep, chunk)
    other_keep = prob_keep(other_words[:, 0], seq_len)
    attn_corner, attended, wide_across, other_keep = together(
        attn_corner, attended, wide_across, other_keep
    )
    wide_corner = swap_dp(wide_across, 2)
    branch_other = swap_tensor(tie(send_branch, wide_across))
    attn_far = gather_core((attn_across, attn_corner))
    qkv_other = project(1, token_own, attn_far)
    attended_other = attend(qkv_other, other_keep, chunk)
    branch_rows = in_order(own_branch[:, :, 0], branch_other[:, :, 0], 3)
    keeps = branch_keep(branch_rows, branch_select)
    wide_corner, wide_beside, attended_other, keeps = together(
        wide_corner, wide_beside, attended_other, keeps
    )
    attn_low = [attn_near, attn_far]
    spans = ((0, local_width), (local_width, local_width + hidden_local))
    wide_low = [
        gather_core((wide_quarter, wide_beside), spans),
        gather_core((wide_across, wide_corner), spans),
    ]
    out_low = [low[0] for low in wide_low]
    up_low = [low[1] for low in wide_low]
    qkv = [qkv_own, qkv_other]
    contexts = [attended[0], attended_other[0]]
    logsums = [attended[1], attended_other[1]]
    keep_halves = (own_keep, other_keep)
    down_places = jnp.stack(
        [owner * tensor_count + tensor_rank, owner * tensor_count + (1 - tensor_rank)]
    ).astype(jnp.int32)
    down_low = picked(down_blocks.reshape(device_count, rows_local, hidden_local), down_places)

    vectors = dot(jnp.concatenate([gains, shifts[2:6]], axis=0), to_own, 1, 0, EXACT)
    context_flat = [c.reshape(2 * seq_len, local_width) for c in contexts]
    unit_one, inverse_one = first_norm(vectors, contexts, out_low, token_own, keeps[0])
    hidden_halves = jnp.stack(of_rank(hidden_bias, 0, hidden_local))
    normed_low, active_own, active_other, slope, unit_two, inverse_two, unit_sum = hidden_units(
        vectors, hidden_halves, unit_one, keeps[1], up_low, down_low
    )
    normed_low = normed_low.reshape(2 * seq_len, width)
    active = [a.reshape(2 * seq_len, hidden_local) for a in (active_own, active_other)]
    gain_two = vectors[GAIN_TWO]
    shift_two = vectors[SHIFT_TWO]
    pooled = unit_sum * gain_two / seq_len + shift_two
    pooled_rows = dot(pooled, to_own, 1, 1, EXACT)
    everyone = jnp.swapaxes(everyones(pooled_rows), 0, 1)
    place = (data_rank * tensor_count + tensor_rank).astype(jnp.int32).reshape(1)
    loss_value, grad_pooled = loss_and_grad(everyone, place, scale_loss)
    grad_rows = dot(grad_pooled, to_own, 1, 0, EXACT) / seq_len

    grad_shift_two = jnp.sum(grad_rows, axis=0) * seq_len
    grad_gain_two = jnp.sum(grad_rows * unit_sum, axis=0)
    grad_second, grad_ffn = second_back(vectors, grad_rows, unit_two, inverse_two, keeps[1])
    grad_ffn_flat = grad_ffn.reshape(2 * seq_len, width)
    half_width, quarter_width = width // 2, width // 4

    def weight_grads(left, right):
        return (
            dot(left[:, :half_width], right, 0, 0),
            dot(left[:, half_width:], right, 0, 0),
        )

    def both_cores(grads):
        kept, sent = grads
        return kept, swap_dp(sent, 1)

    def rows_of(parts, first):
        return tuple(
            part[:quarter_width] if first else part[quarter_width:] for part in parts
        )

    def low_sum(parts):
        return added(*parts).astype(BF)

    def context_back(half, grad_rows):
        return dot(grad_rows, out_low[half], 1, 0).astype(BF)

    def queries_back(half, grad_context):
        return attend_back(
            qkv[half],
            keep_halves[half],
            logsums[half],
            contexts[half],
            grad_context.reshape(2, seq_len, local_width),
            chunk,
        )

    down_other = weight_grads(grad_ffn_flat, active[1])
    down_own = weight_grads(grad_ffn_flat, active[0])
    down_other, down_own, grad_ffn_flat = together(down_other, down_own, grad_ffn_flat)

    down_other, down_own = both_cores(down_other), both_cores(down_own)
    hidden_grads = hidden_back(
        vectors,
        grad_ffn_flat.reshape(2, seq_len, width),
        slope,
        grad_second,
        unit_one,
        inverse_one,
        keeps[0],
        up_low,
        down_low,
    )
    down_other, down_own, hidden_grads = together(down_other, down_own, hidden_grads)
    grad_hidden_own, grad_hidden_other, grad_attn, grad_first, column_sums, hidden_sums = (
        hidden_grads
    )
    grad_attn_flat = grad_attn.reshape(2 * seq_len, width)

    down_across = swap_tensor(low_sum(down_other))
    up_other = weight_grads(normed_low, grad_hidden_other.reshape(2 * seq_len, hidden_local))
    up_own = weight_grads(normed_low, grad_hidden_own.reshape(2 * seq_len, hidden_local))
    up_other, up_own = both_cores(up_other), both_cores(up_own)
    out_other = both_cores(weight_grads(grad_attn_flat, context_flat[1]))
    out_own = both_cores(weight_grads(grad_attn_flat, context_flat[0]))
    down_across, up_other, up_own, out_other, out_own, grad_attn_flat = together(
        down_across, up_other, up_own, out_other, out_own, grad_attn_flat
    )

    down_own = down_own + (down_across,)
    down_beside = swap_dp(low_sum(rows_of(down_own, False)), 2)
    up_across = swap_tensor(low_sum(up_other))
    out_across = swap_tensor(low_sum(out_other))
    grad_other = queries_back(1, context_back(1, grad_attn_flat))
    attn_other = weight_grads(token_own, grad_other)
    down_beside, up_across, out_across, out_own, attn_other, grad_other, grad_attn_flat = together(
        down_beside, up_across, out_across, out_own, attn_other, grad_other, grad_attn_flat
    )

    attn_other = both_cores(attn_other)
    up_own = up_own + (up_across,)
    up_sent = low_sum(rows_of(up_own, False))
    context_own = context_back(0, grad_attn_flat)
    token_back = dot(grad_other, attn_low[1], 1, 1) + grad_first
    attn_other, up_sent, context_own, token_back = together(
        attn_other, up_sent, context_own, token_back
    )
    attn_sent = low_sum(attn_other)
    up_beside = swap_dp(up_sent, 2)
    attn_across = swap_tensor(attn_sent)
    down_reduced = reduce_upper(rows_of(down_own, True) + (down_beside,))
    grad_own = queries_back(0, tie(context_own, attn_sent))
    attn_own = weight_grads(token_own, grad_own)
    attn_across, up_beside, down_reduced, attn_own, grad_own = together(
        attn_across, up_beside, down_reduced, attn_own, grad_own
    )

    attn_own = both_cores(attn_own)
    up_reduced = reduce_upper(rows_of(up_own, True) + (up_beside,))
    token_back = token_back + dot(grad_own, attn_low[0], 1, 1)
    attn_own, token_back = together(attn_own, token_back)
    attn_own = attn_own + (attn_across,)
    out_own = out_own + (out_across,)
    tail_sent = jnp.concatenate(
        [low_sum(rows_of(attn_own, False)), low_sum(rows_of(out_own, False))], axis=1
    )
    tail_beside = swap_dp(tail_sent, 2)
    token_grad = dot(tie(token_back, tail_sent), to_own, 1, 1, EXACT)
    grad_own = tie(grad_own, tail_sent)
    tail_beside, token_grad, up_reduced = together(tail_beside, token_grad, up_reduced)
    tail = jnp.concatenate(
        [added(*rows_of(attn_own, True)), added(*rows_of(out_own, True))], axis=1
    )
    tail_reduced = reduce_upper((tail, tail_beside))
    attn_reduced, out_reduced = (
        tail_reduced[:, : 3 * local_width],
        tail_reduced[:, 3 * local_width :],
    )
    grad_qkv = [grad_own, grad_other]
    own_half, send_half = of_rank(token_grad, 0, half_len)
    grad_tokens = in_order(own_half[None], swap_tensor(send_half.astype(BF))[None].astype(F32), 0)

    bias_sums = [jnp.sum(grad_qkv[half].astype(F32), axis=0) for half in range(2)]
    query_row = in_order(bias_sums[0][:local_width], bias_sums[1][:local_width], 0)
    value_row = in_order(bias_sums[0][2 * local_width :], bias_sums[1][2 * local_width :], 0)
    hidden_row = in_order(hidden_sums[0], hidden_sums[1], 0)
    feature_rows = dot(
        jnp.stack(
            [
                column_sums[0],
                grad_gain_two,
                column_sums[2],
                column_sums[1],
                column_sums[3],
                grad_shift_two,
            ]
        ),
        to_own,
        1,
        1,
        EXACT,
    )
    small = jnp.concatenate(
        [feature_rows, query_row[None], value_row[None], hidden_row.reshape(-1, width)], axis=0
    )
    small_sums = slices_summed(small.reshape(-1)) * (1.0 / scale_loss)
    small_all = everyones(small_sums.reshape(-1, 128)).reshape(-1)
    small = small_all[: small.size].reshape(small.shape)
    inverse_scale = 1.0 / scale_loss

    def turned(*arrays):
        return [array.T for array in arrays]

    def parts_first(*arrays):
        return [jnp.transpose(array, (1, 0, 2)) for array in arrays]

    down_own_weight, down_firsts, down_seconds = turned(down_weight, down_first, down_second)
    out_own_weight, out_firsts, out_seconds = turned(out_weight, out_first, out_second)
    attn_parts, attn_firsts, attn_seconds = parts_first(attn_weight, attn_first, attn_second)
    (down_new, up_new), sums = adam(
        ("down", "up"),
        (
            (down_own_weight, down_reduced, down_firsts, down_seconds),
            (up_weight, up_reduced, up_first, up_second),
        ),
        jnp.zeros((1, LANES), F32),
        inverse_scale,
    )
    (attn_new, out_new), sums = adam(
        ("attn", "out"),
        (
            (attn_parts, attn_reduced, attn_firsts, attn_seconds),
            (out_own_weight, out_reduced, out_firsts, out_seconds),
        ),
        sums,
        inverse_scale,
    )
    new_attn, new_out, new_up, new_down = apply_updates(
        ("attn", "out", "up", "down"),
        everyones(sums)[:, 0],
        (
            (attn_parts, attn_new[2]),
            (out_own_weight, out_new[2]),
            (up_weight, up_new[2]),
            (down_own_weight, down_new[2]),
        ),
    )
    new_attn, attn_new_first, attn_new_second = parts_first(new_attn, attn_new[0], attn_new[1])
    new_out, out_new_first, out_new_second = turned(new_out, out_new[0], out_new[1])
    new_down, down_new_first, down_new_second = turned(new_down, down_new[0], down_new[1])
    up_new_first, up_new_second = up_new[:2]
    gain_total = small[:2]
    shift_total = jnp.concatenate([small[6:8], small[2:6]], axis=0)
    hidden_total = small[8:].reshape(-1)

    new_gains, new_gains_first, new_gains_second = small_step(
        gains, gain_total, gains_first, gains_second
    )
    new_shifts, new_shifts_first, new_shifts_second = small_step(
        shifts, shift_total, shifts_first, shifts_second
    )
    new_hidden, new_hidden_first, new_hidden_second = small_step(
        hidden_bias, hidden_total, hidden_first, hidden_second
    )
    return (
        loss_value.reshape(()),
        grad_tokens,
        new_attn,
        attn_new_first,
        attn_new_second,
        new_out,
        out_new_first,
        out_new_second,
        new_up,
        up_new_first,
        up_new_second,
        new_down,
        down_new_first,
        down_new_second,
        new_gains,
        new_gains_first,
        new_gains_second,
        new_shifts,
        new_shifts_first,
        new_shifts_second,
        new_hidden,
        new_hidden_first,
        new_hidden_second,
    )


def solution(mesh):
    row_split = P("dp", None, "tensor")
    column_split = P("tensor", "dp")
    matrix_split = P("dp", "tensor")
    return jax.shard_map(
        shards,
        mesh=mesh,
        in_specs=(
            P("dp", "tensor", None),
            P(None, "dp", "tensor", None, None),
            P(None, None, "dp", "tensor", None),
        )
        + (row_split,) * 3
        + (column_split,) * 3
        + (matrix_split,) * 3
        + (column_split,) * 3
        + (P(),) * 9,
        out_specs=(P(), P("dp", "tensor", None))
        + (row_split,) * 3
        + (column_split,) * 3
        + (matrix_split,) * 3
        + (column_split,) * 3
        + (P(),) * 9,
        check_vma=False,
    )
```

```python
import functools

import jax
import jax.numpy as jnp
import numpy as np
from jax import lax
from jax.experimental import pallas as pl
from jax.experimental.pallas import tpu as pltpu
from jax.sharding import PartitionSpec as P

HD = 64
STEP = 10
KEEP_SCALE = 1.0 / 0.9
PROB_BITS = 13
BRANCH_BITS = 15
LOW_BITS = 7
BF = jnp.bfloat16
F32 = jnp.float32
EXACT = lax.Precision.HIGHEST
VMEM_LIMIT = 56 << 20


def work(flops):
    return pl.CostEstimate(flops=int(flops), bytes_accessed=0, transcendentals=0)


def dot(left, right, left_dim, right_dim, precision=None):
    return lax.dot_general(
        left,
        right,
        (((left_dim,), (right_dim,)), ((), ())),
        preferred_element_type=F32,
        precision=precision,
    )


def swap_dp(value, distance):
    count = lax.axis_size("dp")
    return lax.ppermute(value, "dp", [(i, i ^ distance) for i in range(count)])


def swap_tensor(value):
    return lax.ppermute(value, "tensor", [(0, 1), (1, 0)])


def bit_groups(count):
    bits = count.bit_length() - 1
    groups, top = [], bits
    while top - 2 >= 2:
        groups.append((top - 2, top - 1))
        top -= 2
    while top > 0:
        groups.append((top - 1,))
        top -= 1
    return groups


def distances(group):
    out = [0]
    for bit in group:
        out = out + [o | (1 << bit) for o in out]
    return out


def gathered_order(count):
    order = [0]
    for group in bit_groups(count):
        order = [o | step for step in distances(group) for o in order]
    return order


def joined_kernel(spans, *refs):
    count = len(refs) - 1 - len(spans)
    pieces, out_refs, arrived = refs[:count], refs[count:-1], refs[-1]
    copies, start = [], 0
    for index, piece in enumerate(pieces):
        rows = piece.shape[0]
        for place, (first, last) in enumerate(spans):
            copies.append(
                pltpu.make_async_copy(
                    piece.at[:, pl.ds(first, last - first)],
                    out_refs[place].at[pl.ds(start, rows)],
                    arrived.at[index, place],
                )
            )
        start += rows
    for copy in copies:
        copy.start()
    for copy in copies:
        copy.wait()


def joined(pieces, spans=None):
    rows = sum(piece.shape[0] for piece in pieces)
    columns = pieces[0].shape[1]
    parts = spans or ((0, columns),)
    if any(piece.shape[0] % 16 for piece in pieces):
        whole = jnp.concatenate(pieces, axis=0)
        return [whole[:, first:last] for first, last in parts] if spans else whole
    out = pl.pallas_call(
        functools.partial(joined_kernel, parts),
        in_specs=[pl.BlockSpec(memory_space=pl.ANY)] * len(pieces),
        out_specs=[pl.BlockSpec(memory_space=pltpu.VMEM)] * len(parts),
        out_shape=[
            jax.ShapeDtypeStruct((rows, last - first), pieces[0].dtype) for first, last in parts
        ],
        scratch_shapes=[pltpu.SemaphoreType.DMA((len(pieces), len(parts)))],
        compiler_params=pltpu.CompilerParams(vmem_limit_bytes=VMEM_LIMIT),
        name="joined",
    )(*pieces)
    return out if spans else out[0]


def whole_tiles(blocks, places):
    _, rows, columns = blocks.shape
    count = places.shape[1]
    if rows % 16 == 0:
        return blocks, places
    quarters = blocks[places.reshape(-1)].reshape(8, count * rows // 4, columns)
    return quarters, jnp.arange(8, dtype=jnp.int32).reshape(2, 4)


def tie(value, *others):
    return lax.optimization_barrier((value,) + others)[0]


def together(*values):
    return lax.optimization_barrier(values)


def upper_groups():
    return bit_groups(lax.axis_size("dp"))[:-2]


def gather_upper(block):
    for group in upper_groups():
        block = joined([block] + [swap_dp(block, s) for s in distances(group)[1:]])
    return block


def gather_bit(block, bit):
    return joined([block, swap_dp(block, 1 << bit)])


def gather_sides(mine, corner_by_tensor):
    beside = swap_dp(mine, 2)
    across = swap_tensor(mine)
    corner = swap_tensor(beside) if corner_by_tensor else swap_dp(across, 2)
    return (mine, beside), (across, corner)


def gather_core(quarters, spans=None):
    near, far = quarters
    return joined([near, far, swap_dp(near, 1), swap_dp(far, 1)], spans)


def upper_parts(parts):
    for group in reversed(upper_groups()):
        steps = distances(group)
        rows = parts[0].shape[0] // len(steps)
        kept_rows = [part[:rows].astype(F32) for part in parts]
        for index, step in enumerate(steps[1:], 1):
            sent = sum(part[index * rows : (index + 1) * rows].astype(F32) for part in parts)
            kept_rows.append(swap_dp(sent.astype(BF), step))
        parts = kept_rows
    return tuple(parts)


def added(*parts):
    return sum(part.astype(F32) for part in parts)


def slices_summed(values):
    count = lax.axis_size("dp") * lax.axis_size("tensor")
    values = jnp.pad(values, (0, -values.size % (128 * count)))
    spread = values.reshape(count, -1, 128)
    return jnp.sum(lax.all_to_all(spread, ("dp", "tensor"), 0, 0, tiled=True), axis=0).reshape(-1)


def everyones(value):
    count = lax.axis_size("dp") * lax.axis_size("tensor")
    spread = jnp.broadcast_to(value[None], (count,) + value.shape)
    return lax.all_to_all(spread, ("dp", "tensor"), 0, 0, tiled=True)


def selector(places, words, word_bits):
    out = np.zeros((places, 2 * words), np.float32)
    for place in range(places):
        word, bit = divmod(place, word_bits)
        if bit < LOW_BITS:
            out[place, word] = 2.0**-bit
        else:
            out[place, words + word] = 2.0 ** (LOW_BITS - bit)
    return out


def split_words(words):
    words = words.astype(jnp.int32)
    low = jnp.bitwise_and(words, (1 << LOW_BITS) - 1)
    high = jnp.right_shift(words, LOW_BITS)
    return jnp.concatenate([low.astype(F32), high.astype(F32)], axis=0).astype(BF)


def units_bit(values):
    return jnp.bitwise_and(values.astype(jnp.int32), 1).astype(F32).astype(BF)


def prob_keep_kernel(select_ref, words_ref, keep_ref):
    for view in range(2):
        keep_ref[view, 0] = units_bit(
            dot(select_ref[...], split_words(words_ref[view, 0]), 1, 0)
        )


def prob_keep(words, length):
    _, heads, rows, _ = words.shape
    select = jnp.asarray(selector(length, rows, PROB_BITS), BF)
    return pl.pallas_call(
        prob_keep_kernel,
        grid=(heads,),
        in_specs=[
            pl.BlockSpec(select.shape, lambda h: (0, 0)),
            pl.BlockSpec((2, 1, rows, length), lambda h: (0, h, 0, 0)),
        ],
        out_specs=pl.BlockSpec((2, 1, length, length), lambda h: (0, h, 0, 0)),
        out_shape=jax.ShapeDtypeStruct((2, heads, length, length), BF),
        compiler_params=pltpu.CompilerParams(vmem_limit_bytes=VMEM_LIMIT),
        name="prob_keep",
        cost_estimate=work(3.5e9),
    )(select, words)


def branch_keep_kernel(select_ref, words_ref, keep_ref):
    keep_ref[0, 0] = units_bit(dot(split_words(words_ref[0, 0]), select_ref[...], 0, 0))


def branch_keep(words, select):
    _, _, rows, length = words.shape
    width = select.shape[1]
    return pl.pallas_call(
        branch_keep_kernel,
        grid=(2, 2),
        in_specs=[
            pl.BlockSpec(select.shape, lambda b, v: (0, 0)),
            pl.BlockSpec((1, 1, rows, length), lambda b, v: (b, v, 0, 0)),
        ],
        out_specs=pl.BlockSpec((1, 1, length, width), lambda b, v: (b, v, 0, 0)),
        out_shape=jax.ShapeDtypeStruct((2, 2, length, width), BF),
        compiler_params=pltpu.CompilerParams(vmem_limit_bytes=VMEM_LIMIT),
        name="branch_keep",
        cost_estimate=work(2.5e9),
    )(select, words)


def head_lanes(shape, head):
    lane = lax.broadcasted_iota(jnp.int32, shape, 1)
    return jnp.logical_and(lane >= head * HD, lane < (head + 1) * HD)


def attend_kernel(chunk, q_ref, k_ref, v_ref, keep_ref, context_ref, logsum_ref, turned):
    length = q_ref.shape[0]
    queries = q_ref[...] * BF(0.125)
    key_rows = k_ref[...]
    values_turned = v_ref[...].T
    for head in range(2):
        own = jnp.where(head_lanes(queries.shape, head), queries, BF(0))
        span = slice(head * HD, (head + 1) * HD)
        for start in range(0, length, chunk):
            part = slice(start, start + chunk)
            scores = dot(key_rows, own[part], 1, 1)
            peak = jnp.max(scores, axis=0, keepdims=True)
            powers = jnp.exp(scores - peak)
            total = jnp.sum(powers, axis=0, keepdims=True)
            weighted = (powers * (KEEP_SCALE / total)).astype(BF)
            logsum_ref[head, :, part] = peak + jnp.log(total * (1.0 / KEEP_SCALE))
            for view in range(2):
                kept = weighted * keep_ref[view, head, :, part]
                turned[view, span, part] = dot(values_turned[span], kept, 1, 0).astype(BF)
    for view in range(2):
        context_ref[view] = turned[view].T


def attend(qkv, keep, chunk):
    length = qkv.shape[0]
    heads = keep.shape[1]
    pairs = heads // 2

    def part(p):
        return pl.BlockSpec((length, 2 * HD), lambda h: (0, p * pairs + h))

    return pl.pallas_call(
        functools.partial(attend_kernel, chunk),
        grid=(pairs,),
        in_specs=[
            part(0),
            part(1),
            part(2),
            pl.BlockSpec((2, 2, length, length), lambda h: (0, h, 0, 0)),
        ],
        out_specs=[
            pl.BlockSpec((2, length, 2 * HD), lambda h: (0, 0, h)),
            pl.BlockSpec((2, 1, length), lambda h: (h, 0, 0)),
        ],
        out_shape=[
            jax.ShapeDtypeStruct((2, length, heads * HD), BF),
            jax.ShapeDtypeStruct((heads, 1, length), F32),
        ],
        scratch_shapes=[pltpu.VMEM((2, 2 * HD, length), BF)],
        compiler_params=pltpu.CompilerParams(vmem_limit_bytes=VMEM_LIMIT),
        name="attend",
        cost_estimate=work(4e9),
    )(qkv, qkv, qkv, keep)


def attend_back_kernel(
    chunk,
    q_ref,
    k_ref,
    v_ref,
    keep_ref,
    logsum_ref,
    context_ref,
    grad_ref,
    out_ref,
    turned,
    grad_keys,
    grad_values,
):
    length = q_ref.shape[0]
    width = 2 * HD
    pairs = pl.num_programs(0)
    queries = q_ref[...] * BF(0.125)
    key_rows = k_ref[...]
    values = v_ref[...]
    keys_turned = key_rows.T
    grads = [grad_ref[0], grad_ref[1]]
    product = sum(
        grads[view].astype(F32) * context_ref[view].astype(F32) for view in range(2)
    ).T
    for head in range(2):
        span = slice(head * HD, (head + 1) * HD)
        mine = head_lanes(queries.shape, head)
        own = jnp.where(mine, queries, BF(0))
        own_grads = [jnp.where(mine, grad, BF(0)) for grad in grads]
        inner = jnp.sum(product[span], axis=0, keepdims=True) * (1.0 / KEEP_SCALE)
        total_keys, total_values = None, None
        for start in range(0, length, chunk):
            part = slice(start, start + chunk)
            scores = dot(key_rows, own[part], 1, 1)
            scaled = jnp.exp(scores - logsum_ref[head, :, part])
            weighted = scaled.astype(BF)
            change = None
            for view in range(2):
                keep = keep_ref[view, head, :, part]
                more = dot(weighted * keep, grads[view][part], 1, 0)
                total_values = more if total_values is None else total_values + more
                term = dot(values, own_grads[view][part], 1, 1) * keep.astype(F32)
                change = term if change is None else change + term
            grad_scores = (scaled * (change - inner[:, part])).astype(BF)
            more = dot(grad_scores, queries[part], 1, 0)
            total_keys = more if total_keys is None else total_keys + more
            turned[span, part] = (dot(keys_turned[span], grad_scores, 1, 0) * 0.125).astype(BF)
        if head == 0:
            grad_keys[...] = total_keys
            grad_values[...] = total_values
        else:
            grad_keys[...] = jnp.where(mine, total_keys, grad_keys[...])
            grad_values[...] = jnp.where(mine, total_values, grad_values[...])
    pair = pl.program_id(0)

    def columns(p):
        return pl.ds(pl.multiple_of((p * pairs + pair) * width, width), width)

    out_ref[:, columns(0)] = turned[...].T
    out_ref[:, columns(1)] = grad_keys[...].astype(BF)
    out_ref[:, columns(2)] = grad_values[...].astype(BF)


def attend_back(qkv, keep, logsum, context, grad_context, chunk):
    length = qkv.shape[0]
    heads = keep.shape[1]
    pairs = heads // 2

    def part(p):
        return pl.BlockSpec((length, 2 * HD), lambda h: (0, p * pairs + h))

    sides = pl.BlockSpec((2, length, 2 * HD), lambda h: (0, 0, h))
    return pl.pallas_call(
        functools.partial(attend_back_kernel, chunk),
        grid=(pairs,),
        in_specs=[
            part(0),
            part(1),
            part(2),
            pl.BlockSpec((2, 2, length, length), lambda h: (0, h, 0, 0)),
            pl.BlockSpec((2, 1, length), lambda h: (h, 0, 0)),
            sides,
            sides,
        ],
        out_specs=pl.BlockSpec(qkv.shape, lambda h: (0, 0)),
        out_shape=jax.ShapeDtypeStruct(qkv.shape, BF),
        scratch_shapes=[
            pltpu.VMEM((2 * HD, length), BF),
            pltpu.VMEM((length, 2 * HD), F32),
            pltpu.VMEM((length, 2 * HD), F32),
        ],
        compiler_params=pltpu.CompilerParams(vmem_limit_bytes=VMEM_LIMIT),
        name="attend_back",
        cost_estimate=work(6e9),
    )(qkv, qkv, qkv, keep, logsum, context, grad_context)


GAIN_ONE, GAIN_TWO, OUT_BIAS, SHIFT_ONE, DOWN_BIAS, SHIFT_TWO = range(6)
ROWS = 128
COLUMNS = 256


def rows_block(width):
    return pl.BlockSpec((2, ROWS, width), lambda i: (0, i, 0))


def constant_block(shape):
    return pl.BlockSpec(shape, lambda i: (0,) * len(shape), pipeline_mode=pl.Buffered(1))


def flat(values):
    return values.reshape(values.shape[0] * values.shape[1], values.shape[2])


def norm_parts(values):
    center = values - jnp.mean(values, axis=-1, keepdims=True)
    spread = jnp.mean(center * center, axis=-1, keepdims=True)
    inverse = lax.rsqrt(spread + 1e-12)
    return center * inverse, inverse


def norm_back(grad, unit, inverse, gain):
    scaled = grad * gain
    mean = jnp.mean(scaled, axis=-1, keepdims=True)
    along = jnp.mean(scaled * unit, axis=-1, keepdims=True)
    return inverse * (scaled - mean - unit * along)


def kept(keep_ref):
    return flat(keep_ref[...]).astype(F32) * KEEP_SCALE


def row_copies(pieces, first, target, arrived):
    copies, start = [], 0
    for index, piece in enumerate(pieces):
        rows = piece.shape[0]
        copies.append(
            pltpu.make_async_copy(
                piece.at[:, pl.ds(first, target.shape[1])],
                target.at[pl.ds(start, rows)],
                arrived.at[index],
            )
        )
        start += rows
    return copies


def block_copies(blocks, places, half, target, arrived):
    rows = blocks.shape[1]
    return [
        pltpu.make_async_copy(
            blocks.at[places[half, index]],
            target.at[pl.ds(index * rows, rows)],
            arrived.at[index],
        )
        for index in range(target.shape[0] // rows)
    ]


def at_first_step(action):
    pl.when(pl.program_id(0) == 0)(action)


def start_all(copies):
    for copy in copies:
        copy.start()


def wait_all(copies):
    for copy in copies:
        copy.wait()


def far_spec():
    return pl.BlockSpec(memory_space=pl.ANY)


def first_norm_kernel(*refs):
    vectors_ref, own_ref, other_ref, token_ref, keep_ref = refs[:5]
    pieces, (unit_ref, inverse_ref, own_out, other_out), arrived = refs[5:-5], refs[-5:-1], refs[-1]
    count = len(pieces) // 2
    copies = row_copies(pieces[:count], 0, own_out, arrived.at[0]) + row_copies(
        pieces[count:], 0, other_out, arrived.at[1]
    )

    @at_first_step
    def _():
        start_all(copies)
        wait_all(copies)

    attn_out = dot(flat(own_ref[...]), own_out[...], 1, 1) + dot(
        flat(other_ref[...]), other_out[...], 1, 1
    )
    change = (attn_out + vectors_ref[OUT_BIAS : OUT_BIAS + 1]) * kept(keep_ref)
    token = token_ref[...].astype(F32)
    unit, inverse = norm_parts(change.reshape(unit_ref.shape) + token[None])
    unit_ref[...] = unit
    inverse_ref[...] = inverse


def first_norm(vectors, contexts, pieces, token, keep):
    _, length, width = keep.shape
    local = contexts[0].shape[2]
    whole = pl.BlockSpec((width, local), lambda i: (0, 0))
    return pl.pallas_call(
        first_norm_kernel,
        grid=(length // ROWS,),
        in_specs=[constant_block(vectors.shape)]
        + [rows_block(local)] * 2
        + [pl.BlockSpec((ROWS, width), lambda i: (i, 0)), rows_block(width)]
        + [far_spec()] * (len(pieces[0]) + len(pieces[1])),
        out_specs=[rows_block(width), rows_block(1), whole, whole],
        out_shape=[
            jax.ShapeDtypeStruct((2, length, width), F32),
            jax.ShapeDtypeStruct((2, length, 1), F32),
            jax.ShapeDtypeStruct((width, local), BF),
            jax.ShapeDtypeStruct((width, local), BF),
        ],
        scratch_shapes=[pltpu.SemaphoreType.DMA((2, len(pieces[0])))],
        compiler_params=pltpu.CompilerParams(vmem_limit_bytes=VMEM_LIMIT),
        name="first_norm",
        cost_estimate=work(3.5e9),
    )(vectors, *contexts, token, keep, *pieces[0], *pieces[1])


def hidden_kernel(first, *refs):
    places_ref, vectors_ref, bias_ref, unit_ref, keep_ref, blocks_ref = refs[:6]
    pieces, rest = refs[6:-16], refs[-16:]
    low_ref, active_own, active_other, slope_own, slope_other = rest[:5]
    unit_two_ref, inverse_two_ref, sum_ref = rest[5:8]
    up_own, up_other, down_own, down_other = rest[8:12]
    up_arrived, down_arrived = rest[12:14], rest[14:16]
    count = len(pieces) // 2
    up_copies = [
        row_copies(pieces[:count], first, up_own, up_arrived[0]),
        row_copies(pieces[count:], first, up_other, up_arrived[1]),
    ]
    down_copies = [
        block_copies(blocks_ref, places_ref, half, down, down_arrived[half])
        for half, down in enumerate((down_own, down_other))
    ]

    @at_first_step
    def _():
        for half in range(2):
            start_all(up_copies[half])
            start_all(down_copies[half])

    vector = lambda row: vectors_ref[row : row + 1]
    normed = flat(unit_ref[...]) * vector(GAIN_ONE) + vector(SHIFT_ONE)
    low = normed.astype(BF)
    low_ref[...] = low.reshape(low_ref.shape)
    hidden = up_own.shape[1]
    step = min(COLUMNS, hidden)
    total = vector(DOWN_BIAS)
    for half, (up, down, active_ref, slope_ref) in enumerate(
        (
            (up_own, down_own, active_own, slope_own),
            (up_other, down_other, active_other, slope_other),
        )
    ):
        at_first_step(functools.partial(wait_all, up_copies[half] + down_copies[half]))
        for start in range(0, hidden, step):
            part = slice(start, start + step)
            pre = dot(low, up[:, part], 1, 0) + bias_ref[half : half + 1, part]
            cumulative = 0.5 + 0.5 * lax.erf(pre * (0.5**0.5))
            density = jnp.exp(-0.5 * pre * pre) * (1.0 / (2.0 * np.pi) ** 0.5)
            active = (pre * cumulative).astype(BF)
            slope = (cumulative + pre * density).astype(BF)
            active_ref[:, :, part] = active.reshape(2, ROWS, step)
            slope_ref[:, :, part] = slope.reshape(2, ROWS, step)
            total = total + dot(active, down[:, part], 1, 1)
    unit, inverse = norm_parts((normed + total * kept(keep_ref)).reshape(unit_two_ref.shape))
    unit_two_ref[...] = unit
    inverse_two_ref[...] = inverse
    added_rows = jnp.sum(unit, axis=1)

    @at_first_step
    def _():
        sum_ref[...] = added_rows

    @pl.when(pl.program_id(0) > 0)
    def _():
        sum_ref[...] += added_rows


def weights_scratch(width, hidden, halves, pieces, blocks):
    return (
        [pltpu.VMEM((width, hidden), BF)] * (2 * halves)
        + [pltpu.SemaphoreType.DMA((pieces,))] * halves
        + [pltpu.SemaphoreType.DMA((blocks,))] * halves
    )


def smem_spec():
    return pl.BlockSpec(memory_space=pltpu.SMEM)


def hidden_units(vectors, bias, unit, keep, pieces, first, blocks, places):
    _, length, width = keep.shape
    hidden = blocks.shape[2]
    return pl.pallas_call(
        functools.partial(hidden_kernel, first),
        grid=(length // ROWS,),
        in_specs=[
            smem_spec(),
            constant_block(vectors.shape),
            constant_block(bias.shape),
            rows_block(width),
            rows_block(width),
        ]
        + [far_spec()] * (1 + len(pieces[0]) + len(pieces[1])),
        out_specs=[
            rows_block(width),
            rows_block(hidden),
            rows_block(hidden),
            rows_block(hidden),
            rows_block(hidden),
            rows_block(width),
            rows_block(1),
            pl.BlockSpec((2, width), lambda i: (0, 0)),
        ],
        out_shape=[
            jax.ShapeDtypeStruct((2, length, width), BF),
            jax.ShapeDtypeStruct((2, length, hidden), BF),
            jax.ShapeDtypeStruct((2, length, hidden), BF),
            jax.ShapeDtypeStruct((2, length, hidden), BF),
            jax.ShapeDtypeStruct((2, length, hidden), BF),
            jax.ShapeDtypeStruct((2, length, width), F32),
            jax.ShapeDtypeStruct((2, length, 1), F32),
            jax.ShapeDtypeStruct((2, width), F32),
        ],
        scratch_shapes=weights_scratch(width, hidden, 2, len(pieces[0]), places.shape[1]),
        compiler_params=pltpu.CompilerParams(vmem_limit_bytes=VMEM_LIMIT),
        name="hidden_units",
        cost_estimate=work(11e9),
    )(places, vectors, bias, unit, keep, blocks, *pieces[0], *pieces[1])


def second_back_kernel(
    vectors_ref, rows_ref, unit_ref, inverse_ref, keep_ref, second_ref, low_ref
):
    grad = norm_back(
        rows_ref[...][:, None, :],
        unit_ref[...],
        inverse_ref[...],
        vectors_ref[GAIN_TWO : GAIN_TWO + 1],
    )
    second_ref[...] = grad
    low_ref[...] = (grad * (keep_ref[...].astype(F32) * KEEP_SCALE)).astype(BF)


def second_back(vectors, rows, unit, inverse, keep):
    _, length, width = keep.shape
    return pl.pallas_call(
        second_back_kernel,
        grid=(length // ROWS,),
        in_specs=[
            constant_block(vectors.shape),
            constant_block(rows.shape),
            rows_block(width),
            rows_block(1),
            rows_block(width),
        ],
        out_specs=[rows_block(width)] * 2,
        out_shape=[
            jax.ShapeDtypeStruct(keep.shape, F32),
            jax.ShapeDtypeStruct(keep.shape, BF),
        ],
        compiler_params=pltpu.CompilerParams(vmem_limit_bytes=VMEM_LIMIT),
        name="second_back",
        cost_estimate=work(3e9),
    )(vectors, rows, unit, inverse, keep)


def half_back(grad, slope_ref, up, down, hidden_ref, hidden_sums_ref, back):
    hidden = up.shape[1]
    step = min(COLUMNS, hidden)
    for start in range(0, hidden, step):
        part = slice(start, start + step)
        slope = flat(slope_ref[:, :, part]).astype(F32)
        grad_hidden = (dot(grad, down[:, part], 1, 0) * slope).astype(BF)
        hidden_ref[:, :, part] = grad_hidden.reshape(2, ROWS, step)
        hidden_sums_ref[:, part] += jnp.sum(grad_hidden.astype(F32), axis=0, keepdims=True)
        back = back + dot(grad_hidden, up[:, part], 1, 1)
    return back


def own_back_kernel(first, *refs):
    places_ref, grad_ref, slope_ref, second_ref, blocks_ref = refs[:5]
    pieces = refs[5:-7]
    hidden_ref, back_ref, hidden_sums_ref, up, down, up_arrived, down_arrived = refs[-7:]
    copies = row_copies(pieces, first, up, up_arrived) + block_copies(
        blocks_ref, places_ref, 0, down, down_arrived
    )

    @at_first_step
    def _():
        start_all(copies)
        hidden_sums_ref[...] = jnp.zeros_like(hidden_sums_ref)
        wait_all(copies)

    back = half_back(
        flat(grad_ref[...]),
        slope_ref,
        up,
        down,
        hidden_ref,
        hidden_sums_ref,
        flat(second_ref[...]),
    )
    back_ref[...] = back.reshape(back_ref.shape)


def own_back(grad, slope, second, pieces, first, blocks, places):
    _, length, width = grad.shape
    hidden = blocks.shape[2]
    return pl.pallas_call(
        functools.partial(own_back_kernel, first),
        grid=(length // ROWS,),
        in_specs=[smem_spec(), rows_block(width), rows_block(hidden), rows_block(width)]
        + [far_spec()] * (1 + len(pieces)),
        out_specs=[
            rows_block(hidden),
            rows_block(width),
            pl.BlockSpec((1, hidden), lambda i: (0, 0)),
        ],
        out_shape=[
            jax.ShapeDtypeStruct((2, length, hidden), BF),
            jax.ShapeDtypeStruct((2, length, width), F32),
            jax.ShapeDtypeStruct((1, hidden), F32),
        ],
        scratch_shapes=weights_scratch(width, hidden, 1, len(pieces), places.shape[1]),
        compiler_params=pltpu.CompilerParams(vmem_limit_bytes=VMEM_LIMIT),
        name="own_back",
        cost_estimate=work(6e9),
    )(places, grad, slope, second, blocks, *pieces)


def other_back_kernel(first, *refs):
    places_ref, vectors_ref, grad_ref, slope_ref, before_ref = refs[:5]
    unit_ref, inverse_ref, keep_ref, blocks_ref = refs[5:9]
    pieces = refs[9:-9]
    hidden_ref, attn_ref, first_ref, sums_ref, hidden_sums_ref = refs[-9:-4]
    up, down, up_arrived, down_arrived = refs[-4:]
    copies = row_copies(pieces, first, up, up_arrived) + block_copies(
        blocks_ref, places_ref, 1, down, down_arrived
    )

    @at_first_step
    def _():
        start_all(copies)
        sums_ref[...] = jnp.zeros_like(sums_ref)
        hidden_sums_ref[...] = jnp.zeros_like(hidden_sums_ref)
        wait_all(copies)

    grad = flat(grad_ref[...])
    back = half_back(
        grad, slope_ref, up, down, hidden_ref, hidden_sums_ref, flat(before_ref[...])
    )
    unit = flat(unit_ref[...])
    grad_first = norm_back(
        back, unit, flat(inverse_ref[...]), vectors_ref[GAIN_ONE : GAIN_ONE + 1]
    )
    grad_attn = (grad_first * kept(keep_ref)).astype(BF)
    attn_ref[...] = grad_attn.reshape(attn_ref.shape)
    first_ref[...] = grad_first[:ROWS] + grad_first[ROWS:]
    for row, values in enumerate(
        (back * unit, back, grad_attn.astype(F32), grad.astype(F32))
    ):
        sums_ref[row : row + 1] += jnp.sum(values, axis=0, keepdims=True)


def other_back(vectors, grad, slope, before, unit, inverse, keep, pieces, first, blocks, places):
    _, length, width = keep.shape
    hidden = blocks.shape[2]
    return pl.pallas_call(
        functools.partial(other_back_kernel, first),
        grid=(length // ROWS,),
        in_specs=[
            smem_spec(),
            constant_block(vectors.shape),
            rows_block(width),
            rows_block(hidden),
            rows_block(width),
            rows_block(width),
            rows_block(1),
            rows_block(width),
        ]
        + [far_spec()] * (1 + len(pieces)),
        out_specs=[
            rows_block(hidden),
            rows_block(width),
            pl.BlockSpec((ROWS, width), lambda i: (i, 0)),
            pl.BlockSpec((4, width), lambda i: (0, 0)),
            pl.BlockSpec((1, hidden), lambda i: (0, 0)),
        ],
        out_shape=[
            jax.ShapeDtypeStruct((2, length, hidden), BF),
            jax.ShapeDtypeStruct((2, length, width), BF),
            jax.ShapeDtypeStruct((length, width), F32),
            jax.ShapeDtypeStruct((4, width), F32),
            jax.ShapeDtypeStruct((1, hidden), F32),
        ],
        scratch_shapes=weights_scratch(width, hidden, 1, len(pieces), places.shape[1]),
        compiler_params=pltpu.CompilerParams(vmem_limit_bytes=VMEM_LIMIT),
        name="other_back",
        cost_estimate=work(7e9),
    )(places, vectors, grad, slope, before, unit, inverse, keep, blocks, *pieces)


def loss_kernel(rows_ref, place_ref, loss_ref, grad_ref, *, scale):
    first, second = rows_ref[0], rows_ref[1]
    count = first.shape[0]
    inverse = [
        lax.rsqrt(jnp.sum(rows * rows, axis=-1, keepdims=True) + 1e-06) for rows in (first, second)
    ]
    units = [first * inverse[0], second * inverse[1]]
    logits = dot(units[0], units[1], 1, 1, EXACT) * 20.0
    peak = jnp.max(logits, axis=1, keepdims=True)
    powers = jnp.exp(logits - peak)
    total = jnp.sum(powers, axis=1, keepdims=True)
    row = lax.broadcasted_iota(jnp.int32, logits.shape, 0)
    column = lax.broadcasted_iota(jnp.int32, logits.shape, 1)
    on_diagonal = row == column
    losses = (
        peak
        + jnp.log(total)
        - jnp.sum(jnp.where(on_diagonal, logits, 0.0), axis=1, keepdims=True)
    )
    loss_ref[...] = jnp.sum(losses, axis=0, keepdims=True) * (1.0 / count)
    grad_logits = (powers / total - jnp.where(on_diagonal, 1.0, 0.0)) * (20.0 * scale / count)
    grad_units = [
        dot(grad_logits, units[1], 1, 0, EXACT),
        dot(grad_logits, units[0], 0, 0, EXACT),
    ]
    mine = lax.broadcasted_iota(jnp.int32, first.shape, 0) == place_ref[0]
    for view in range(2):
        along = jnp.sum(units[view] * grad_units[view], axis=-1, keepdims=True)
        grad_rows = (grad_units[view] - units[view] * along) * inverse[view]
        grad_ref[view : view + 1] = jnp.sum(
            jnp.where(mine, grad_rows, 0.0), axis=0, keepdims=True
        )


def loss_and_grad(rows, place, scale):
    width = rows.shape[-1]
    return pl.pallas_call(
        functools.partial(loss_kernel, scale=scale),
        in_specs=[
            pl.BlockSpec(memory_space=pltpu.VMEM),
            pl.BlockSpec(memory_space=pltpu.SMEM),
        ],
        out_shape=[
            jax.ShapeDtypeStruct((1, 1), F32),
            jax.ShapeDtypeStruct((2, width), F32),
        ],
        compiler_params=pltpu.CompilerParams(vmem_limit_bytes=VMEM_LIMIT),
        name="contrast",
    )(rows, place)


def adam_direction(weight, gradient, first_moment, second, decay_rate):
    new_first = 0.9 * first_moment + 0.1 * gradient
    new_second = 0.999 * second + 0.001 * gradient * gradient
    first_hat = new_first / (1.0 - 0.9**STEP)
    second_hat = new_second / (1.0 - 0.999**STEP)
    update = first_hat / (jnp.sqrt(second_hat) + 1e-06) + decay_rate * weight
    return (new_first, new_second, update)


LANES = 128
SQUARES = {"attn": 0, "out": 3, "up": 4, "down": 5}
MATRICES = 6


def in_lane(lane, value):
    lanes = lax.broadcasted_iota(jnp.int32, (1, LANES), 1)
    return jnp.where(lanes == lane, value, 0.0)


def pieces_of(matrix_ref):
    if len(matrix_ref.shape) == 3:
        return [(part,) for part in range(matrix_ref.shape[0])]
    return [(slice(None),)]


def adam_kernel(names, offsets, scale, *refs):
    count = len(names)
    ins, before_ref = refs[: 4 * count], refs[4 * count]
    outs, sums_ref = refs[4 * count + 1 : -1], refs[-1]
    sums = before_ref[...]
    for place, name in enumerate(names):
        weight_ref, grad_ref, first_ref, second_ref = ins[4 * place : 4 * place + 4]
        out_refs = outs[3 * place : 3 * place + 3]
        for part, where in enumerate(pieces_of(weight_ref)):
            weight = weight_ref[where]
            columns = weight.shape[-1]
            start = offsets[place] + part * columns
            grad = grad_ref[:, start : start + columns] * scale
            results = adam_direction(weight, grad, first_ref[where], second_ref[where], 0.01)
            for out_ref, result in zip(out_refs, results):
                out_ref[where] = result
            lane = SQUARES[name] + part
            sums = sums + in_lane(lane, jnp.sum(weight * weight))
            sums = sums + in_lane(lane + MATRICES, jnp.sum(results[2] * results[2]))
    sums_ref[...] = sums


def adam(names, offsets, matrices, before, scale):
    args = [array for matrix in matrices for array in matrix]
    shapes = [
        jax.ShapeDtypeStruct(matrix[0].shape, F32) for matrix in matrices for _ in range(3)
    ] + [jax.ShapeDtypeStruct(before.shape, F32)]
    out = pl.pallas_call(
        functools.partial(adam_kernel, names, offsets, scale),
        out_shape=shapes,
        compiler_params=pltpu.CompilerParams(vmem_limit_bytes=VMEM_LIMIT),
        name="adam",
    )(*args, before)
    return [out[3 * i : 3 * i + 3] for i in range(len(names))], out[-1]


def apply_kernel(names, scale, *refs):
    count = len(names)
    gathered_ref, pairs, rest = refs[0], refs[1 : 1 + 2 * count], refs[1 + 2 * count :]
    small_ins, outs = rest[:9], rest[9:]
    sums = jnp.sum(gathered_ref[:, 0], axis=0, keepdims=True)
    roots = jnp.sqrt(sums)
    for place, name in enumerate(names):
        weight_ref, update_ref = pairs[2 * place : 2 * place + 2]
        for part, where in enumerate(pieces_of(weight_ref)):
            lane = SQUARES[name] + part
            ratio = roots[:, lane : lane + 1] / roots[:, lane + MATRICES : lane + MATRICES + 1]
            outs[place][where] = weight_ref[where] - 0.25 * ratio * update_ref[where]
    slices = gathered_ref.shape[1] - 1
    line = 0
    for place in range(3):
        weight_ref, first_ref, second_ref = small_ins[3 * place : 3 * place + 3]
        rows, columns = weight_ref.shape
        lines = []
        for _ in range(rows):
            parts = []
            for _ in range(columns // LANES):
                device, slot = divmod(line, slices)
                parts.append(gathered_ref[device, 1 + slot : 2 + slot])
                line += 1
            lines.append(jnp.concatenate(parts, axis=1))
        grad = jnp.concatenate(lines, axis=0) * scale
        results = small_step(weight_ref[...], grad, first_ref[...], second_ref[...])
        for out_ref, result in zip(outs[count + 3 * place : count + 3 * place + 3], results):
            out_ref[...] = result


def apply_updates(names, gathered, pairs, small, scale):
    shapes = [jax.ShapeDtypeStruct(weight.shape, F32) for weight, _ in pairs] + [
        jax.ShapeDtypeStruct(array.shape, F32) for array in small
    ]
    return pl.pallas_call(
        functools.partial(apply_kernel, names, scale),
        out_shape=shapes,
        compiler_params=pltpu.CompilerParams(vmem_limit_bytes=VMEM_LIMIT),
        name="apply_updates",
    )(gathered, *(array for pair in pairs for array in pair), *small)


def small_step(weight, gradient, first_moment, second):
    new_first, new_second, update = adam_direction(weight, gradient, first_moment, second, 0.0)
    trust_ratio = jnp.sqrt(jnp.sum(weight * weight, axis=-1, keepdims=True)) / jnp.sqrt(
        jnp.sum(update * update, axis=-1, keepdims=True)
    )
    return (weight - 0.25 * trust_ratio * update, new_first, new_second)


def shards(
    tokens,
    prob_masks,
    branch_masks,
    attn_weight,
    attn_first,
    attn_second,
    out_weight,
    out_first,
    out_second,
    up_weight,
    up_first,
    up_second,
    down_weight,
    down_first,
    down_second,
    gains,
    gains_first,
    gains_second,
    shifts,
    shifts_first,
    shifts_second,
    hidden_bias,
    hidden_first,
    hidden_second,
):
    tensor_count = lax.axis_size("tensor")
    tensor_rank = lax.axis_index("tensor")
    data_count = lax.axis_size("dp")
    data_rank = lax.axis_index("dp")
    seq_local, half_len, width = tokens.shape
    assert tensor_count == 2 and seq_local == 2
    seq_len = half_len * tensor_count
    heads_local = prob_masks.shape[2]
    local_width = heads_local * HD
    hidden_local = up_weight.shape[1]
    rows_local = width // data_count
    scale_loss = 64.0 * data_count * seq_local * seq_len
    chunk = min(256, seq_len)
    is_first = tensor_rank == 0

    def in_order(mine, others, axis):
        return jnp.where(
            is_first,
            jnp.concatenate([mine, others], axis=axis),
            jnp.concatenate([others, mine], axis=axis),
        )

    def of_rank(whole, axis, length):
        mine = lax.dynamic_slice_in_dim(whole, tensor_rank * length, length, axis)
        others = lax.dynamic_slice_in_dim(whole, (1 - tensor_rank) * length, length, axis)
        return mine, others

    own_tokens, send_tokens = of_rank(tokens, 0, 1)
    words = jnp.pad(
        jnp.swapaxes(prob_masks.astype(jnp.int16), 3, 4),
        ((0, 0), (0, 0), (0, 0), (0, -prob_masks.shape[4] % 16), (0, 0)),
    )
    own_words, send_words = of_rank(words, 1, 1)
    branch_words = jnp.pad(
        jnp.swapaxes(branch_masks.astype(jnp.int16), 3, 4),
        ((0, 0), (0, 0), (0, 0), (0, -branch_masks.shape[4] % 16), (0, 0)),
    )
    own_branch, send_branch = of_rank(branch_words, 2, 1)

    order = jnp.asarray(np.array(gathered_order(data_count), np.int32))
    owner = jnp.bitwise_xor(order, data_rank)
    feature = (owner[:, None] * rows_local + jnp.arange(rows_local, dtype=jnp.int32)).reshape(-1)
    places = lax.broadcasted_iota(jnp.int32, (width, width), 0)
    to_own = (places == feature[None, :]).astype(F32)
    to_own_low = to_own.astype(BF)

    attn_block = attn_weight.astype(BF).reshape(rows_local, 3 * local_width)
    out_block = out_weight.astype(BF).T
    up_block = up_weight.astype(BF)
    down_block = down_weight.astype(BF).T
    device_count = data_count * tensor_count
    down_blocks = lax.all_gather(down_block, ("dp", "tensor"), axis=0, tiled=False)
    branch_rows_padded = branch_words.shape[3]
    word = feature // BRANCH_BITS
    bit = feature % BRANCH_BITS
    high = bit >= LOW_BITS
    row = jnp.where(high, word + branch_rows_padded, word)
    power = jnp.exp2(-jnp.where(high, bit - LOW_BITS, bit).astype(F32))
    branch_select = jnp.where(
        lax.broadcasted_iota(jnp.int32, (2 * branch_rows_padded, width), 0) == row[None, :],
        power[None, :],
        0.0,
    ).astype(BF)

    bias_q = of_rank(shifts[0], 0, local_width)
    bias_v = of_rank(shifts[1], 0, local_width)

    def project(half, rows, matrix):
        bias = jnp.concatenate([bias_q[half], jnp.zeros_like(bias_q[half]), bias_v[half]])
        return (dot(rows, matrix, 1, 0) + bias).astype(BF)

    first_bit, *later_bits = [bit for group in upper_groups() for bit in group]
    token_other = swap_tensor(send_tokens)
    attn_quarter = gather_upper(attn_block)
    wide_quarter = jnp.concatenate([out_block, up_block], axis=1)
    wide_sent = swap_dp(wide_quarter, 1 << first_bit)
    own_keep = prob_keep(own_words[:, 0], seq_len)
    attn_quarter, own_keep, wide_sent = together(attn_quarter, own_keep, wide_sent)

    attn_beside, attn_across = swap_dp(attn_quarter, 2), swap_tensor(attn_quarter)
    wide_quarter = joined([wide_quarter, wide_sent])
    for bit in later_bits[:-1]:
        wide_quarter = gather_bit(wide_quarter, bit)
    wide_sent = swap_dp(wide_quarter, 1 << later_bits[-1])
    token_rows = in_order(own_tokens[0], token_other[0], 0)
    token_own = dot(token_rows, to_own_low, 1, 0).astype(BF)
    attn_beside, attn_across, token_own, wide_quarter = together(
        attn_beside, attn_across, token_own, wide_quarter
    )

    attn_corner = swap_dp(attn_across, 2)
    other_words = swap_tensor(tie(send_words, attn_across))
    attn_near = gather_core((attn_quarter, attn_beside))
    qkv_own = project(0, token_own, attn_near)
    attn_corner, qkv_own, wide_sent, wide_quarter = together(
        attn_corner, qkv_own, wide_sent, wide_quarter
    )

    wide_quarter = joined([wide_quarter, wide_sent])
    wide_beside = swap_dp(wide_quarter, 2)
    wide_across = swap_tensor(wide_quarter)
    attended = attend(qkv_own, own_keep, chunk)
    other_keep = prob_keep(other_words[:, 0], seq_len)
    attn_far = gather_core((attn_across, attn_corner))
    qkv_other = project(1, token_own, attn_far)
    attended, other_keep, qkv_other, wide_beside, wide_across = together(
        attended, other_keep, qkv_other, wide_beside, wide_across
    )

    wide_corner = swap_dp(wide_across, 2)
    branch_other = swap_tensor(tie(send_branch, wide_across))
    attended_other = attend(qkv_other, other_keep, chunk)
    branch_rows = in_order(own_branch[:, :, 0], branch_other[:, :, 0], 3)
    keeps = branch_keep(branch_rows, branch_select)
    down_places = jnp.stack(
        [owner * tensor_count + tensor_rank, owner * tensor_count + (1 - tensor_rank)]
    ).astype(jnp.int32)
    down_blocks, down_places = whole_tiles(
        down_blocks.reshape(device_count, rows_local, hidden_local), down_places
    )
    wide_corner, attended_other, keeps, down_blocks = together(
        wide_corner, attended_other, keeps, down_blocks
    )
    attn_low = [attn_near, attn_far]
    wide_pieces = [
        quarters + tuple(swap_dp(quarter, 1) for quarter in quarters)
        for quarters in ((wide_quarter, wide_beside), (wide_across, wide_corner))
    ]
    qkv = [qkv_own, qkv_other]
    contexts = [attended[0], attended_other[0]]
    logsums = [attended[1], attended_other[1]]
    keep_halves = (own_keep, other_keep)
    vectors = dot(jnp.concatenate([gains, shifts[2:6]], axis=0), to_own, 1, 0, EXACT)
    context_flat = [c.reshape(2 * seq_len, local_width) for c in contexts]
    unit_one, inverse_one, *out_low = first_norm(
        vectors, contexts, wide_pieces, token_own, keeps[0]
    )
    hidden_halves = jnp.stack(of_rank(hidden_bias, 0, hidden_local))
    normed_low, active_own, active_other, slope_own, slope_other, unit_two, inverse_two, unit_sum = hidden_units(
        vectors,
        hidden_halves,
        unit_one,
        keeps[1],
        wide_pieces,
        local_width,
        down_blocks,
        down_places,
    )
    normed_low = normed_low.reshape(2 * seq_len, width)
    active = [a.reshape(2 * seq_len, hidden_local) for a in (active_own, active_other)]
    gain_two = vectors[GAIN_TWO]
    shift_two = vectors[SHIFT_TWO]
    pooled = unit_sum * gain_two / seq_len + shift_two
    pooled_rows = dot(pooled, to_own, 1, 1, EXACT)
    everyone = jnp.swapaxes(everyones(pooled_rows), 0, 1)
    place = (data_rank * tensor_count + tensor_rank).astype(jnp.int32).reshape(1)
    loss_value, grad_pooled = loss_and_grad(everyone, place, scale_loss)
    grad_rows = dot(grad_pooled, to_own, 1, 0, EXACT) / seq_len

    grad_shift_two = jnp.sum(grad_rows, axis=0) * seq_len
    grad_gain_two = jnp.sum(grad_rows * unit_sum, axis=0)
    grad_second, grad_ffn = second_back(vectors, grad_rows, unit_two, inverse_two, keeps[1])
    grad_ffn_flat = grad_ffn.reshape(2 * seq_len, width)
    half_width, quarter_width = width // 2, width // 4

    def weight_grads(left, right):
        return (
            dot(left[:, :half_width], right, 0, 0),
            dot(left[:, half_width:], right, 0, 0),
        )

    def both_cores(grads):
        kept, sent = grads
        return kept, swap_dp(sent, 1)

    def rows_of(parts, first):
        return tuple(
            part[:quarter_width] if first else part[quarter_width:] for part in parts
        )

    def low_sum(parts):
        return added(*parts).astype(BF)

    def context_back(half, grad_rows):
        return dot(grad_rows, out_low[half], 1, 0).astype(BF)

    def queries_back(half, grad_context):
        return attend_back(
            qkv[half],
            keep_halves[half],
            logsums[half],
            contexts[half],
            grad_context.reshape(2, seq_len, local_width),
            chunk,
        )

    eighth = quarter_width // 2

    def corner_out(other):
        return (
            swap_tensor(added(*(p[quarter_width : quarter_width + eighth] for p in other)).astype(BF)),
            swap_dp(added(*(p[quarter_width + eighth :] for p in other)).astype(BF), 2),
        )

    def sides_sent(own, other, corner):
        from_tensor, from_beside = corner
        to_tensor = jnp.concatenate(
            [
                low_sum(tuple(p[:eighth] for p in other)),
                low_sum(tuple(p[eighth:quarter_width] for p in other) + (from_beside,)),
            ]
        )
        to_beside = jnp.concatenate(
            [
                low_sum(
                    tuple(p[quarter_width : quarter_width + eighth] for p in own) + (from_tensor,)
                ),
                low_sum(tuple(p[quarter_width + eighth :] for p in own)),
            ]
        )
        return to_tensor, to_beside

    def sides_out(sent):
        return swap_tensor(sent[0]), swap_dp(sent[1], 2)

    def side_by_side(first, second):
        return tuple(jnp.concatenate(pair, axis=1) for pair in zip(first, second))

    rows_shape = (2, seq_len, width)
    down_other = weight_grads(grad_ffn_flat, active[1])
    down_own = weight_grads(grad_ffn_flat, active[0])
    down_other, down_own, grad_ffn_flat = together(down_other, down_own, grad_ffn_flat)

    down_other, down_own = both_cores(down_other), both_cores(down_own)
    grad_hidden_own, back, hidden_sums_own = own_back(
        grad_ffn_flat.reshape(rows_shape),
        slope_own,
        grad_second,
        wide_pieces[0],
        local_width,
        down_blocks,
        down_places,
    )
    down_other, down_own, back = together(down_other, down_own, back)

    down_corner = corner_out(down_other)
    grad_hidden_other, grad_attn, grad_first, column_sums, hidden_sums_other = other_back(
        vectors,
        grad_ffn_flat.reshape(rows_shape),
        slope_other,
        back,
        unit_one,
        inverse_one,
        keeps[0],
        wide_pieces[1],
        local_width,
        down_blocks,
        down_places,
    )
    down_corner, grad_hidden_other, grad_attn = together(down_corner, grad_hidden_other, grad_attn)
    grad_attn_flat = grad_attn.reshape(2 * seq_len, width)

    down_sent = sides_sent(down_own, down_other, down_corner)
    up_other = weight_grads(
        tie(normed_low, *down_sent), grad_hidden_other.reshape(2 * seq_len, hidden_local)
    )
    up_own = weight_grads(normed_low, grad_hidden_own.reshape(2 * seq_len, hidden_local))
    up_other, up_own = both_cores(up_other), both_cores(up_own)
    out_other = both_cores(weight_grads(grad_attn_flat, context_flat[1]))
    out_own = both_cores(weight_grads(grad_attn_flat, context_flat[0]))
    down_sides = sides_out(down_sent)
    context_other = context_back(1, grad_attn_flat)
    down_sides, up_other, up_own, out_other, out_own, context_other = together(
        down_sides, up_other, up_own, out_other, out_own, context_other
    )

    wide_other, wide_own = side_by_side(out_other, up_other), side_by_side(out_own, up_own)
    wide_corner = corner_out(wide_other)
    down_parts = rows_of(down_own, True) + down_sides
    grad_other = queries_back(1, context_other)
    wide_corner, grad_other = together(wide_corner, grad_other)

    wide_leaving = sides_sent(wide_own, wide_other, wide_corner)
    wide_sides = sides_out(wide_leaving)
    down_reduced = upper_parts(down_parts)
    attn_other = both_cores(weight_grads(token_own, tie(grad_other, *wide_leaving)))
    context_own = context_back(0, grad_attn_flat)
    token_back = dot(grad_other, attn_low[1], 1, 1) + grad_first
    attn_other, context_own, token_back, wide_sides, down_reduced = together(
        attn_other, context_own, token_back, wide_sides, down_reduced
    )

    attn_sent = low_sum(attn_other)
    attn_across = swap_tensor(attn_sent)
    wide_reduced = upper_parts(rows_of(wide_own, True) + wide_sides)
    grad_own = queries_back(0, tie(context_own, attn_sent))
    attn_own = weight_grads(token_own, grad_own)
    attn_across, wide_reduced, attn_own, grad_own = together(
        attn_across, wide_reduced, attn_own, grad_own
    )

    attn_own = both_cores(attn_own)
    token_back = token_back + dot(grad_own, attn_low[0], 1, 1)
    attn_own, token_back = together(attn_own, token_back)
    attn_own = attn_own + (attn_across,)
    attn_sent = low_sum(rows_of(attn_own, False))
    attn_beside = swap_dp(attn_sent, 2)
    token_grad = dot(tie(token_back, attn_sent), to_own, 1, 1, EXACT)
    grad_own = tie(grad_own, attn_sent)
    hidden_sums = (hidden_sums_own[0], hidden_sums_other[0])
    grad_qkv = [grad_own, grad_other]
    bias_sums = [jnp.sum(grad_qkv[half].astype(F32), axis=0) for half in range(2)]
    query_row = in_order(bias_sums[0][:local_width], bias_sums[1][:local_width], 0)
    value_row = in_order(bias_sums[0][2 * local_width :], bias_sums[1][2 * local_width :], 0)
    hidden_row = in_order(hidden_sums[0], hidden_sums[1], 0)
    feature_rows = dot(
        jnp.stack(
            [
                column_sums[0],
                grad_gain_two,
                column_sums[2],
                column_sums[1],
                column_sums[3],
                grad_shift_two,
            ]
        ),
        to_own,
        1,
        1,
        EXACT,
    )
    small = jnp.concatenate(
        [
            feature_rows[:2],
            query_row[None],
            value_row[None],
            feature_rows[2:],
            hidden_row.reshape(-1, width),
        ],
        axis=0,
    )
    small_sums = slices_summed(small.reshape(-1)).reshape(-1, LANES)
    attn_beside, token_grad, small_sums = together(attn_beside, token_grad, small_sums)
    attn_reduced = added(*upper_parts(rows_of(attn_own, True) + (attn_beside,)))
    down_reduced, wide_reduced = added(*down_reduced), added(*wide_reduced)
    own_half, send_half = of_rank(token_grad, 0, half_len)
    grad_tokens = in_order(own_half[None], swap_tensor(send_half.astype(BF))[None].astype(F32), 0)

    inverse_scale = 1.0 / scale_loss

    def turned(*arrays):
        return [array.T for array in arrays]

    def parts_first(*arrays):
        return [jnp.transpose(array, (1, 0, 2)) for array in arrays]

    down_own_weight, down_firsts, down_seconds = turned(down_weight, down_first, down_second)
    out_own_weight, out_firsts, out_seconds = turned(out_weight, out_first, out_second)
    attn_parts, attn_firsts, attn_seconds = parts_first(attn_weight, attn_first, attn_second)
    (down_new,), sums = adam(
        ("down",),
        (0,),
        ((down_own_weight, down_reduced, down_firsts, down_seconds),),
        jnp.zeros((1, LANES), F32),
        inverse_scale,
    )
    (up_new, out_new, attn_new), sums = adam(
        ("up", "out", "attn"),
        (local_width, 0, 0),
        (
            (up_weight, wide_reduced, up_first, up_second),
            (out_own_weight, wide_reduced, out_firsts, out_seconds),
            (attn_parts, attn_reduced, attn_firsts, attn_seconds),
        ),
        sums,
        inverse_scale,
    )
    hidden_args = [array.reshape(1, -1) for array in (hidden_bias, hidden_first, hidden_second)]
    gathered = everyones(jnp.concatenate([sums, small_sums], axis=0))
    gathered, grad_tokens = together(gathered, grad_tokens)
    (
        new_attn,
        new_out,
        new_up,
        new_down,
        new_gains,
        new_gains_first,
        new_gains_second,
        new_shifts,
        new_shifts_first,
        new_shifts_second,
        new_hidden,
        new_hidden_first,
        new_hidden_second,
    ) = apply_updates(
        ("attn", "out", "up", "down"),
        gathered,
        (
            (attn_parts, attn_new[2]),
            (out_own_weight, out_new[2]),
            (up_weight, up_new[2]),
            (down_own_weight, down_new[2]),
        ),
        (gains, gains_first, gains_second, shifts, shifts_first, shifts_second, *hidden_args),
        inverse_scale,
    )
    new_hidden, new_hidden_first, new_hidden_second = (
        array.reshape(-1) for array in (new_hidden, new_hidden_first, new_hidden_second)
    )
    new_attn, attn_new_first, attn_new_second = parts_first(new_attn, attn_new[0], attn_new[1])
    new_out, out_new_first, out_new_second = turned(new_out, out_new[0], out_new[1])
    new_down, down_new_first, down_new_second = turned(new_down, down_new[0], down_new[1])
    up_new_first, up_new_second = up_new[:2]
    return (
        loss_value.reshape(()),
        grad_tokens,
        new_attn,
        attn_new_first,
        attn_new_second,
        new_out,
        out_new_first,
        out_new_second,
        new_up,
        up_new_first,
        up_new_second,
        new_down,
        down_new_first,
        down_new_second,
        new_gains,
        new_gains_first,
        new_gains_second,
        new_shifts,
        new_shifts_first,
        new_shifts_second,
        new_hidden,
        new_hidden_first,
        new_hidden_second,
    )


def solution(mesh):
    row_split = P("dp", None, "tensor")
    column_split = P("tensor", "dp")
    matrix_split = P("dp", "tensor")
    return jax.shard_map(
        shards,
        mesh=mesh,
        in_specs=(
            P("dp", "tensor", None),
            P(None, "dp", "tensor", None, None),
            P(None, None, "dp", "tensor", None),
        )
        + (row_split,) * 3
        + (column_split,) * 3
        + (matrix_split,) * 3
        + (column_split,) * 3
        + (P(),) * 9,
        out_specs=(P(), P("dp", "tensor", None))
        + (row_split,) * 3
        + (column_split,) * 3
        + (matrix_split,) * 3
        + (column_split,) * 3
        + (P(),) * 9,
        check_vma=False,
    )
```

```python
import functools

import jax
import jax.numpy as jnp
import numpy as np
from jax import lax
from jax.experimental import pallas as pl
from jax.experimental.pallas import tpu as pltpu
from jax.sharding import PartitionSpec as P

HD = 64
STEP = 10
KEEP_SCALE = 1.0 / 0.9
PROB_BITS = 13
BRANCH_BITS = 15
LOW_BITS = 7
BF = jnp.bfloat16
F32 = jnp.float32
EXACT = lax.Precision.HIGHEST
VMEM_LIMIT = 56 << 20


def work(flops):
    return pl.CostEstimate(flops=int(flops), bytes_accessed=0, transcendentals=0)


def dot(left, right, left_dim, right_dim, precision=None):
    return lax.dot_general(
        left,
        right,
        (((left_dim,), (right_dim,)), ((), ())),
        preferred_element_type=F32,
        precision=precision,
    )


def swap_dp(value, distance):
    count = lax.axis_size("dp")
    return lax.ppermute(value, "dp", [(i, i ^ distance) for i in range(count)])


def swap_tensor(value):
    return lax.ppermute(value, "tensor", [(0, 1), (1, 0)])


def bit_groups(count):
    bits = count.bit_length() - 1
    groups, top = [], bits
    while top - 2 >= 2:
        groups.append((top - 2, top - 1))
        top -= 2
    while top > 0:
        groups.append((top - 1,))
        top -= 1
    return groups


def distances(group):
    out = [0]
    for bit in group:
        out = out + [o | (1 << bit) for o in out]
    return out


def gathered_order(count):
    order = [0]
    for group in bit_groups(count):
        order = [o | step for step in distances(group) for o in order]
    return order


def joined_kernel(spans, *refs):
    count = len(refs) - 1 - len(spans)
    pieces, out_refs, arrived = refs[:count], refs[count:-1], refs[-1]
    copies, start = [], 0
    for index, piece in enumerate(pieces):
        rows = piece.shape[0]
        for place, (first, last) in enumerate(spans):
            copies.append(
                pltpu.make_async_copy(
                    piece.at[:, pl.ds(first, last - first)],
                    out_refs[place].at[pl.ds(start, rows)],
                    arrived.at[index, place],
                )
            )
        start += rows
    for copy in copies:
        copy.start()
    for copy in copies:
        copy.wait()


def joined(pieces, spans=None):
    rows = sum(piece.shape[0] for piece in pieces)
    columns = pieces[0].shape[1]
    parts = spans or ((0, columns),)
    if any(piece.shape[0] % 16 for piece in pieces):
        whole = jnp.concatenate(pieces, axis=0)
        return [whole[:, first:last] for first, last in parts] if spans else whole
    out = pl.pallas_call(
        functools.partial(joined_kernel, parts),
        in_specs=[pl.BlockSpec(memory_space=pl.ANY)] * len(pieces),
        out_specs=[pl.BlockSpec(memory_space=pltpu.VMEM)] * len(parts),
        out_shape=[
            jax.ShapeDtypeStruct((rows, last - first), pieces[0].dtype) for first, last in parts
        ],
        scratch_shapes=[pltpu.SemaphoreType.DMA((len(pieces), len(parts)))],
        compiler_params=pltpu.CompilerParams(vmem_limit_bytes=VMEM_LIMIT),
        name="joined",
    )(*pieces)
    return out if spans else out[0]


def tie(value, *others):
    return lax.optimization_barrier((value,) + others)[0]


def together(*values):
    return lax.optimization_barrier(values)


def upper_groups():
    return bit_groups(lax.axis_size("dp"))[:-2]


def gather_upper(block):
    for group in upper_groups():
        block = joined([block] + [swap_dp(block, s) for s in distances(group)[1:]])
    return block


def gather_bit(block, bit):
    return joined([block, swap_dp(block, 1 << bit)])


def gather_sides(mine, corner_by_tensor):
    beside = swap_dp(mine, 2)
    across = swap_tensor(mine)
    corner = swap_tensor(beside) if corner_by_tensor else swap_dp(across, 2)
    return (mine, beside), (across, corner)


def gather_core(quarters, spans=None):
    near, far = quarters
    return joined([near, far, swap_dp(near, 1), swap_dp(far, 1)], spans)


def upper_parts(parts):
    for group in reversed(upper_groups()):
        steps = distances(group)
        rows = parts[0].shape[0] // len(steps)
        kept_rows = [part[:rows].astype(F32) for part in parts]
        for index, step in enumerate(steps[1:], 1):
            sent = sum(part[index * rows : (index + 1) * rows].astype(F32) for part in parts)
            kept_rows.append(swap_dp(sent.astype(BF), step))
        parts = kept_rows
    return tuple(parts)


def added(*parts):
    return sum(part.astype(F32) for part in parts)


def slices_summed(values):
    count = lax.axis_size("dp") * lax.axis_size("tensor")
    values = jnp.pad(values, (0, -values.size % (128 * count)))
    spread = values.reshape(count, -1, 128)
    return jnp.sum(lax.all_to_all(spread, ("dp", "tensor"), 0, 0, tiled=True), axis=0).reshape(-1)


def everyones(value):
    count = lax.axis_size("dp") * lax.axis_size("tensor")
    spread = jnp.broadcast_to(value[None], (count,) + value.shape)
    return lax.all_to_all(spread, ("dp", "tensor"), 0, 0, tiled=True)


def selector(places, words, word_bits):
    out = np.zeros((places, 2 * words), np.float32)
    for place in range(places):
        word, bit = divmod(place, word_bits)
        if bit < LOW_BITS:
            out[place, word] = 2.0**-bit
        else:
            out[place, words + word] = 2.0 ** (LOW_BITS - bit)
    return out


def split_words(words):
    words = words.astype(jnp.int32)
    low = jnp.bitwise_and(words, (1 << LOW_BITS) - 1)
    high = jnp.right_shift(words, LOW_BITS)
    return jnp.concatenate([low.astype(F32), high.astype(F32)], axis=0).astype(BF)


def units_bit(values):
    return jnp.bitwise_and(values.astype(jnp.int32), 1).astype(F32).astype(BF)


def prob_keep_kernel(select_ref, words_ref, keep_ref):
    for view in range(2):
        keep_ref[view, 0] = units_bit(
            dot(select_ref[...], split_words(words_ref[view, 0]), 1, 0)
        )


def prob_keep(words, length):
    _, heads, rows, _ = words.shape
    select = jnp.asarray(selector(length, rows, PROB_BITS), BF)
    return pl.pallas_call(
        prob_keep_kernel,
        grid=(heads,),
        in_specs=[
            pl.BlockSpec(select.shape, lambda h: (0, 0)),
            pl.BlockSpec((2, 1, rows, length), lambda h: (0, h, 0, 0)),
        ],
        out_specs=pl.BlockSpec((2, 1, length, length), lambda h: (0, h, 0, 0)),
        out_shape=jax.ShapeDtypeStruct((2, heads, length, length), BF),
        compiler_params=pltpu.CompilerParams(vmem_limit_bytes=VMEM_LIMIT),
        name="prob_keep",
        cost_estimate=work(3.5e9),
    )(select, words)


def branch_keep_kernel(select_ref, words_ref, keep_ref):
    keep_ref[0, 0] = units_bit(dot(split_words(words_ref[0, 0]), select_ref[...], 0, 0))


def branch_keep(words, select):
    _, _, rows, length = words.shape
    width = select.shape[1]
    return pl.pallas_call(
        branch_keep_kernel,
        grid=(2, 2),
        in_specs=[
            pl.BlockSpec(select.shape, lambda b, v: (0, 0)),
            pl.BlockSpec((1, 1, rows, length), lambda b, v: (b, v, 0, 0)),
        ],
        out_specs=pl.BlockSpec((1, 1, length, width), lambda b, v: (b, v, 0, 0)),
        out_shape=jax.ShapeDtypeStruct((2, 2, length, width), BF),
        compiler_params=pltpu.CompilerParams(vmem_limit_bytes=VMEM_LIMIT),
        name="branch_keep",
        cost_estimate=work(2.5e9),
    )(select, words)


def head_lanes(shape, head):
    lane = lax.broadcasted_iota(jnp.int32, shape, 1)
    return jnp.logical_and(lane >= head * HD, lane < (head + 1) * HD)


def attend_kernel(chunk, q_ref, k_ref, v_ref, keep_ref, context_ref, logsum_ref, turned):
    length = q_ref.shape[0]
    queries = q_ref[...] * BF(0.125)
    key_rows = k_ref[...]
    values_turned = v_ref[...].T
    for head in range(2):
        own = jnp.where(head_lanes(queries.shape, head), queries, BF(0))
        span = slice(head * HD, (head + 1) * HD)
        for start in range(0, length, chunk):
            part = slice(start, start + chunk)
            scores = dot(key_rows, own[part], 1, 1)
            peak = jnp.max(scores, axis=0, keepdims=True)
            powers = jnp.exp(scores - peak)
            total = jnp.sum(powers, axis=0, keepdims=True)
            weighted = (powers * (KEEP_SCALE / total)).astype(BF)
            logsum_ref[head, :, part] = peak + jnp.log(total * (1.0 / KEEP_SCALE))
            for view in range(2):
                kept = weighted * keep_ref[view, head, :, part]
                turned[view, span, part] = dot(values_turned[span], kept, 1, 0).astype(BF)
    for view in range(2):
        context_ref[view] = turned[view].T


def attend(qkv, keep, chunk):
    length = qkv.shape[0]
    heads = keep.shape[1]
    pairs = heads // 2

    def part(p):
        return pl.BlockSpec((length, 2 * HD), lambda h: (0, p * pairs + h))

    return pl.pallas_call(
        functools.partial(attend_kernel, chunk),
        grid=(pairs,),
        in_specs=[
            part(0),
            part(1),
            part(2),
            pl.BlockSpec((2, 2, length, length), lambda h: (0, h, 0, 0)),
        ],
        out_specs=[
            pl.BlockSpec((2, length, 2 * HD), lambda h: (0, 0, h)),
            pl.BlockSpec((2, 1, length), lambda h: (h, 0, 0)),
        ],
        out_shape=[
            jax.ShapeDtypeStruct((2, length, heads * HD), BF),
            jax.ShapeDtypeStruct((heads, 1, length), F32),
        ],
        scratch_shapes=[pltpu.VMEM((2, 2 * HD, length), BF)],
        compiler_params=pltpu.CompilerParams(vmem_limit_bytes=VMEM_LIMIT),
        name="attend",
        cost_estimate=work(4e9),
    )(qkv, qkv, qkv, keep)


def attend_back_kernel(
    chunk,
    q_ref,
    k_ref,
    v_ref,
    keep_ref,
    logsum_ref,
    context_ref,
    grad_ref,
    out_ref,
    turned,
    grad_keys,
    grad_values,
):
    length = q_ref.shape[0]
    width = 2 * HD
    pairs = pl.num_programs(0)
    queries = q_ref[...] * BF(0.125)
    key_rows = k_ref[...]
    values = v_ref[...]
    keys_turned = key_rows.T
    grads = [grad_ref[0], grad_ref[1]]
    product = sum(
        grads[view].astype(F32) * context_ref[view].astype(F32) for view in range(2)
    ).T
    for head in range(2):
        span = slice(head * HD, (head + 1) * HD)
        mine = head_lanes(queries.shape, head)
        own = jnp.where(mine, queries, BF(0))
        own_grads = [jnp.where(mine, grad, BF(0)) for grad in grads]
        inner = jnp.sum(product[span], axis=0, keepdims=True) * (1.0 / KEEP_SCALE)
        total_keys, total_values = None, None
        for start in range(0, length, chunk):
            part = slice(start, start + chunk)
            scores = dot(key_rows, own[part], 1, 1)
            scaled = jnp.exp(scores - logsum_ref[head, :, part])
            weighted = scaled.astype(BF)
            change = None
            for view in range(2):
                keep = keep_ref[view, head, :, part]
                more = dot(weighted * keep, grads[view][part], 1, 0)
                total_values = more if total_values is None else total_values + more
                term = dot(values, own_grads[view][part], 1, 1) * keep.astype(F32)
                change = term if change is None else change + term
            grad_scores = (scaled * (change - inner[:, part])).astype(BF)
            more = dot(grad_scores, queries[part], 1, 0)
            total_keys = more if total_keys is None else total_keys + more
            turned[span, part] = (dot(keys_turned[span], grad_scores, 1, 0) * 0.125).astype(BF)
        if head == 0:
            grad_keys[...] = total_keys
            grad_values[...] = total_values
        else:
            grad_keys[...] = jnp.where(mine, total_keys, grad_keys[...])
            grad_values[...] = jnp.where(mine, total_values, grad_values[...])
    pair = pl.program_id(0)

    def columns(p):
        return pl.ds(pl.multiple_of((p * pairs + pair) * width, width), width)

    out_ref[:, columns(0)] = turned[...].T
    out_ref[:, columns(1)] = grad_keys[...].astype(BF)
    out_ref[:, columns(2)] = grad_values[...].astype(BF)


def attend_back(qkv, keep, logsum, context, grad_context, chunk):
    length = qkv.shape[0]
    heads = keep.shape[1]
    pairs = heads // 2

    def part(p):
        return pl.BlockSpec((length, 2 * HD), lambda h: (0, p * pairs + h))

    sides = pl.BlockSpec((2, length, 2 * HD), lambda h: (0, 0, h))
    return pl.pallas_call(
        functools.partial(attend_back_kernel, chunk),
        grid=(pairs,),
        in_specs=[
            part(0),
            part(1),
            part(2),
            pl.BlockSpec((2, 2, length, length), lambda h: (0, h, 0, 0)),
            pl.BlockSpec((2, 1, length), lambda h: (h, 0, 0)),
            sides,
            sides,
        ],
        out_specs=pl.BlockSpec(qkv.shape, lambda h: (0, 0)),
        out_shape=jax.ShapeDtypeStruct(qkv.shape, BF),
        scratch_shapes=[
            pltpu.VMEM((2 * HD, length), BF),
            pltpu.VMEM((length, 2 * HD), F32),
            pltpu.VMEM((length, 2 * HD), F32),
        ],
        compiler_params=pltpu.CompilerParams(vmem_limit_bytes=VMEM_LIMIT),
        name="attend_back",
        cost_estimate=work(6e9),
    )(qkv, qkv, qkv, keep, logsum, context, grad_context)


GAIN_ONE, GAIN_TWO, OUT_BIAS, SHIFT_ONE, DOWN_BIAS, SHIFT_TWO = range(6)
ROWS = 128
COLUMNS = 256


def rows_block(width):
    return pl.BlockSpec((2, ROWS, width), lambda i: (0, i, 0))


def constant_block(shape):
    return pl.BlockSpec(shape, lambda i: (0,) * len(shape), pipeline_mode=pl.Buffered(1))


def flat(values):
    return values.reshape(values.shape[0] * values.shape[1], values.shape[2])


def norm_parts(values):
    center = values - jnp.mean(values, axis=-1, keepdims=True)
    spread = jnp.mean(center * center, axis=-1, keepdims=True)
    inverse = lax.rsqrt(spread + 1e-12)
    return center * inverse, inverse


def norm_back(grad, unit, inverse, gain):
    scaled = grad * gain
    mean = jnp.mean(scaled, axis=-1, keepdims=True)
    along = jnp.mean(scaled * unit, axis=-1, keepdims=True)
    return inverse * (scaled - mean - unit * along)


def kept(keep_ref):
    return flat(keep_ref[...]).astype(F32) * KEEP_SCALE


def row_copies(pieces, first, target, arrived):
    copies, start = [], 0
    for index, piece in enumerate(pieces):
        rows = piece.shape[0]
        copies.append(
            pltpu.make_async_copy(
                piece.at[:, pl.ds(first, target.shape[1])],
                target.at[pl.ds(start, rows)],
                arrived.at[index],
            )
        )
        start += rows
    return copies


def at_first_step(action):
    pl.when(pl.program_id(0) == 0)(action)


def start_all(copies):
    for copy in copies:
        copy.start()


def wait_all(copies):
    for copy in copies:
        copy.wait()


def far_spec():
    return pl.BlockSpec(memory_space=pl.ANY)


def first_norm_kernel(*refs):
    vectors_ref, own_ref, other_ref, token_ref, keep_ref = refs[:5]
    pieces, (unit_ref, inverse_ref, own_out, other_out), arrived = refs[5:-6], refs[-6:-2], refs[-2:]
    count = arrived[0].shape[0]
    copies = row_copies(pieces[:count], 0, own_out, arrived[0]) + row_copies(
        pieces[count:], 0, other_out, arrived[1]
    )

    @at_first_step
    def _():
        start_all(copies)
        wait_all(copies)

    attn_out = dot(flat(own_ref[...]), own_out[...], 1, 1) + dot(
        flat(other_ref[...]), other_out[...], 1, 1
    )
    change = (attn_out + vectors_ref[OUT_BIAS : OUT_BIAS + 1]) * kept(keep_ref)
    token = token_ref[...].astype(F32)
    unit, inverse = norm_parts(change.reshape(unit_ref.shape) + token[None])
    unit_ref[...] = unit
    inverse_ref[...] = inverse


def first_norm(vectors, contexts, pieces, token, keep):
    _, length, width = keep.shape
    local = contexts[0].shape[2]
    whole = pl.BlockSpec((width, local), lambda i: (0, 0))
    return pl.pallas_call(
        first_norm_kernel,
        grid=(length // ROWS,),
        in_specs=[constant_block(vectors.shape)]
        + [rows_block(local)] * 2
        + [pl.BlockSpec((ROWS, width), lambda i: (i, 0)), rows_block(width)]
        + [far_spec()] * (len(pieces[0]) + len(pieces[1])),
        out_specs=[rows_block(width), rows_block(1), whole, whole],
        out_shape=[
            jax.ShapeDtypeStruct((2, length, width), F32),
            jax.ShapeDtypeStruct((2, length, 1), F32),
            jax.ShapeDtypeStruct((width, local), BF),
            jax.ShapeDtypeStruct((width, local), BF),
        ],
        scratch_shapes=[pltpu.SemaphoreType.DMA((len(half),)) for half in pieces],
        compiler_params=pltpu.CompilerParams(vmem_limit_bytes=VMEM_LIMIT),
        name="first_norm",
        cost_estimate=work(3.5e9),
    )(vectors, *contexts, token, keep, *pieces[0], *pieces[1])


def hidden_kernel(first, *refs):
    vectors_ref, bias_ref, unit_ref, keep_ref = refs[:4]
    pieces, rest = refs[4:-16], refs[-16:]
    low_ref, active_own, active_other, slope_own, slope_other = rest[:5]
    unit_two_ref, inverse_two_ref, sum_ref = rest[5:8]
    up_own, up_other, down_own, down_other = rest[8:12]
    up_arrived, down_arrived = rest[12:14], rest[14:16]
    count = up_arrived[0].shape[0]
    sides = (pieces[:count], pieces[count:])
    hidden = up_own.shape[1]
    up_copies = [
        row_copies(sides[half], first, up, up_arrived[half])
        for half, up in enumerate((up_own, up_other))
    ]
    down_copies = [
        row_copies(sides[half], first + hidden, down, down_arrived[half])
        for half, down in enumerate((down_own, down_other))
    ]

    @at_first_step
    def _():
        for half in range(2):
            start_all(up_copies[half])
            start_all(down_copies[half])

    vector = lambda row: vectors_ref[row : row + 1]
    normed = flat(unit_ref[...]) * vector(GAIN_ONE) + vector(SHIFT_ONE)
    low = normed.astype(BF)
    low_ref[...] = low.reshape(low_ref.shape)
    hidden = up_own.shape[1]
    step = min(COLUMNS, hidden)
    total = vector(DOWN_BIAS)
    for half, (up, down, active_ref, slope_ref) in enumerate(
        (
            (up_own, down_own, active_own, slope_own),
            (up_other, down_other, active_other, slope_other),
        )
    ):
        at_first_step(functools.partial(wait_all, up_copies[half] + down_copies[half]))
        for start in range(0, hidden, step):
            part = slice(start, start + step)
            pre = dot(low, up[:, part], 1, 0) + bias_ref[half : half + 1, part]
            cumulative = 0.5 + 0.5 * lax.erf(pre * (0.5**0.5))
            density = jnp.exp(-0.5 * pre * pre) * (1.0 / (2.0 * np.pi) ** 0.5)
            active = (pre * cumulative).astype(BF)
            slope = (cumulative + pre * density).astype(BF)
            active_ref[:, :, part] = active.reshape(2, ROWS, step)
            slope_ref[:, :, part] = slope.reshape(2, ROWS, step)
            total = total + dot(active, down[:, part], 1, 1)
    unit, inverse = norm_parts((normed + total * kept(keep_ref)).reshape(unit_two_ref.shape))
    unit_two_ref[...] = unit
    inverse_two_ref[...] = inverse
    added_rows = jnp.sum(unit, axis=1)

    @at_first_step
    def _():
        sum_ref[...] = added_rows

    @pl.when(pl.program_id(0) > 0)
    def _():
        sum_ref[...] += added_rows


def weights_scratch(width, hidden, *pieces):
    return (
        [pltpu.VMEM((width, hidden), BF)] * (2 * len(pieces))
        + [pltpu.SemaphoreType.DMA((len(half),)) for half in pieces]
        + [pltpu.SemaphoreType.DMA((len(half),)) for half in pieces]
    )


def hidden_units(vectors, bias, unit, keep, pieces, first):
    _, length, width = keep.shape
    hidden = (pieces[0][0].shape[1] - first) // 2
    return pl.pallas_call(
        functools.partial(hidden_kernel, first),
        grid=(length // ROWS,),
        in_specs=[
            constant_block(vectors.shape),
            constant_block(bias.shape),
            rows_block(width),
            rows_block(width),
        ]
        + [far_spec()] * (len(pieces[0]) + len(pieces[1])),
        out_specs=[
            rows_block(width),
            rows_block(hidden),
            rows_block(hidden),
            rows_block(hidden),
            rows_block(hidden),
            rows_block(width),
            rows_block(1),
            pl.BlockSpec((2, width), lambda i: (0, 0)),
        ],
        out_shape=[
            jax.ShapeDtypeStruct((2, length, width), BF),
            jax.ShapeDtypeStruct((2, length, hidden), BF),
            jax.ShapeDtypeStruct((2, length, hidden), BF),
            jax.ShapeDtypeStruct((2, length, hidden), BF),
            jax.ShapeDtypeStruct((2, length, hidden), BF),
            jax.ShapeDtypeStruct((2, length, width), F32),
            jax.ShapeDtypeStruct((2, length, 1), F32),
            jax.ShapeDtypeStruct((2, width), F32),
        ],
        scratch_shapes=weights_scratch(width, hidden, *pieces),
        compiler_params=pltpu.CompilerParams(vmem_limit_bytes=VMEM_LIMIT),
        name="hidden_units",
        cost_estimate=work(11e9),
    )(vectors, bias, unit, keep, *pieces[0], *pieces[1])


def second_back_kernel(
    vectors_ref, rows_ref, unit_ref, inverse_ref, keep_ref, second_ref, low_ref
):
    grad = norm_back(
        rows_ref[...][:, None, :],
        unit_ref[...],
        inverse_ref[...],
        vectors_ref[GAIN_TWO : GAIN_TWO + 1],
    )
    second_ref[...] = grad
    low_ref[...] = (grad * (keep_ref[...].astype(F32) * KEEP_SCALE)).astype(BF)


def second_back(vectors, rows, unit, inverse, keep):
    _, length, width = keep.shape
    return pl.pallas_call(
        second_back_kernel,
        grid=(length // ROWS,),
        in_specs=[
            constant_block(vectors.shape),
            constant_block(rows.shape),
            rows_block(width),
            rows_block(1),
            rows_block(width),
        ],
        out_specs=[rows_block(width)] * 2,
        out_shape=[
            jax.ShapeDtypeStruct(keep.shape, F32),
            jax.ShapeDtypeStruct(keep.shape, BF),
        ],
        compiler_params=pltpu.CompilerParams(vmem_limit_bytes=VMEM_LIMIT),
        name="second_back",
        cost_estimate=work(3e9),
    )(vectors, rows, unit, inverse, keep)


def half_back(grad, slope_ref, up, down, hidden_ref, hidden_sums_ref, back):
    hidden = up.shape[1]
    step = min(COLUMNS, hidden)
    for start in range(0, hidden, step):
        part = slice(start, start + step)
        slope = flat(slope_ref[:, :, part]).astype(F32)
        grad_hidden = (dot(grad, down[:, part], 1, 0) * slope).astype(BF)
        hidden_ref[:, :, part] = grad_hidden.reshape(2, ROWS, step)
        hidden_sums_ref[:, part] += jnp.sum(grad_hidden.astype(F32), axis=0, keepdims=True)
        back = back + dot(grad_hidden, up[:, part], 1, 1)
    return back


def own_back_kernel(first, *refs):
    grad_ref, slope_ref, second_ref = refs[:3]
    pieces = refs[3:-7]
    hidden_ref, back_ref, hidden_sums_ref, up, down, up_arrived, down_arrived = refs[-7:]
    copies = row_copies(pieces, first, up, up_arrived) + row_copies(
        pieces, first + up.shape[1], down, down_arrived
    )

    @at_first_step
    def _():
        start_all(copies)
        hidden_sums_ref[...] = jnp.zeros_like(hidden_sums_ref)
        wait_all(copies)

    back = half_back(
        flat(grad_ref[...]),
        slope_ref,
        up,
        down,
        hidden_ref,
        hidden_sums_ref,
        flat(second_ref[...]),
    )
    back_ref[...] = back.reshape(back_ref.shape)


def own_back(grad, slope, second, pieces, first):
    _, length, width = grad.shape
    hidden = slope.shape[2]
    return pl.pallas_call(
        functools.partial(own_back_kernel, first),
        grid=(length // ROWS,),
        in_specs=[rows_block(width), rows_block(hidden), rows_block(width)]
        + [far_spec()] * len(pieces),
        out_specs=[
            rows_block(hidden),
            rows_block(width),
            pl.BlockSpec((1, hidden), lambda i: (0, 0)),
        ],
        out_shape=[
            jax.ShapeDtypeStruct((2, length, hidden), BF),
            jax.ShapeDtypeStruct((2, length, width), F32),
            jax.ShapeDtypeStruct((1, hidden), F32),
        ],
        scratch_shapes=weights_scratch(width, hidden, pieces),
        compiler_params=pltpu.CompilerParams(vmem_limit_bytes=VMEM_LIMIT),
        name="own_back",
        cost_estimate=work(6e9),
    )(grad, slope, second, *pieces)


def other_back_kernel(first, *refs):
    vectors_ref, grad_ref, slope_ref, before_ref = refs[:4]
    unit_ref, inverse_ref, keep_ref = refs[4:7]
    pieces = refs[7:-9]
    hidden_ref, attn_ref, first_ref, sums_ref, hidden_sums_ref = refs[-9:-4]
    up, down, up_arrived, down_arrived = refs[-4:]
    copies = row_copies(pieces, first, up, up_arrived) + row_copies(
        pieces, first + up.shape[1], down, down_arrived
    )

    @at_first_step
    def _():
        start_all(copies)
        sums_ref[...] = jnp.zeros_like(sums_ref)
        hidden_sums_ref[...] = jnp.zeros_like(hidden_sums_ref)
        wait_all(copies)

    grad = flat(grad_ref[...])
    back = half_back(
        grad, slope_ref, up, down, hidden_ref, hidden_sums_ref, flat(before_ref[...])
    )
    unit = flat(unit_ref[...])
    grad_first = norm_back(
        back, unit, flat(inverse_ref[...]), vectors_ref[GAIN_ONE : GAIN_ONE + 1]
    )
    grad_attn = (grad_first * kept(keep_ref)).astype(BF)
    attn_ref[...] = grad_attn.reshape(attn_ref.shape)
    first_ref[...] = grad_first[:ROWS] + grad_first[ROWS:]
    for row, values in enumerate(
        (back * unit, back, grad_attn.astype(F32), grad.astype(F32))
    ):
        sums_ref[row : row + 1] += jnp.sum(values, axis=0, keepdims=True)


def other_back(vectors, grad, slope, before, unit, inverse, keep, pieces, first):
    _, length, width = keep.shape
    hidden = slope.shape[2]
    return pl.pallas_call(
        functools.partial(other_back_kernel, first),
        grid=(length // ROWS,),
        in_specs=[
            constant_block(vectors.shape),
            rows_block(width),
            rows_block(hidden),
            rows_block(width),
            rows_block(width),
            rows_block(1),
            rows_block(width),
        ]
        + [far_spec()] * len(pieces),
        out_specs=[
            rows_block(hidden),
            rows_block(width),
            pl.BlockSpec((ROWS, width), lambda i: (i, 0)),
            pl.BlockSpec((4, width), lambda i: (0, 0)),
            pl.BlockSpec((1, hidden), lambda i: (0, 0)),
        ],
        out_shape=[
            jax.ShapeDtypeStruct((2, length, hidden), BF),
            jax.ShapeDtypeStruct((2, length, width), BF),
            jax.ShapeDtypeStruct((length, width), F32),
            jax.ShapeDtypeStruct((4, width), F32),
            jax.ShapeDtypeStruct((1, hidden), F32),
        ],
        scratch_shapes=weights_scratch(width, hidden, pieces),
        compiler_params=pltpu.CompilerParams(vmem_limit_bytes=VMEM_LIMIT),
        name="other_back",
        cost_estimate=work(7e9),
    )(vectors, grad, slope, before, unit, inverse, keep, *pieces)


def matrix_grad_kernel(left_ref, right_ref, kept_ref, sent_ref, turned):
    @at_first_step
    def _():
        turned[...] = left_ref[...].T

    half = kept_ref.shape[0]
    right = right_ref[...]
    kept_ref[...] = dot(turned[:half], right, 1, 0)
    sent_ref[...] = dot(turned[half:], right, 1, 0)


def matrix_grad(left, right):
    rows, width = left.shape
    columns = right.shape[1]
    step = 384
    half = pl.BlockSpec((width // 2, step), lambda i: (0, i))
    return tuple(
        pl.pallas_call(
            matrix_grad_kernel,
            grid=(columns // step,),
            in_specs=[constant_block(left.shape), pl.BlockSpec((rows, step), lambda i: (0, i))],
            out_specs=[half, half],
            out_shape=[jax.ShapeDtypeStruct((width // 2, columns), F32)] * 2,
            scratch_shapes=[pltpu.VMEM((width, rows), BF)],
            compiler_params=pltpu.CompilerParams(vmem_limit_bytes=VMEM_LIMIT),
            name="matrix_grad",
            cost_estimate=work(1.5e6 * columns),
        )(left, right)
    )


def loss_kernel(rows_ref, place_ref, loss_ref, grad_ref, *, scale):
    first, second = rows_ref[0], rows_ref[1]
    count = first.shape[0]
    inverse = [
        lax.rsqrt(jnp.sum(rows * rows, axis=-1, keepdims=True) + 1e-06) for rows in (first, second)
    ]
    units = [first * inverse[0], second * inverse[1]]
    logits = dot(units[0], units[1], 1, 1, EXACT) * 20.0
    peak = jnp.max(logits, axis=1, keepdims=True)
    powers = jnp.exp(logits - peak)
    total = jnp.sum(powers, axis=1, keepdims=True)
    row = lax.broadcasted_iota(jnp.int32, logits.shape, 0)
    column = lax.broadcasted_iota(jnp.int32, logits.shape, 1)
    on_diagonal = row == column
    losses = (
        peak
        + jnp.log(total)
        - jnp.sum(jnp.where(on_diagonal, logits, 0.0), axis=1, keepdims=True)
    )
    loss_ref[...] = jnp.sum(losses, axis=0, keepdims=True) * (1.0 / count)
    grad_logits = (powers / total - jnp.where(on_diagonal, 1.0, 0.0)) * (20.0 * scale / count)
    grad_units = [
        dot(grad_logits, units[1], 1, 0, EXACT),
        dot(grad_logits, units[0], 0, 0, EXACT),
    ]
    mine = lax.broadcasted_iota(jnp.int32, first.shape, 0) == place_ref[0]
    for view in range(2):
        along = jnp.sum(units[view] * grad_units[view], axis=-1, keepdims=True)
        grad_rows = (grad_units[view] - units[view] * along) * inverse[view]
        grad_ref[view : view + 1] = jnp.sum(
            jnp.where(mine, grad_rows, 0.0), axis=0, keepdims=True
        )


def loss_and_grad(rows, place, scale):
    width = rows.shape[-1]
    return pl.pallas_call(
        functools.partial(loss_kernel, scale=scale),
        in_specs=[
            pl.BlockSpec(memory_space=pltpu.VMEM),
            pl.BlockSpec(memory_space=pltpu.SMEM),
        ],
        out_shape=[
            jax.ShapeDtypeStruct((1, 1), F32),
            jax.ShapeDtypeStruct((2, width), F32),
        ],
        compiler_params=pltpu.CompilerParams(vmem_limit_bytes=VMEM_LIMIT),
        name="contrast",
    )(rows, place)


def adam_direction(weight, gradient, first_moment, second, decay_rate):
    new_first = 0.9 * first_moment + 0.1 * gradient
    new_second = 0.999 * second + 0.001 * gradient * gradient
    first_hat = new_first / (1.0 - 0.9**STEP)
    second_hat = new_second / (1.0 - 0.999**STEP)
    update = first_hat / (jnp.sqrt(second_hat) + 1e-06) + decay_rate * weight
    return (new_first, new_second, update)


LANES = 128
SQUARES = {"attn": 0, "out": 3, "up": 4, "down": 5}
MATRICES = 6


def in_lane(lane, value):
    lanes = lax.broadcasted_iota(jnp.int32, (1, LANES), 1)
    return jnp.where(lanes == lane, value, 0.0)


def pieces_of(matrix_ref):
    if len(matrix_ref.shape) == 3:
        return [(part,) for part in range(matrix_ref.shape[0])]
    return [(slice(None),)]


def adam_kernel(names, offsets, scale, *refs):
    count = len(names)
    ins, before_ref = refs[: 4 * count], refs[4 * count]
    outs, sums_ref = refs[4 * count + 1 : -1], refs[-1]
    sums = before_ref[...]
    for place, name in enumerate(names):
        weight_ref, grad_ref, first_ref, second_ref = ins[4 * place : 4 * place + 4]
        out_refs = outs[3 * place : 3 * place + 3]
        for part, where in enumerate(pieces_of(weight_ref)):
            weight = weight_ref[where]
            columns = weight.shape[-1]
            start = offsets[place] + part * columns
            grad = grad_ref[:, start : start + columns] * scale
            results = adam_direction(weight, grad, first_ref[where], second_ref[where], 0.01)
            for out_ref, result in zip(out_refs, results):
                out_ref[where] = result
            lane = SQUARES[name] + part
            sums = sums + in_lane(lane, jnp.sum(weight * weight))
            sums = sums + in_lane(lane + MATRICES, jnp.sum(results[2] * results[2]))
    sums_ref[...] = sums


def adam(names, offsets, matrices, before, scale):
    args = [array for matrix in matrices for array in matrix]
    shapes = [
        jax.ShapeDtypeStruct(matrix[0].shape, F32) for matrix in matrices for _ in range(3)
    ] + [jax.ShapeDtypeStruct(before.shape, F32)]
    out = pl.pallas_call(
        functools.partial(adam_kernel, names, offsets, scale),
        out_shape=shapes,
        compiler_params=pltpu.CompilerParams(vmem_limit_bytes=VMEM_LIMIT),
        name="adam",
    )(*args, before)
    return [out[3 * i : 3 * i + 3] for i in range(len(names))], out[-1]


def apply_kernel(names, scale, *refs):
    count = len(names)
    gathered_ref, pairs, rest = refs[0], refs[1 : 1 + 2 * count], refs[1 + 2 * count :]
    small_ins, outs = rest[:9], rest[9:]
    sums = jnp.sum(gathered_ref[:, 0], axis=0, keepdims=True)
    roots = jnp.sqrt(sums)
    for place, name in enumerate(names):
        weight_ref, update_ref = pairs[2 * place : 2 * place + 2]
        for part, where in enumerate(pieces_of(weight_ref)):
            lane = SQUARES[name] + part
            ratio = roots[:, lane : lane + 1] / roots[:, lane + MATRICES : lane + MATRICES + 1]
            outs[place][where] = weight_ref[where] - 0.25 * ratio * update_ref[where]
    slices = gathered_ref.shape[1] - 1
    line = 0
    for place in range(3):
        weight_ref, first_ref, second_ref = small_ins[3 * place : 3 * place + 3]
        rows, columns = weight_ref.shape
        lines = []
        for _ in range(rows):
            parts = []
            for _ in range(columns // LANES):
                device, slot = divmod(line, slices)
                parts.append(gathered_ref[device, 1 + slot : 2 + slot])
                line += 1
            lines.append(jnp.concatenate(parts, axis=1))
        grad = jnp.concatenate(lines, axis=0) * scale
        results = small_step(weight_ref[...], grad, first_ref[...], second_ref[...])
        for out_ref, result in zip(outs[count + 3 * place : count + 3 * place + 3], results):
            out_ref[...] = result


def apply_updates(names, gathered, pairs, small, scale):
    shapes = [jax.ShapeDtypeStruct(weight.shape, F32) for weight, _ in pairs] + [
        jax.ShapeDtypeStruct(array.shape, F32) for array in small
    ]
    return pl.pallas_call(
        functools.partial(apply_kernel, names, scale),
        out_shape=shapes,
        compiler_params=pltpu.CompilerParams(vmem_limit_bytes=VMEM_LIMIT),
        name="apply_updates",
    )(gathered, *(array for pair in pairs for array in pair), *small)


def small_step(weight, gradient, first_moment, second):
    new_first, new_second, update = adam_direction(weight, gradient, first_moment, second, 0.0)
    trust_ratio = jnp.sqrt(jnp.sum(weight * weight, axis=-1, keepdims=True)) / jnp.sqrt(
        jnp.sum(update * update, axis=-1, keepdims=True)
    )
    return (weight - 0.25 * trust_ratio * update, new_first, new_second)


def shards(
    tokens,
    prob_masks,
    branch_masks,
    attn_weight,
    attn_first,
    attn_second,
    out_weight,
    out_first,
    out_second,
    up_weight,
    up_first,
    up_second,
    down_weight,
    down_first,
    down_second,
    gains,
    gains_first,
    gains_second,
    shifts,
    shifts_first,
    shifts_second,
    hidden_bias,
    hidden_first,
    hidden_second,
):
    tensor_count = lax.axis_size("tensor")
    tensor_rank = lax.axis_index("tensor")
    data_count = lax.axis_size("dp")
    data_rank = lax.axis_index("dp")
    seq_local, half_len, width = tokens.shape
    assert tensor_count == 2 and seq_local == 2
    seq_len = half_len * tensor_count
    heads_local = prob_masks.shape[2]
    local_width = heads_local * HD
    hidden_local = up_weight.shape[1]
    rows_local = width // data_count
    scale_loss = 64.0 * data_count * seq_local * seq_len
    chunk = min(256, seq_len)
    is_first = tensor_rank == 0

    def in_order(mine, others, axis):
        return jnp.where(
            is_first,
            jnp.concatenate([mine, others], axis=axis),
            jnp.concatenate([others, mine], axis=axis),
        )

    def of_rank(whole, axis, length):
        mine = lax.dynamic_slice_in_dim(whole, tensor_rank * length, length, axis)
        others = lax.dynamic_slice_in_dim(whole, (1 - tensor_rank) * length, length, axis)
        return mine, others

    own_tokens, send_tokens = of_rank(tokens, 0, 1)
    words = jnp.pad(
        jnp.swapaxes(prob_masks.astype(jnp.int16), 3, 4),
        ((0, 0), (0, 0), (0, 0), (0, -prob_masks.shape[4] % 16), (0, 0)),
    )
    own_words, send_words = of_rank(words, 1, 1)
    branch_words = jnp.pad(
        jnp.swapaxes(branch_masks.astype(jnp.int16), 3, 4),
        ((0, 0), (0, 0), (0, 0), (0, -branch_masks.shape[4] % 16), (0, 0)),
    )
    own_branch, send_branch = of_rank(branch_words, 2, 1)

    order = jnp.asarray(np.array(gathered_order(data_count), np.int32))
    owner = jnp.bitwise_xor(order, data_rank)
    feature = (owner[:, None] * rows_local + jnp.arange(rows_local, dtype=jnp.int32)).reshape(-1)
    places = lax.broadcasted_iota(jnp.int32, (width, width), 0)
    to_own = (places == feature[None, :]).astype(F32)
    to_own_low = to_own.astype(BF)

    attn_block = attn_weight.astype(BF).reshape(rows_local, 3 * local_width)
    out_block = out_weight.astype(BF).T
    up_block = up_weight.astype(BF)
    down_block = down_weight.astype(BF).T
    branch_rows_padded = branch_words.shape[3]
    word = feature // BRANCH_BITS
    bit = feature % BRANCH_BITS
    high = bit >= LOW_BITS
    row = jnp.where(high, word + branch_rows_padded, word)
    power = jnp.exp2(-jnp.where(high, bit - LOW_BITS, bit).astype(F32))
    branch_select = jnp.where(
        lax.broadcasted_iota(jnp.int32, (2 * branch_rows_padded, width), 0) == row[None, :],
        power[None, :],
        0.0,
    ).astype(BF)

    bias_q = of_rank(shifts[0], 0, local_width)
    bias_v = of_rank(shifts[1], 0, local_width)

    def project(half, rows, matrix):
        bias = jnp.concatenate([bias_q[half], jnp.zeros_like(bias_q[half]), bias_v[half]])
        return (dot(rows, matrix, 1, 0) + bias).astype(BF)

    first_bit, *later_bits = [bit for group in upper_groups() for bit in group]
    token_other = swap_tensor(send_tokens)
    attn_quarter = gather_upper(attn_block)
    wide_quarter = jnp.concatenate([out_block, up_block, down_block], axis=1)
    wide_sent = swap_dp(wide_quarter, 1 << first_bit)
    own_keep = prob_keep(own_words[:, 0], seq_len)
    attn_quarter, own_keep, wide_sent = together(attn_quarter, own_keep, wide_sent)

    attn_beside, attn_across = swap_dp(attn_quarter, 2), swap_tensor(attn_quarter)
    wide_quarter = joined([wide_quarter, wide_sent])
    for bit in later_bits[:-1]:
        wide_quarter = gather_bit(wide_quarter, bit)
    wide_sent = swap_dp(wide_quarter, 1 << later_bits[-1])
    token_rows = in_order(own_tokens[0], token_other[0], 0)
    token_own = dot(token_rows, to_own_low, 1, 0).astype(BF)
    attn_corner = swap_dp(attn_across, 2)
    other_words = swap_tensor(tie(send_words, attn_across))
    attn_near = gather_core((attn_quarter, attn_beside))
    qkv_own = project(0, token_own, attn_near)
    attended = attend(qkv_own, own_keep, chunk)
    other_keep = prob_keep(other_words[:, 0], seq_len)
    attn_corner, attended, other_keep, wide_sent, wide_quarter = together(
        attn_corner, attended, other_keep, wide_sent, wide_quarter
    )

    wide_quarter = joined([wide_quarter, wide_sent])
    wide_beside = swap_dp(wide_quarter, 2)
    wide_across = swap_tensor(wide_quarter)
    attn_far = gather_core((attn_across, attn_corner))
    qkv_other = project(1, token_own, attn_far)
    attended_other = attend(qkv_other, other_keep, chunk)
    qkv_other, attended_other, wide_beside, wide_across = together(
        qkv_other, attended_other, wide_beside, wide_across
    )

    eighth = width // 8
    wide_corner = (swap_tensor(wide_beside[:eighth]), swap_dp(wide_across[eighth:], 2))
    branch_other = swap_tensor(tie(send_branch, wide_across))
    branch_rows = in_order(own_branch[:, :, 0], branch_other[:, :, 0], 3)
    keeps = branch_keep(branch_rows, branch_select)
    wide_corner, keeps = together(wide_corner, keeps)
    attn_low = [attn_near, attn_far]
    wide_pieces = [
        quarters + tuple(swap_dp(quarter, 1) for quarter in quarters)
        for quarters in ((wide_quarter, wide_beside), (wide_across, *wide_corner))
    ]
    qkv = [qkv_own, qkv_other]
    contexts = [attended[0], attended_other[0]]
    logsums = [attended[1], attended_other[1]]
    keep_halves = (own_keep, other_keep)
    vectors = dot(jnp.concatenate([gains, shifts[2:6]], axis=0), to_own, 1, 0, EXACT)
    context_flat = [c.reshape(2 * seq_len, local_width) for c in contexts]
    unit_one, inverse_one, *out_low = first_norm(
        vectors, contexts, wide_pieces, token_own, keeps[0]
    )
    hidden_halves = jnp.stack(of_rank(hidden_bias, 0, hidden_local))
    normed_low, active_own, active_other, slope_own, slope_other, unit_two, inverse_two, unit_sum = hidden_units(
        vectors,
        hidden_halves,
        unit_one,
        keeps[1],
        wide_pieces,
        local_width,
    )
    normed_low = normed_low.reshape(2 * seq_len, width)
    active = [a.reshape(2 * seq_len, hidden_local) for a in (active_own, active_other)]
    gain_two = vectors[GAIN_TWO]
    shift_two = vectors[SHIFT_TWO]
    pooled = unit_sum * gain_two / seq_len + shift_two
    pooled_rows = dot(pooled, to_own, 1, 1, EXACT)
    everyone = jnp.swapaxes(everyones(pooled_rows), 0, 1)
    place = (data_rank * tensor_count + tensor_rank).astype(jnp.int32).reshape(1)
    loss_value, grad_pooled = loss_and_grad(everyone, place, scale_loss)
    grad_rows = dot(grad_pooled, to_own, 1, 0, EXACT) / seq_len

    grad_shift_two = jnp.sum(grad_rows, axis=0) * seq_len
    grad_gain_two = jnp.sum(grad_rows * unit_sum, axis=0)
    grad_second, grad_ffn = second_back(vectors, grad_rows, unit_two, inverse_two, keeps[1])
    grad_ffn_flat = grad_ffn.reshape(2 * seq_len, width)
    quarter_width = width // 4

    weight_grads = matrix_grad

    def both_cores(grads):
        kept, sent = grads
        return kept, swap_dp(sent, 1)

    def rows_of(parts, first):
        return tuple(
            part[:quarter_width] if first else part[quarter_width:] for part in parts
        )

    def low_sum(parts):
        return added(*parts).astype(BF)

    def context_back(half, grad_rows):
        return dot(grad_rows, out_low[half], 1, 0).astype(BF)

    def queries_back(half, grad_context):
        return attend_back(
            qkv[half],
            keep_halves[half],
            logsums[half],
            contexts[half],
            grad_context.reshape(2, seq_len, local_width),
            chunk,
        )

    eighth = quarter_width // 2

    def corner_out(other):
        return (
            swap_tensor(added(*(p[quarter_width : quarter_width + eighth] for p in other)).astype(BF)),
            swap_dp(added(*(p[quarter_width + eighth :] for p in other)).astype(BF), 2),
        )

    def sides_sent(own, other, corner):
        from_tensor, from_beside = corner
        to_tensor = jnp.concatenate(
            [
                low_sum(tuple(p[:eighth] for p in other)),
                low_sum(tuple(p[eighth:quarter_width] for p in other) + (from_beside,)),
            ]
        )
        to_beside = jnp.concatenate(
            [
                low_sum(
                    tuple(p[quarter_width : quarter_width + eighth] for p in own) + (from_tensor,)
                ),
                low_sum(tuple(p[quarter_width + eighth :] for p in own)),
            ]
        )
        return to_tensor, to_beside

    def sides_out(sent):
        return swap_tensor(sent[0]), swap_dp(sent[1], 2)

    def side_by_side(first, second):
        return tuple(jnp.concatenate(pair, axis=1) for pair in zip(first, second))

    rows_shape = (2, seq_len, width)
    down_other = weight_grads(grad_ffn_flat, active[1])
    down_own = weight_grads(grad_ffn_flat, active[0])
    down_other, down_own, grad_ffn_flat = together(down_other, down_own, grad_ffn_flat)

    down_other, down_own = both_cores(down_other), both_cores(down_own)
    grad_hidden_own, back, hidden_sums_own = own_back(
        grad_ffn_flat.reshape(rows_shape),
        slope_own,
        grad_second,
        wide_pieces[0],
        local_width,
    )
    down_other, down_own, back = together(down_other, down_own, back)

    down_corner = corner_out(down_other)
    grad_hidden_other, grad_attn, grad_first, column_sums, hidden_sums_other = other_back(
        vectors,
        grad_ffn_flat.reshape(rows_shape),
        slope_other,
        back,
        unit_one,
        inverse_one,
        keeps[0],
        wide_pieces[1],
        local_width,
    )
    down_corner, grad_hidden_other, grad_attn = together(down_corner, grad_hidden_other, grad_attn)
    grad_attn_flat = grad_attn.reshape(2 * seq_len, width)

    down_sent = sides_sent(down_own, down_other, down_corner)
    up_other = weight_grads(
        tie(normed_low, *down_sent), grad_hidden_other.reshape(2 * seq_len, hidden_local)
    )
    up_own = weight_grads(normed_low, grad_hidden_own.reshape(2 * seq_len, hidden_local))
    up_other, up_own = both_cores(up_other), both_cores(up_own)
    out_other = both_cores(weight_grads(grad_attn_flat, context_flat[1]))
    out_own = both_cores(weight_grads(grad_attn_flat, context_flat[0]))
    down_sides = sides_out(down_sent)
    context_other = context_back(1, grad_attn_flat)
    down_sides, up_other, up_own, out_other, out_own, context_other = together(
        down_sides, up_other, up_own, out_other, out_own, context_other
    )

    wide_other, wide_own = side_by_side(out_other, up_other), side_by_side(out_own, up_own)
    wide_corner = corner_out(wide_other)
    down_parts = rows_of(down_own, True) + down_sides
    grad_other = queries_back(1, context_other)
    wide_corner, grad_other = together(wide_corner, grad_other)

    wide_leaving = sides_sent(wide_own, wide_other, wide_corner)
    wide_sides = sides_out(wide_leaving)
    down_reduced = upper_parts(down_parts)
    attn_other = both_cores(weight_grads(token_own, tie(grad_other, *wide_leaving)))
    context_own = context_back(0, grad_attn_flat)
    token_back = dot(grad_other, attn_low[1], 1, 1) + grad_first
    attn_other, context_own, token_back, wide_sides, down_reduced = together(
        attn_other, context_own, token_back, wide_sides, down_reduced
    )

    attn_sent = low_sum(attn_other)
    attn_across = swap_tensor(attn_sent)
    wide_reduced = upper_parts(rows_of(wide_own, True) + wide_sides)
    grad_own = queries_back(0, tie(context_own, attn_sent))
    attn_own = weight_grads(token_own, grad_own)
    attn_across, wide_reduced, attn_own, grad_own = together(
        attn_across, wide_reduced, attn_own, grad_own
    )

    attn_own = both_cores(attn_own)
    token_back = token_back + dot(grad_own, attn_low[0], 1, 1)
    attn_own, token_back = together(attn_own, token_back)
    attn_own = attn_own + (attn_across,)
    attn_sent = low_sum(rows_of(attn_own, False))
    attn_beside = swap_dp(attn_sent, 2)
    token_back = tie(token_back, attn_sent)
    token_high = token_back.astype(BF)
    token_low = (token_back - token_high.astype(F32)).astype(BF)
    token_grad = dot(
        jnp.concatenate([token_high, token_low], axis=0), to_own_low, 1, 1
    )
    token_grad = token_grad[:seq_len] + token_grad[seq_len:]
    grad_own = tie(grad_own, attn_sent)
    hidden_sums = (hidden_sums_own[0], hidden_sums_other[0])
    grad_qkv = [grad_own, grad_other]
    bias_sums = [jnp.sum(grad_qkv[half].astype(F32), axis=0) for half in range(2)]
    query_row = in_order(bias_sums[0][:local_width], bias_sums[1][:local_width], 0)
    value_row = in_order(bias_sums[0][2 * local_width :], bias_sums[1][2 * local_width :], 0)
    hidden_row = in_order(hidden_sums[0], hidden_sums[1], 0)
    feature_rows = dot(
        jnp.stack(
            [
                column_sums[0],
                grad_gain_two,
                column_sums[2],
                column_sums[1],
                column_sums[3],
                grad_shift_two,
            ]
        ),
        to_own,
        1,
        1,
        EXACT,
    )
    small = jnp.concatenate(
        [
            feature_rows[:2],
            query_row[None],
            value_row[None],
            feature_rows[2:],
            hidden_row.reshape(-1, width),
        ],
        axis=0,
    )
    small_sums = slices_summed(small.reshape(-1)).reshape(-1, LANES)
    attn_beside, token_grad, small_sums = together(attn_beside, token_grad, small_sums)
    attn_reduced = added(*upper_parts(rows_of(attn_own, True) + (attn_beside,)))
    down_reduced, wide_reduced = added(*down_reduced), added(*wide_reduced)
    own_half, send_half = of_rank(token_grad, 0, half_len)
    grad_tokens = in_order(own_half[None], swap_tensor(send_half.astype(BF))[None].astype(F32), 0)

    inverse_scale = 1.0 / scale_loss

    def turned(*arrays):
        return [array.T for array in arrays]

    def parts_first(*arrays):
        return [jnp.transpose(array, (1, 0, 2)) for array in arrays]

    down_own_weight, down_firsts, down_seconds = turned(down_weight, down_first, down_second)
    out_own_weight, out_firsts, out_seconds = turned(out_weight, out_first, out_second)
    attn_parts, attn_firsts, attn_seconds = parts_first(attn_weight, attn_first, attn_second)
    (down_new,), sums = adam(
        ("down",),
        (0,),
        ((down_own_weight, down_reduced, down_firsts, down_seconds),),
        jnp.zeros((1, LANES), F32),
        inverse_scale,
    )
    (up_new, out_new, attn_new), sums = adam(
        ("up", "out", "attn"),
        (local_width, 0, 0),
        (
            (up_weight, wide_reduced, up_first, up_second),
            (out_own_weight, wide_reduced, out_firsts, out_seconds),
            (attn_parts, attn_reduced, attn_firsts, attn_seconds),
        ),
        sums,
        inverse_scale,
    )
    hidden_args = [array.reshape(1, -1) for array in (hidden_bias, hidden_first, hidden_second)]
    gathered = everyones(jnp.concatenate([sums, small_sums], axis=0))
    gathered, grad_tokens = together(gathered, grad_tokens)
    (
        new_attn,
        new_out,
        new_up,
        new_down,
        new_gains,
        new_gains_first,
        new_gains_second,
        new_shifts,
        new_shifts_first,
        new_shifts_second,
        new_hidden,
        new_hidden_first,
        new_hidden_second,
    ) = apply_updates(
        ("attn", "out", "up", "down"),
        gathered,
        (
            (attn_parts, attn_new[2]),
            (out_own_weight, out_new[2]),
            (up_weight, up_new[2]),
            (down_own_weight, down_new[2]),
        ),
        (gains, gains_first, gains_second, shifts, shifts_first, shifts_second, *hidden_args),
        inverse_scale,
    )
    new_hidden, new_hidden_first, new_hidden_second = (
        array.reshape(-1) for array in (new_hidden, new_hidden_first, new_hidden_second)
    )
    new_attn, attn_new_first, attn_new_second = parts_first(new_attn, attn_new[0], attn_new[1])
    new_out, out_new_first, out_new_second = turned(new_out, out_new[0], out_new[1])
    new_down, down_new_first, down_new_second = turned(new_down, down_new[0], down_new[1])
    up_new_first, up_new_second = up_new[:2]
    return (
        loss_value.reshape(()),
        grad_tokens,
        new_attn,
        attn_new_first,
        attn_new_second,
        new_out,
        out_new_first,
        out_new_second,
        new_up,
        up_new_first,
        up_new_second,
        new_down,
        down_new_first,
        down_new_second,
        new_gains,
        new_gains_first,
        new_gains_second,
        new_shifts,
        new_shifts_first,
        new_shifts_second,
        new_hidden,
        new_hidden_first,
        new_hidden_second,
    )


def solution(mesh):
    row_split = P("dp", None, "tensor")
    column_split = P("tensor", "dp")
    matrix_split = P("dp", "tensor")
    return jax.shard_map(
        shards,
        mesh=mesh,
        in_specs=(
            P("dp", "tensor", None),
            P(None, "dp", "tensor", None, None),
            P(None, None, "dp", "tensor", None),
        )
        + (row_split,) * 3
        + (column_split,) * 3
        + (matrix_split,) * 3
        + (column_split,) * 3
        + (P(),) * 9,
        out_specs=(P(), P("dp", "tensor", None))
        + (row_split,) * 3
        + (column_split,) * 3
        + (matrix_split,) * 3
        + (column_split,) * 3
        + (P(),) * 9,
        check_vma=False,
    )
```

```python
import functools

import jax
import jax.numpy as jnp
import numpy as np
from jax import lax
from jax.experimental import pallas as pl
from jax.experimental.pallas import tpu as pltpu
from jax.sharding import PartitionSpec as P

HD = 64
STEP = 10
KEEP_SCALE = 1.0 / 0.9
PROB_BITS = 13
BRANCH_BITS = 15
LOW_BITS = 7
BF = jnp.bfloat16
F32 = jnp.float32
EXACT = lax.Precision.HIGHEST
VMEM_LIMIT = 56 << 20


def work(flops):
    return pl.CostEstimate(flops=int(flops), bytes_accessed=0, transcendentals=0)


def dot(left, right, left_dim, right_dim, precision=None):
    return lax.dot_general(
        left,
        right,
        (((left_dim,), (right_dim,)), ((), ())),
        preferred_element_type=F32,
        precision=precision,
    )


def swap_dp(value, distance):
    count = lax.axis_size("dp")
    return lax.ppermute(value, "dp", [(i, i ^ distance) for i in range(count)])


def swap_tensor(value):
    return lax.ppermute(value, "tensor", [(0, 1), (1, 0)])


def bit_groups(count):
    bits = count.bit_length() - 1
    groups, top = [], bits
    while top - 2 >= 2:
        groups.append((top - 2, top - 1))
        top -= 2
    while top > 0:
        groups.append((top - 1,))
        top -= 1
    return groups


def distances(group):
    out = [0]
    for bit in group:
        out = out + [o | (1 << bit) for o in out]
    return out


def gathered_order(count):
    order = [0]
    for group in bit_groups(count):
        order = [o | step for step in distances(group) for o in order]
    return order


def joined_kernel(spans, *refs):
    count = len(refs) - 1 - len(spans)
    pieces, out_refs, arrived = refs[:count], refs[count:-1], refs[-1]
    copies, start = [], 0
    for index, piece in enumerate(pieces):
        rows = piece.shape[0]
        for place, (first, last) in enumerate(spans):
            copies.append(
                pltpu.make_async_copy(
                    piece.at[:, pl.ds(first, last - first)],
                    out_refs[place].at[pl.ds(start, rows)],
                    arrived.at[index, place],
                )
            )
        start += rows
    for copy in copies:
        copy.start()
    for copy in copies:
        copy.wait()


def joined(pieces, spans=None):
    rows = sum(piece.shape[0] for piece in pieces)
    columns = pieces[0].shape[1]
    parts = spans or ((0, columns),)
    if any(piece.shape[0] % 16 for piece in pieces):
        whole = jnp.concatenate(pieces, axis=0)
        return [whole[:, first:last] for first, last in parts] if spans else whole
    out = pl.pallas_call(
        functools.partial(joined_kernel, parts),
        in_specs=[pl.BlockSpec(memory_space=pl.ANY)] * len(pieces),
        out_specs=[pl.BlockSpec(memory_space=pltpu.VMEM)] * len(parts),
        out_shape=[
            jax.ShapeDtypeStruct((rows, last - first), pieces[0].dtype) for first, last in parts
        ],
        scratch_shapes=[pltpu.SemaphoreType.DMA((len(pieces), len(parts)))],
        compiler_params=pltpu.CompilerParams(vmem_limit_bytes=VMEM_LIMIT),
        name="joined",
    )(*pieces)
    return out if spans else out[0]


def whole_tiles(blocks, places):
    _, rows, columns = blocks.shape
    count = places.shape[1]
    if rows % 16 == 0:
        return blocks, places
    quarters = blocks[places.reshape(-1)].reshape(8, count * rows // 4, columns)
    return quarters, jnp.arange(8, dtype=jnp.int32).reshape(2, 4)


def tie(value, *others):
    return lax.optimization_barrier((value,) + others)[0]


def together(*values):
    return lax.optimization_barrier(values)


def upper_groups():
    return bit_groups(lax.axis_size("dp"))[:-2]


def gather_upper(block):
    for group in upper_groups():
        block = joined([block] + [swap_dp(block, s) for s in distances(group)[1:]])
    return block


def gather_bit(block, bit):
    return joined([block, swap_dp(block, 1 << bit)])


def gather_sides(mine, corner_by_tensor):
    beside = swap_dp(mine, 2)
    across = swap_tensor(mine)
    corner = swap_tensor(beside) if corner_by_tensor else swap_dp(across, 2)
    return (mine, beside), (across, corner)


def gather_core(quarters, spans=None):
    near, far = quarters
    return joined([near, far, swap_dp(near, 1), swap_dp(far, 1)], spans)


def upper_parts(parts):
    for group in reversed(upper_groups()):
        steps = distances(group)
        rows = parts[0].shape[0] // len(steps)
        kept_rows = [part[:rows].astype(F32) for part in parts]
        for index, step in enumerate(steps[1:], 1):
            sent = sum(part[index * rows : (index + 1) * rows].astype(F32) for part in parts)
            kept_rows.append(swap_dp(sent.astype(BF), step))
        parts = kept_rows
    return tuple(parts)


def added(*parts):
    return sum(part.astype(F32) for part in parts)


def slices_summed(values):
    count = lax.axis_size("dp") * lax.axis_size("tensor")
    values = jnp.pad(values, (0, -values.size % (128 * count)))
    spread = values.reshape(count, -1, 128)
    return jnp.sum(lax.all_to_all(spread, ("dp", "tensor"), 0, 0, tiled=True), axis=0).reshape(-1)


def everyones(value):
    count = lax.axis_size("dp") * lax.axis_size("tensor")
    spread = jnp.broadcast_to(value[None], (count,) + value.shape)
    return lax.all_to_all(spread, ("dp", "tensor"), 0, 0, tiled=True)


def selector(places, words, word_bits):
    out = np.zeros((places, 2 * words), np.float32)
    for place in range(places):
        word, bit = divmod(place, word_bits)
        if bit < LOW_BITS:
            out[place, word] = 2.0**-bit
        else:
            out[place, words + word] = 2.0 ** (LOW_BITS - bit)
    return out


def split_words(words):
    words = words.astype(jnp.int32)
    low = jnp.bitwise_and(words, (1 << LOW_BITS) - 1)
    high = jnp.right_shift(words, LOW_BITS)
    return jnp.concatenate([low.astype(F32), high.astype(F32)], axis=0).astype(BF)


def units_bit(values):
    return jnp.bitwise_and(values.astype(jnp.int32), 1).astype(F32).astype(BF)


def prob_keep_kernel(select_ref, words_ref, keep_ref):
    for view in range(2):
        keep_ref[view, 0] = units_bit(
            dot(select_ref[...], split_words(words_ref[view, 0]), 1, 0)
        )


def prob_keep(words, length):
    _, heads, rows, _ = words.shape
    select = jnp.asarray(selector(length, rows, PROB_BITS), BF)
    return pl.pallas_call(
        prob_keep_kernel,
        grid=(heads,),
        in_specs=[
            pl.BlockSpec(select.shape, lambda h: (0, 0)),
            pl.BlockSpec((2, 1, rows, length), lambda h: (0, h, 0, 0)),
        ],
        out_specs=pl.BlockSpec((2, 1, length, length), lambda h: (0, h, 0, 0)),
        out_shape=jax.ShapeDtypeStruct((2, heads, length, length), BF),
        compiler_params=pltpu.CompilerParams(vmem_limit_bytes=VMEM_LIMIT),
        name="prob_keep",
        cost_estimate=work(3.5e9),
    )(select, words)


def branch_keep_kernel(select_ref, words_ref, keep_ref):
    keep_ref[0, 0] = units_bit(dot(split_words(words_ref[0, 0]), select_ref[...], 0, 0))


def branch_keep(words, select):
    _, _, rows, length = words.shape
    width = select.shape[1]
    return pl.pallas_call(
        branch_keep_kernel,
        grid=(2, 2),
        in_specs=[
            pl.BlockSpec(select.shape, lambda b, v: (0, 0)),
            pl.BlockSpec((1, 1, rows, length), lambda b, v: (b, v, 0, 0)),
        ],
        out_specs=pl.BlockSpec((1, 1, length, width), lambda b, v: (b, v, 0, 0)),
        out_shape=jax.ShapeDtypeStruct((2, 2, length, width), BF),
        compiler_params=pltpu.CompilerParams(vmem_limit_bytes=VMEM_LIMIT),
        name="branch_keep",
        cost_estimate=work(2.5e9),
    )(select, words)


def head_lanes(shape, head):
    lane = lax.broadcasted_iota(jnp.int32, shape, 1)
    return jnp.logical_and(lane >= head * HD, lane < (head + 1) * HD)


def attend_kernel(chunk, q_ref, k_ref, v_ref, keep_ref, context_ref, logsum_ref, turned):
    length = q_ref.shape[0]
    queries = q_ref[...] * BF(0.125)
    key_rows = k_ref[...]
    values_turned = v_ref[...].T
    for head in range(2):
        own = jnp.where(head_lanes(queries.shape, head), queries, BF(0))
        span = slice(head * HD, (head + 1) * HD)
        for start in range(0, length, chunk):
            part = slice(start, start + chunk)
            scores = dot(key_rows, own[part], 1, 1)
            peak = jnp.max(scores, axis=0, keepdims=True)
            powers = jnp.exp(scores - peak)
            total = jnp.sum(powers, axis=0, keepdims=True)
            weighted = (powers * (KEEP_SCALE / total)).astype(BF)
            logsum_ref[head, :, part] = peak + jnp.log(total * (1.0 / KEEP_SCALE))
            for view in range(2):
                kept = weighted * keep_ref[view, head, :, part]
                turned[view, span, part] = dot(values_turned[span], kept, 1, 0).astype(BF)
    for view in range(2):
        context_ref[view] = turned[view].T


def attend(qkv, keep, chunk):
    length = qkv.shape[0]
    heads = keep.shape[1]
    pairs = heads // 2

    def part(p):
        return pl.BlockSpec((length, 2 * HD), lambda h: (0, p * pairs + h))

    return pl.pallas_call(
        functools.partial(attend_kernel, chunk),
        grid=(pairs,),
        in_specs=[
            part(0),
            part(1),
            part(2),
            pl.BlockSpec((2, 2, length, length), lambda h: (0, h, 0, 0)),
        ],
        out_specs=[
            pl.BlockSpec((2, length, 2 * HD), lambda h: (0, 0, h)),
            pl.BlockSpec((2, 1, length), lambda h: (h, 0, 0)),
        ],
        out_shape=[
            jax.ShapeDtypeStruct((2, length, heads * HD), BF),
            jax.ShapeDtypeStruct((heads, 1, length), F32),
        ],
        scratch_shapes=[pltpu.VMEM((2, 2 * HD, length), BF)],
        compiler_params=pltpu.CompilerParams(vmem_limit_bytes=VMEM_LIMIT),
        name="attend",
        cost_estimate=work(4e9),
    )(qkv, qkv, qkv, keep)


def attend_back_kernel(
    chunk,
    q_ref,
    k_ref,
    v_ref,
    keep_ref,
    logsum_ref,
    context_ref,
    grad_ref,
    out_ref,
    turned,
    grad_keys,
    grad_values,
):
    length = q_ref.shape[0]
    width = 2 * HD
    pairs = pl.num_programs(0)
    queries = q_ref[...] * BF(0.125)
    key_rows = k_ref[...]
    values = v_ref[...]
    keys_turned = key_rows.T
    grads = [grad_ref[0], grad_ref[1]]
    product = sum(
        grads[view].astype(F32) * context_ref[view].astype(F32) for view in range(2)
    ).T
    for head in range(2):
        span = slice(head * HD, (head + 1) * HD)
        mine = head_lanes(queries.shape, head)
        own = jnp.where(mine, queries, BF(0))
        own_grads = [jnp.where(mine, grad, BF(0)) for grad in grads]
        inner = jnp.sum(product[span], axis=0, keepdims=True) * (1.0 / KEEP_SCALE)
        total_keys, total_values = None, None
        for start in range(0, length, chunk):
            part = slice(start, start + chunk)
            scores = dot(key_rows, own[part], 1, 1)
            scaled = jnp.exp(scores - logsum_ref[head, :, part])
            weighted = scaled.astype(BF)
            change = None
            for view in range(2):
                keep = keep_ref[view, head, :, part]
                more = dot(weighted * keep, grads[view][part], 1, 0)
                total_values = more if total_values is None else total_values + more
                term = dot(values, own_grads[view][part], 1, 1) * keep.astype(F32)
                change = term if change is None else change + term
            grad_scores = (scaled * (change - inner[:, part])).astype(BF)
            more = dot(grad_scores, queries[part], 1, 0)
            total_keys = more if total_keys is None else total_keys + more
            turned[span, part] = (dot(keys_turned[span], grad_scores, 1, 0) * 0.125).astype(BF)
        if head == 0:
            grad_keys[...] = total_keys
            grad_values[...] = total_values
        else:
            grad_keys[...] = jnp.where(mine, total_keys, grad_keys[...])
            grad_values[...] = jnp.where(mine, total_values, grad_values[...])
    pair = pl.program_id(0)

    def columns(p):
        return pl.ds(pl.multiple_of((p * pairs + pair) * width, width), width)

    out_ref[:, columns(0)] = turned[...].T
    out_ref[:, columns(1)] = grad_keys[...].astype(BF)
    out_ref[:, columns(2)] = grad_values[...].astype(BF)


def attend_back(qkv, keep, logsum, context, grad_context, chunk):
    length = qkv.shape[0]
    heads = keep.shape[1]
    pairs = heads // 2

    def part(p):
        return pl.BlockSpec((length, 2 * HD), lambda h: (0, p * pairs + h))

    sides = pl.BlockSpec((2, length, 2 * HD), lambda h: (0, 0, h))
    return pl.pallas_call(
        functools.partial(attend_back_kernel, chunk),
        grid=(pairs,),
        in_specs=[
            part(0),
            part(1),
            part(2),
            pl.BlockSpec((2, 2, length, length), lambda h: (0, h, 0, 0)),
            pl.BlockSpec((2, 1, length), lambda h: (h, 0, 0)),
            sides,
            sides,
        ],
        out_specs=pl.BlockSpec(qkv.shape, lambda h: (0, 0)),
        out_shape=jax.ShapeDtypeStruct(qkv.shape, BF),
        scratch_shapes=[
            pltpu.VMEM((2 * HD, length), BF),
            pltpu.VMEM((length, 2 * HD), F32),
            pltpu.VMEM((length, 2 * HD), F32),
        ],
        compiler_params=pltpu.CompilerParams(vmem_limit_bytes=VMEM_LIMIT),
        name="attend_back",
        cost_estimate=work(6e9),
    )(qkv, qkv, qkv, keep, logsum, context, grad_context)


GAIN_ONE, GAIN_TWO, OUT_BIAS, SHIFT_ONE, DOWN_BIAS, SHIFT_TWO = range(6)
ROWS = 128
LIGHT_ROWS = 256
COLUMNS = 256


def rows_block(width, rows=ROWS):
    return pl.BlockSpec((2, rows, width), lambda i: (0, i, 0))


def constant_block(shape):
    return pl.BlockSpec(shape, lambda i: (0,) * len(shape), pipeline_mode=pl.Buffered(1))


def flat(values):
    return values.reshape(values.shape[0] * values.shape[1], values.shape[2])


def norm_parts(values):
    center = values - jnp.mean(values, axis=-1, keepdims=True)
    spread = jnp.mean(center * center, axis=-1, keepdims=True)
    inverse = lax.rsqrt(spread + 1e-12)
    return center * inverse, inverse


def norm_back(grad, unit, inverse, gain):
    scaled = grad * gain
    mean = jnp.mean(scaled, axis=-1, keepdims=True)
    along = jnp.mean(scaled * unit, axis=-1, keepdims=True)
    return inverse * (scaled - mean - unit * along)


def kept(keep_ref):
    return flat(keep_ref[...]).astype(F32) * KEEP_SCALE


def row_copies(pieces, first, target, arrived):
    copies, start = [], 0
    for index, piece in enumerate(pieces):
        rows = piece.shape[0]
        copies.append(
            pltpu.make_async_copy(
                piece.at[:, pl.ds(first, target.shape[1])],
                target.at[pl.ds(start, rows)],
                arrived.at[index],
            )
        )
        start += rows
    return copies


def block_copies(blocks, places, half, target, arrived):
    rows = blocks.shape[1]
    return [
        pltpu.make_async_copy(
            blocks.at[places[half, index]],
            target.at[pl.ds(index * rows, rows)],
            arrived.at[index],
        )
        for index in range(target.shape[0] // rows)
    ]


def at_first_step(action):
    pl.when(pl.program_id(0) == 0)(action)


def start_all(copies):
    for copy in copies:
        copy.start()


def wait_all(copies):
    for copy in copies:
        copy.wait()


def far_spec():
    return pl.BlockSpec(memory_space=pl.ANY)


def first_norm_kernel(*refs):
    vectors_ref, own_ref, other_ref, token_ref, keep_ref = refs[:5]
    pieces, (unit_ref, inverse_ref, own_out, other_out), arrived = refs[5:-5], refs[-5:-1], refs[-1]
    count = len(pieces) // 2
    copies = row_copies(pieces[:count], 0, own_out, arrived.at[0]) + row_copies(
        pieces[count:], 0, other_out, arrived.at[1]
    )

    @at_first_step
    def _():
        start_all(copies)
        wait_all(copies)

    attn_out = dot(flat(own_ref[...]), own_out[...], 1, 1) + dot(
        flat(other_ref[...]), other_out[...], 1, 1
    )
    change = (attn_out + vectors_ref[OUT_BIAS : OUT_BIAS + 1]) * kept(keep_ref)
    token = token_ref[...].astype(F32)
    unit, inverse = norm_parts(change.reshape(unit_ref.shape) + token[None])
    unit_ref[...] = unit
    inverse_ref[...] = inverse


def first_norm(vectors, contexts, pieces, token, keep):
    _, length, width = keep.shape
    local = contexts[0].shape[2]
    whole = pl.BlockSpec((width, local), lambda i: (0, 0))
    return pl.pallas_call(
        first_norm_kernel,
        grid=(length // LIGHT_ROWS,),
        in_specs=[constant_block(vectors.shape)]
        + [rows_block(local, LIGHT_ROWS)] * 2
        + [pl.BlockSpec((LIGHT_ROWS, width), lambda i: (i, 0)), rows_block(width, LIGHT_ROWS)]
        + [far_spec()] * (len(pieces[0]) + len(pieces[1])),
        out_specs=[rows_block(width, LIGHT_ROWS), rows_block(1, LIGHT_ROWS), whole, whole],
        out_shape=[
            jax.ShapeDtypeStruct((2, length, width), F32),
            jax.ShapeDtypeStruct((2, length, 1), F32),
            jax.ShapeDtypeStruct((width, local), BF),
            jax.ShapeDtypeStruct((width, local), BF),
        ],
        scratch_shapes=[pltpu.SemaphoreType.DMA((2, len(pieces[0])))],
        compiler_params=pltpu.CompilerParams(vmem_limit_bytes=VMEM_LIMIT),
        name="first_norm",
        cost_estimate=work(3.5e9),
    )(vectors, *contexts, token, keep, *pieces[0], *pieces[1])


def hidden_kernel(first, *refs):
    places_ref, vectors_ref, bias_ref, unit_ref, keep_ref, blocks_ref = refs[:6]
    pieces, rest = refs[6:-16], refs[-16:]
    low_ref, active_own, active_other, slope_own, slope_other = rest[:5]
    unit_two_ref, inverse_two_ref, sum_ref = rest[5:8]
    up_own, up_other, down_own, down_other = rest[8:12]
    up_arrived, down_arrived = rest[12:14], rest[14:16]
    count = len(pieces) // 2
    up_copies = [
        row_copies(pieces[:count], first, up_own, up_arrived[0]),
        row_copies(pieces[count:], first, up_other, up_arrived[1]),
    ]
    down_copies = [
        block_copies(blocks_ref, places_ref, half, down, down_arrived[half])
        for half, down in enumerate((down_own, down_other))
    ]

    @at_first_step
    def _():
        for half in range(2):
            start_all(up_copies[half])
            start_all(down_copies[half])

    vector = lambda row: vectors_ref[row : row + 1]
    normed = flat(unit_ref[...]) * vector(GAIN_ONE) + vector(SHIFT_ONE)
    low = normed.astype(BF)
    low_ref[...] = low.reshape(low_ref.shape)
    hidden = up_own.shape[1]
    step = min(COLUMNS, hidden)
    total = vector(DOWN_BIAS)
    for half, (up, down, active_ref, slope_ref) in enumerate(
        (
            (up_own, down_own, active_own, slope_own),
            (up_other, down_other, active_other, slope_other),
        )
    ):
        at_first_step(functools.partial(wait_all, up_copies[half] + down_copies[half]))
        for start in range(0, hidden, step):
            part = slice(start, start + step)
            pre = dot(low, up[:, part], 1, 0) + bias_ref[half : half + 1, part]
            cumulative = 0.5 + 0.5 * lax.erf(pre * (0.5**0.5))
            density = jnp.exp(-0.5 * pre * pre) * (1.0 / (2.0 * np.pi) ** 0.5)
            active = (pre * cumulative).astype(BF)
            slope = (cumulative + pre * density).astype(BF)
            active_ref[:, :, part] = active.reshape(2, ROWS, step)
            slope_ref[:, :, part] = slope.reshape(2, ROWS, step)
            total = total + dot(active, down[:, part], 1, 1)
    unit, inverse = norm_parts((normed + total * kept(keep_ref)).reshape(unit_two_ref.shape))
    unit_two_ref[...] = unit
    inverse_two_ref[...] = inverse
    added_rows = jnp.sum(unit, axis=1)

    @at_first_step
    def _():
        sum_ref[...] = added_rows

    @pl.when(pl.program_id(0) > 0)
    def _():
        sum_ref[...] += added_rows


def weights_scratch(width, hidden, halves, pieces, blocks):
    return (
        [pltpu.VMEM((width, hidden), BF)] * (2 * halves)
        + [pltpu.SemaphoreType.DMA((pieces,))] * halves
        + [pltpu.SemaphoreType.DMA((blocks,))] * halves
    )


def smem_spec():
    return pl.BlockSpec(memory_space=pltpu.SMEM)


def hidden_units(vectors, bias, unit, keep, pieces, first, blocks, places):
    _, length, width = keep.shape
    hidden = blocks.shape[2]
    return pl.pallas_call(
        functools.partial(hidden_kernel, first),
        grid=(length // ROWS,),
        in_specs=[
            smem_spec(),
            constant_block(vectors.shape),
            constant_block(bias.shape),
            rows_block(width),
            rows_block(width),
        ]
        + [far_spec()] * (1 + len(pieces[0]) + len(pieces[1])),
        out_specs=[
            rows_block(width),
            rows_block(hidden),
            rows_block(hidden),
            rows_block(hidden),
            rows_block(hidden),
            rows_block(width),
            rows_block(1),
            pl.BlockSpec((2, width), lambda i: (0, 0)),
        ],
        out_shape=[
            jax.ShapeDtypeStruct((2, length, width), BF),
            jax.ShapeDtypeStruct((2, length, hidden), BF),
            jax.ShapeDtypeStruct((2, length, hidden), BF),
            jax.ShapeDtypeStruct((2, length, hidden), BF),
            jax.ShapeDtypeStruct((2, length, hidden), BF),
            jax.ShapeDtypeStruct((2, length, width), F32),
            jax.ShapeDtypeStruct((2, length, 1), F32),
            jax.ShapeDtypeStruct((2, width), F32),
        ],
        scratch_shapes=weights_scratch(width, hidden, 2, len(pieces[0]), places.shape[1]),
        compiler_params=pltpu.CompilerParams(vmem_limit_bytes=VMEM_LIMIT),
        name="hidden_units",
        cost_estimate=work(11e9),
    )(places, vectors, bias, unit, keep, blocks, *pieces[0], *pieces[1])


def second_back_kernel(
    vectors_ref, rows_ref, unit_ref, inverse_ref, keep_ref, second_ref, low_ref
):
    grad = norm_back(
        rows_ref[...][:, None, :],
        unit_ref[...],
        inverse_ref[...],
        vectors_ref[GAIN_TWO : GAIN_TWO + 1],
    )
    second_ref[...] = grad
    low_ref[...] = (grad * (keep_ref[...].astype(F32) * KEEP_SCALE)).astype(BF)


def second_back(vectors, rows, unit, inverse, keep):
    _, length, width = keep.shape
    return pl.pallas_call(
        second_back_kernel,
        grid=(length // LIGHT_ROWS,),
        in_specs=[
            constant_block(vectors.shape),
            constant_block(rows.shape),
            rows_block(width, LIGHT_ROWS),
            rows_block(1, LIGHT_ROWS),
            rows_block(width, LIGHT_ROWS),
        ],
        out_specs=[rows_block(width, LIGHT_ROWS)] * 2,
        out_shape=[
            jax.ShapeDtypeStruct(keep.shape, F32),
            jax.ShapeDtypeStruct(keep.shape, BF),
        ],
        compiler_params=pltpu.CompilerParams(vmem_limit_bytes=VMEM_LIMIT),
        name="second_back",
        cost_estimate=work(3e9),
    )(vectors, rows, unit, inverse, keep)


def half_back(grad, slope_ref, up, down, hidden_ref, hidden_sums_ref, back):
    hidden = up.shape[1]
    step = min(COLUMNS, hidden)
    for start in range(0, hidden, step):
        part = slice(start, start + step)
        slope = flat(slope_ref[:, :, part]).astype(F32)
        grad_hidden = (dot(grad, down[:, part], 1, 0) * slope).astype(BF)
        hidden_ref[:, :, part] = grad_hidden.reshape(2, ROWS, step)
        hidden_sums_ref[:, part] += jnp.sum(grad_hidden.astype(F32), axis=0, keepdims=True)
        back = back + dot(grad_hidden, up[:, part], 1, 1)
    return back


def own_back_kernel(first, *refs):
    places_ref, grad_ref, slope_ref, second_ref, blocks_ref = refs[:5]
    pieces = refs[5:-7]
    hidden_ref, back_ref, hidden_sums_ref, up, down, up_arrived, down_arrived = refs[-7:]
    copies = row_copies(pieces, first, up, up_arrived) + block_copies(
        blocks_ref, places_ref, 0, down, down_arrived
    )

    @at_first_step
    def _():
        start_all(copies)
        hidden_sums_ref[...] = jnp.zeros_like(hidden_sums_ref)
        wait_all(copies)

    back = half_back(
        flat(grad_ref[...]),
        slope_ref,
        up,
        down,
        hidden_ref,
        hidden_sums_ref,
        flat(second_ref[...]),
    )
    back_ref[...] = back.reshape(back_ref.shape)


def own_back(grad, slope, second, pieces, first, blocks, places):
    _, length, width = grad.shape
    hidden = blocks.shape[2]
    return pl.pallas_call(
        functools.partial(own_back_kernel, first),
        grid=(length // ROWS,),
        in_specs=[smem_spec(), rows_block(width), rows_block(hidden), rows_block(width)]
        + [far_spec()] * (1 + len(pieces)),
        out_specs=[
            rows_block(hidden),
            rows_block(width),
            pl.BlockSpec((1, hidden), lambda i: (0, 0)),
        ],
        out_shape=[
            jax.ShapeDtypeStruct((2, length, hidden), BF),
            jax.ShapeDtypeStruct((2, length, width), F32),
            jax.ShapeDtypeStruct((1, hidden), F32),
        ],
        scratch_shapes=weights_scratch(width, hidden, 1, len(pieces), places.shape[1]),
        compiler_params=pltpu.CompilerParams(vmem_limit_bytes=VMEM_LIMIT),
        name="own_back",
        cost_estimate=work(6e9),
    )(places, grad, slope, second, blocks, *pieces)


def other_back_kernel(first, *refs):
    places_ref, vectors_ref, grad_ref, slope_ref, before_ref = refs[:5]
    unit_ref, inverse_ref, keep_ref, blocks_ref = refs[5:9]
    pieces = refs[9:-9]
    hidden_ref, attn_ref, first_ref, sums_ref, hidden_sums_ref = refs[-9:-4]
    up, down, up_arrived, down_arrived = refs[-4:]
    copies = row_copies(pieces, first, up, up_arrived) + block_copies(
        blocks_ref, places_ref, 1, down, down_arrived
    )

    @at_first_step
    def _():
        start_all(copies)
        sums_ref[...] = jnp.zeros_like(sums_ref)
        hidden_sums_ref[...] = jnp.zeros_like(hidden_sums_ref)
        wait_all(copies)

    grad = flat(grad_ref[...])
    back = half_back(
        grad, slope_ref, up, down, hidden_ref, hidden_sums_ref, flat(before_ref[...])
    )
    unit = flat(unit_ref[...])
    grad_first = norm_back(
        back, unit, flat(inverse_ref[...]), vectors_ref[GAIN_ONE : GAIN_ONE + 1]
    )
    grad_attn = (grad_first * kept(keep_ref)).astype(BF)
    attn_ref[...] = grad_attn.reshape(attn_ref.shape)
    first_ref[...] = grad_first[:ROWS] + grad_first[ROWS:]
    for row, values in enumerate(
        (back * unit, back, grad_attn.astype(F32), grad.astype(F32))
    ):
        sums_ref[row : row + 1] += jnp.sum(values, axis=0, keepdims=True)


def other_back(vectors, grad, slope, before, unit, inverse, keep, pieces, first, blocks, places):
    _, length, width = keep.shape
    hidden = blocks.shape[2]
    return pl.pallas_call(
        functools.partial(other_back_kernel, first),
        grid=(length // ROWS,),
        in_specs=[
            smem_spec(),
            constant_block(vectors.shape),
            rows_block(width),
            rows_block(hidden),
            rows_block(width),
            rows_block(width),
            rows_block(1),
            rows_block(width),
        ]
        + [far_spec()] * (1 + len(pieces)),
        out_specs=[
            rows_block(hidden),
            rows_block(width),
            pl.BlockSpec((ROWS, width), lambda i: (i, 0)),
            pl.BlockSpec((4, width), lambda i: (0, 0)),
            pl.BlockSpec((1, hidden), lambda i: (0, 0)),
        ],
        out_shape=[
            jax.ShapeDtypeStruct((2, length, hidden), BF),
            jax.ShapeDtypeStruct((2, length, width), BF),
            jax.ShapeDtypeStruct((length, width), F32),
            jax.ShapeDtypeStruct((4, width), F32),
            jax.ShapeDtypeStruct((1, hidden), F32),
        ],
        scratch_shapes=weights_scratch(width, hidden, 1, len(pieces), places.shape[1]),
        compiler_params=pltpu.CompilerParams(vmem_limit_bytes=VMEM_LIMIT),
        name="other_back",
        cost_estimate=work(7e9),
    )(places, vectors, grad, slope, before, unit, inverse, keep, blocks, *pieces)


def loss_kernel(rows_ref, place_ref, loss_ref, grad_ref, *, scale):
    first, second = rows_ref[0], rows_ref[1]
    count = first.shape[0]
    inverse = [
        lax.rsqrt(jnp.sum(rows * rows, axis=-1, keepdims=True) + 1e-06) for rows in (first, second)
    ]
    units = [first * inverse[0], second * inverse[1]]
    logits = dot(units[0], units[1], 1, 1, EXACT) * 20.0
    peak = jnp.max(logits, axis=1, keepdims=True)
    powers = jnp.exp(logits - peak)
    total = jnp.sum(powers, axis=1, keepdims=True)
    row = lax.broadcasted_iota(jnp.int32, logits.shape, 0)
    column = lax.broadcasted_iota(jnp.int32, logits.shape, 1)
    on_diagonal = row == column
    losses = (
        peak
        + jnp.log(total)
        - jnp.sum(jnp.where(on_diagonal, logits, 0.0), axis=1, keepdims=True)
    )
    loss_ref[...] = jnp.sum(losses, axis=0, keepdims=True) * (1.0 / count)
    grad_logits = (powers / total - jnp.where(on_diagonal, 1.0, 0.0)) * (20.0 * scale / count)
    grad_units = [
        dot(grad_logits, units[1], 1, 0, EXACT),
        dot(grad_logits, units[0], 0, 0, EXACT),
    ]
    mine = lax.broadcasted_iota(jnp.int32, first.shape, 0) == place_ref[0]
    for view in range(2):
        along = jnp.sum(units[view] * grad_units[view], axis=-1, keepdims=True)
        grad_rows = (grad_units[view] - units[view] * along) * inverse[view]
        grad_ref[view : view + 1] = jnp.sum(
            jnp.where(mine, grad_rows, 0.0), axis=0, keepdims=True
        )


def loss_and_grad(rows, place, scale):
    width = rows.shape[-1]
    return pl.pallas_call(
        functools.partial(loss_kernel, scale=scale),
        in_specs=[
            pl.BlockSpec(memory_space=pltpu.VMEM),
            pl.BlockSpec(memory_space=pltpu.SMEM),
        ],
        out_shape=[
            jax.ShapeDtypeStruct((1, 1), F32),
            jax.ShapeDtypeStruct((2, width), F32),
        ],
        compiler_params=pltpu.CompilerParams(vmem_limit_bytes=VMEM_LIMIT),
        name="contrast",
    )(rows, place)


def adam_direction(weight, gradient, first_moment, second, decay_rate):
    new_first = 0.9 * first_moment + 0.1 * gradient
    new_second = 0.999 * second + 0.001 * gradient * gradient
    first_hat = new_first / (1.0 - 0.9**STEP)
    second_hat = new_second / (1.0 - 0.999**STEP)
    update = first_hat / (jnp.sqrt(second_hat) + 1e-06) + decay_rate * weight
    return (new_first, new_second, update)


LANES = 128
SQUARES = {"attn": 0, "out": 3, "up": 4, "down": 5}
MATRICES = 6


def in_lane(lane, value):
    lanes = lax.broadcasted_iota(jnp.int32, (1, LANES), 1)
    return jnp.where(lanes == lane, value, 0.0)


def pieces_of(matrix_ref):
    if len(matrix_ref.shape) == 3:
        return [(part,) for part in range(matrix_ref.shape[0])]
    return [(slice(None),)]


def adam_kernel(names, offsets, scale, *refs):
    count = len(names)
    ins, before_ref = refs[: 4 * count], refs[4 * count]
    outs, sums_ref = refs[4 * count + 1 : -1], refs[-1]
    sums = before_ref[...]
    for place, name in enumerate(names):
        weight_ref, grad_ref, first_ref, second_ref = ins[4 * place : 4 * place + 4]
        out_refs = outs[3 * place : 3 * place + 3]
        for part, where in enumerate(pieces_of(weight_ref)):
            weight = weight_ref[where]
            columns = weight.shape[-1]
            start = offsets[place] + part * columns
            grad = grad_ref[:, start : start + columns] * scale
            results = adam_direction(weight, grad, first_ref[where], second_ref[where], 0.01)
            for out_ref, result in zip(out_refs, results):
                out_ref[where] = result
            lane = SQUARES[name] + part
            sums = sums + in_lane(lane, jnp.sum(weight * weight))
            sums = sums + in_lane(lane + MATRICES, jnp.sum(results[2] * results[2]))
    sums_ref[...] = sums


def adam(names, offsets, matrices, before, scale):
    args = [array for matrix in matrices for array in matrix]
    shapes = [
        jax.ShapeDtypeStruct(matrix[0].shape, F32) for matrix in matrices for _ in range(3)
    ] + [jax.ShapeDtypeStruct(before.shape, F32)]
    out = pl.pallas_call(
        functools.partial(adam_kernel, names, offsets, scale),
        out_shape=shapes,
        compiler_params=pltpu.CompilerParams(vmem_limit_bytes=VMEM_LIMIT),
        name="adam",
    )(*args, before)
    return [out[3 * i : 3 * i + 3] for i in range(len(names))], out[-1]


def apply_kernel(names, scale, *refs):
    count = len(names)
    gathered_ref, pairs, rest = refs[0], refs[1 : 1 + 2 * count], refs[1 + 2 * count :]
    small_ins, outs = rest[:9], rest[9:]
    sums = jnp.sum(gathered_ref[:, 0], axis=0, keepdims=True)
    roots = jnp.sqrt(sums)
    for place, name in enumerate(names):
        weight_ref, update_ref = pairs[2 * place : 2 * place + 2]
        for part, where in enumerate(pieces_of(weight_ref)):
            lane = SQUARES[name] + part
            ratio = roots[:, lane : lane + 1] / roots[:, lane + MATRICES : lane + MATRICES + 1]
            outs[place][where] = weight_ref[where] - 0.25 * ratio * update_ref[where]
    slices = gathered_ref.shape[1] - 1
    line = 0
    for place in range(3):
        weight_ref, first_ref, second_ref = small_ins[3 * place : 3 * place + 3]
        rows, columns = weight_ref.shape
        lines = []
        for _ in range(rows):
            parts = []
            for _ in range(columns // LANES):
                device, slot = divmod(line, slices)
                parts.append(gathered_ref[device, 1 + slot : 2 + slot])
                line += 1
            lines.append(jnp.concatenate(parts, axis=1))
        grad = jnp.concatenate(lines, axis=0) * scale
        results = small_step(weight_ref[...], grad, first_ref[...], second_ref[...])
        for out_ref, result in zip(outs[count + 3 * place : count + 3 * place + 3], results):
            out_ref[...] = result


def apply_updates(names, gathered, pairs, small, scale):
    shapes = [jax.ShapeDtypeStruct(weight.shape, F32) for weight, _ in pairs] + [
        jax.ShapeDtypeStruct(array.shape, F32) for array in small
    ]
    return pl.pallas_call(
        functools.partial(apply_kernel, names, scale),
        out_shape=shapes,
        compiler_params=pltpu.CompilerParams(vmem_limit_bytes=VMEM_LIMIT),
        name="apply_updates",
    )(gathered, *(array for pair in pairs for array in pair), *small)


def small_step(weight, gradient, first_moment, second):
    new_first, new_second, update = adam_direction(weight, gradient, first_moment, second, 0.0)
    trust_ratio = jnp.sqrt(jnp.sum(weight * weight, axis=-1, keepdims=True)) / jnp.sqrt(
        jnp.sum(update * update, axis=-1, keepdims=True)
    )
    return (weight - 0.25 * trust_ratio * update, new_first, new_second)


def shards(
    tokens,
    prob_masks,
    branch_masks,
    attn_weight,
    attn_first,
    attn_second,
    out_weight,
    out_first,
    out_second,
    up_weight,
    up_first,
    up_second,
    down_weight,
    down_first,
    down_second,
    gains,
    gains_first,
    gains_second,
    shifts,
    shifts_first,
    shifts_second,
    hidden_bias,
    hidden_first,
    hidden_second,
):
    tensor_count = lax.axis_size("tensor")
    tensor_rank = lax.axis_index("tensor")
    data_count = lax.axis_size("dp")
    data_rank = lax.axis_index("dp")
    seq_local, half_len, width = tokens.shape
    assert tensor_count == 2 and seq_local == 2
    seq_len = half_len * tensor_count
    heads_local = prob_masks.shape[2]
    local_width = heads_local * HD
    hidden_local = up_weight.shape[1]
    rows_local = width // data_count
    scale_loss = 64.0 * data_count * seq_local * seq_len
    chunk = min(256, seq_len)
    is_first = tensor_rank == 0

    def in_order(mine, others, axis):
        return jnp.where(
            is_first,
            jnp.concatenate([mine, others], axis=axis),
            jnp.concatenate([others, mine], axis=axis),
        )

    def of_rank(whole, axis, length):
        mine = lax.dynamic_slice_in_dim(whole, tensor_rank * length, length, axis)
        others = lax.dynamic_slice_in_dim(whole, (1 - tensor_rank) * length, length, axis)
        return mine, others

    own_tokens, send_tokens = of_rank(tokens, 0, 1)
    words = jnp.pad(
        jnp.swapaxes(prob_masks.astype(jnp.int16), 3, 4),
        ((0, 0), (0, 0), (0, 0), (0, -prob_masks.shape[4] % 16), (0, 0)),
    )
    own_words, send_words = of_rank(words, 1, 1)
    branch_words = jnp.pad(
        jnp.swapaxes(branch_masks.astype(jnp.int16), 3, 4),
        ((0, 0), (0, 0), (0, 0), (0, -branch_masks.shape[4] % 16), (0, 0)),
    )
    own_branch, send_branch = of_rank(branch_words, 2, 1)

    order = jnp.asarray(np.array(gathered_order(data_count), np.int32))
    owner = jnp.bitwise_xor(order, data_rank)
    feature = (owner[:, None] * rows_local + jnp.arange(rows_local, dtype=jnp.int32)).reshape(-1)
    places = lax.broadcasted_iota(jnp.int32, (width, width), 0)
    to_own = (places == feature[None, :]).astype(F32)
    to_own_low = to_own.astype(BF)

    attn_block = attn_weight.astype(BF).reshape(rows_local, 3 * local_width)
    out_block = out_weight.astype(BF).T
    up_block = up_weight.astype(BF)
    down_block = down_weight.astype(BF).T
    device_count = data_count * tensor_count
    down_blocks = lax.all_gather(down_block, ("dp", "tensor"), axis=0, tiled=False)
    branch_rows_padded = branch_words.shape[3]
    word = feature // BRANCH_BITS
    bit = feature % BRANCH_BITS
    high = bit >= LOW_BITS
    row = jnp.where(high, word + branch_rows_padded, word)
    power = jnp.exp2(-jnp.where(high, bit - LOW_BITS, bit).astype(F32))
    branch_select = jnp.where(
        lax.broadcasted_iota(jnp.int32, (2 * branch_rows_padded, width), 0) == row[None, :],
        power[None, :],
        0.0,
    ).astype(BF)

    bias_q = of_rank(shifts[0], 0, local_width)
    bias_v = of_rank(shifts[1], 0, local_width)

    def project(half, rows, matrix):
        bias = jnp.concatenate([bias_q[half], jnp.zeros_like(bias_q[half]), bias_v[half]])
        return (dot(rows, matrix, 1, 0) + bias).astype(BF)

    first_bit, *later_bits = [bit for group in upper_groups() for bit in group]
    token_other = swap_tensor(send_tokens)
    attn_quarter = gather_upper(attn_block)
    wide_quarter = jnp.concatenate([out_block, up_block], axis=1)
    wide_sent = swap_dp(wide_quarter, 1 << first_bit)
    own_keep = prob_keep(own_words[:, 0], seq_len)
    attn_quarter, own_keep, wide_sent = together(attn_quarter, own_keep, wide_sent)

    attn_beside, attn_across = swap_dp(attn_quarter, 2), swap_tensor(attn_quarter)
    wide_quarter = joined([wide_quarter, wide_sent])
    for bit in later_bits[:-1]:
        wide_quarter = gather_bit(wide_quarter, bit)
    wide_sent = swap_dp(wide_quarter, 1 << later_bits[-1])
    token_rows = in_order(own_tokens[0], token_other[0], 0)
    token_own = dot(token_rows, to_own_low, 1, 0).astype(BF)
    attn_beside, attn_across, token_own, wide_quarter = together(
        attn_beside, attn_across, token_own, wide_quarter
    )

    attn_corner = swap_dp(attn_across, 2)
    other_words = swap_tensor(tie(send_words, attn_across))
    attn_near = gather_core((attn_quarter, attn_beside))
    qkv_own = project(0, token_own, attn_near)
    attn_corner, qkv_own, wide_sent, wide_quarter = together(
        attn_corner, qkv_own, wide_sent, wide_quarter
    )

    wide_quarter = joined([wide_quarter, wide_sent])
    wide_beside = swap_dp(wide_quarter, 2)
    wide_across = swap_tensor(wide_quarter)
    attended = attend(qkv_own, own_keep, chunk)
    other_keep = prob_keep(other_words[:, 0], seq_len)
    attn_far = gather_core((attn_across, attn_corner))
    qkv_other = project(1, token_own, attn_far)
    attended, other_keep, qkv_other, wide_beside, wide_across = together(
        attended, other_keep, qkv_other, wide_beside, wide_across
    )

    wide_corner = swap_dp(wide_across, 2)
    branch_other = swap_tensor(tie(send_branch, wide_across))
    attended_other = attend(qkv_other, other_keep, chunk)
    branch_rows = in_order(own_branch[:, :, 0], branch_other[:, :, 0], 3)
    keeps = branch_keep(branch_rows, branch_select)
    down_places = jnp.stack(
        [owner * tensor_count + tensor_rank, owner * tensor_count + (1 - tensor_rank)]
    ).astype(jnp.int32)
    down_blocks, down_places = whole_tiles(
        down_blocks.reshape(device_count, rows_local, hidden_local), down_places
    )
    wide_corner, attended_other, keeps, down_blocks = together(
        wide_corner, attended_other, keeps, down_blocks
    )
    attn_low = [attn_near, attn_far]
    wide_pieces = [
        quarters + tuple(swap_dp(quarter, 1) for quarter in quarters)
        for quarters in ((wide_quarter, wide_beside), (wide_across, wide_corner))
    ]
    qkv = [qkv_own, qkv_other]
    contexts = [attended[0], attended_other[0]]
    logsums = [attended[1], attended_other[1]]
    keep_halves = (own_keep, other_keep)
    vectors = dot(jnp.concatenate([gains, shifts[2:6]], axis=0), to_own, 1, 0, EXACT)
    context_flat = [c.reshape(2 * seq_len, local_width) for c in contexts]
    unit_one, inverse_one, *out_low = first_norm(
        vectors, contexts, wide_pieces, token_own, keeps[0]
    )
    hidden_halves = jnp.stack(of_rank(hidden_bias, 0, hidden_local))
    normed_low, active_own, active_other, slope_own, slope_other, unit_two, inverse_two, unit_sum = hidden_units(
        vectors,
        hidden_halves,
        unit_one,
        keeps[1],
        wide_pieces,
        local_width,
        down_blocks,
        down_places,
    )
    normed_low = normed_low.reshape(2 * seq_len, width)
    active = [a.reshape(2 * seq_len, hidden_local) for a in (active_own, active_other)]
    gain_two = vectors[GAIN_TWO]
    shift_two = vectors[SHIFT_TWO]
    pooled = unit_sum * gain_two / seq_len + shift_two
    pooled_rows = dot(pooled, to_own, 1, 1, EXACT)
    everyone = jnp.swapaxes(everyones(pooled_rows), 0, 1)
    place = (data_rank * tensor_count + tensor_rank).astype(jnp.int32).reshape(1)
    loss_value, grad_pooled = loss_and_grad(everyone, place, scale_loss)
    grad_rows = dot(grad_pooled, to_own, 1, 0, EXACT) / seq_len

    grad_shift_two = jnp.sum(grad_rows, axis=0) * seq_len
    grad_gain_two = jnp.sum(grad_rows * unit_sum, axis=0)
    grad_second, grad_ffn = second_back(vectors, grad_rows, unit_two, inverse_two, keeps[1])
    grad_ffn_flat = grad_ffn.reshape(2 * seq_len, width)
    half_width, quarter_width = width // 2, width // 4

    def weight_grads(left, right):
        return (
            dot(left[:, :half_width], right, 0, 0),
            dot(left[:, half_width:], right, 0, 0),
        )

    def both_cores(grads):
        kept, sent = grads
        return kept, swap_dp(sent, 1)

    def rows_of(parts, first):
        return tuple(
            part[:quarter_width] if first else part[quarter_width:] for part in parts
        )

    def low_sum(parts):
        return added(*parts).astype(BF)

    def context_back(half, grad_rows):
        return dot(grad_rows, out_low[half], 1, 0).astype(BF)

    def queries_back(half, grad_context):
        return attend_back(
            qkv[half],
            keep_halves[half],
            logsums[half],
            contexts[half],
            grad_context.reshape(2, seq_len, local_width),
            chunk,
        )

    eighth = quarter_width // 2

    def corner_out(other):
        return (
            swap_tensor(added(*(p[quarter_width : quarter_width + eighth] for p in other)).astype(BF)),
            swap_dp(added(*(p[quarter_width + eighth :] for p in other)).astype(BF), 2),
        )

    def sides_sent(own, other, corner):
        from_tensor, from_beside = corner
        to_tensor = jnp.concatenate(
            [
                low_sum(tuple(p[:eighth] for p in other)),
                low_sum(tuple(p[eighth:quarter_width] for p in other) + (from_beside,)),
            ]
        )
        to_beside = jnp.concatenate(
            [
                low_sum(
                    tuple(p[quarter_width : quarter_width + eighth] for p in own) + (from_tensor,)
                ),
                low_sum(tuple(p[quarter_width + eighth :] for p in own)),
            ]
        )
        return to_tensor, to_beside

    def sides_out(sent):
        return swap_tensor(sent[0]), swap_dp(sent[1], 2)

    def side_by_side(first, second):
        return tuple(jnp.concatenate(pair, axis=1) for pair in zip(first, second))

    rows_shape = (2, seq_len, width)
    down_other = weight_grads(grad_ffn_flat, active[1])
    down_own = weight_grads(grad_ffn_flat, active[0])
    down_other, down_own, grad_ffn_flat = together(down_other, down_own, grad_ffn_flat)

    down_other, down_own = both_cores(down_other), both_cores(down_own)
    grad_hidden_own, back, hidden_sums_own = own_back(
        grad_ffn_flat.reshape(rows_shape),
        slope_own,
        grad_second,
        wide_pieces[0],
        local_width,
        down_blocks,
        down_places,
    )
    down_other, down_own, back = together(down_other, down_own, back)

    down_corner = corner_out(down_other)
    grad_hidden_other, grad_attn, grad_first, column_sums, hidden_sums_other = other_back(
        vectors,
        grad_ffn_flat.reshape(rows_shape),
        slope_other,
        back,
        unit_one,
        inverse_one,
        keeps[0],
        wide_pieces[1],
        local_width,
        down_blocks,
        down_places,
    )
    down_corner, grad_hidden_other, grad_attn = together(down_corner, grad_hidden_other, grad_attn)
    grad_attn_flat = grad_attn.reshape(2 * seq_len, width)

    down_sent = sides_sent(down_own, down_other, down_corner)
    up_other = weight_grads(
        tie(normed_low, *down_sent), grad_hidden_other.reshape(2 * seq_len, hidden_local)
    )
    up_own = weight_grads(normed_low, grad_hidden_own.reshape(2 * seq_len, hidden_local))
    up_other, up_own = both_cores(up_other), both_cores(up_own)
    out_other = both_cores(weight_grads(grad_attn_flat, context_flat[1]))
    out_own = both_cores(weight_grads(grad_attn_flat, context_flat[0]))
    down_sides = sides_out(down_sent)
    context_other = context_back(1, grad_attn_flat)
    down_sides, up_other, up_own, out_other, out_own, context_other = together(
        down_sides, up_other, up_own, out_other, out_own, context_other
    )

    wide_other, wide_own = side_by_side(out_other, up_other), side_by_side(out_own, up_own)
    wide_corner = corner_out(wide_other)
    down_parts = rows_of(down_own, True) + down_sides
    grad_other = queries_back(1, context_other)
    wide_corner, grad_other = together(wide_corner, grad_other)

    wide_leaving = sides_sent(wide_own, wide_other, wide_corner)
    wide_sides = sides_out(wide_leaving)
    down_reduced = upper_parts(down_parts)
    attn_other = both_cores(weight_grads(token_own, tie(grad_other, *wide_leaving)))
    context_own = context_back(0, grad_attn_flat)
    token_back = dot(grad_other, attn_low[1], 1, 1) + grad_first
    attn_other, context_own, token_back, wide_sides, down_reduced = together(
        attn_other, context_own, token_back, wide_sides, down_reduced
    )

    attn_sent = low_sum(attn_other)
    attn_across = swap_tensor(attn_sent)
    wide_reduced = upper_parts(rows_of(wide_own, True) + wide_sides)
    grad_own = queries_back(0, tie(context_own, attn_sent))
    attn_own = weight_grads(token_own, grad_own)
    attn_across, wide_reduced, attn_own, grad_own = together(
        attn_across, wide_reduced, attn_own, grad_own
    )

    attn_own = both_cores(attn_own)
    token_back = token_back + dot(grad_own, attn_low[0], 1, 1)
    attn_own, token_back = together(attn_own, token_back)
    attn_own = attn_own + (attn_across,)
    attn_sent = low_sum(rows_of(attn_own, False))
    attn_beside = swap_dp(attn_sent, 2)
    token_grad = dot(tie(token_back, attn_sent), to_own, 1, 1, EXACT)
    grad_own = tie(grad_own, attn_sent)
    hidden_sums = (hidden_sums_own[0], hidden_sums_other[0])
    grad_qkv = [grad_own, grad_other]
    bias_sums = [jnp.sum(grad_qkv[half].astype(F32), axis=0) for half in range(2)]
    query_row = in_order(bias_sums[0][:local_width], bias_sums[1][:local_width], 0)
    value_row = in_order(bias_sums[0][2 * local_width :], bias_sums[1][2 * local_width :], 0)
    hidden_row = in_order(hidden_sums[0], hidden_sums[1], 0)
    feature_rows = dot(
        jnp.stack(
            [
                column_sums[0],
                grad_gain_two,
                column_sums[2],
                column_sums[1],
                column_sums[3],
                grad_shift_two,
            ]
        ),
        to_own,
        1,
        1,
        EXACT,
    )
    small = jnp.concatenate(
        [
            feature_rows[:2],
            query_row[None],
            value_row[None],
            feature_rows[2:],
            hidden_row.reshape(-1, width),
        ],
        axis=0,
    )
    small_sums = slices_summed(small.reshape(-1)).reshape(-1, LANES)
    attn_beside, token_grad, small_sums = together(attn_beside, token_grad, small_sums)
    attn_reduced = added(*upper_parts(rows_of(attn_own, True) + (attn_beside,)))
    down_reduced, wide_reduced = added(*down_reduced), added(*wide_reduced)
    own_half, send_half = of_rank(token_grad, 0, half_len)
    grad_tokens = in_order(own_half[None], swap_tensor(send_half.astype(BF))[None].astype(F32), 0)

    inverse_scale = 1.0 / scale_loss

    def turned(*arrays):
        return [array.T for array in arrays]

    def parts_first(*arrays):
        return [jnp.transpose(array, (1, 0, 2)) for array in arrays]

    down_own_weight, down_firsts, down_seconds = turned(down_weight, down_first, down_second)
    out_own_weight, out_firsts, out_seconds = turned(out_weight, out_first, out_second)
    attn_parts, attn_firsts, attn_seconds = parts_first(attn_weight, attn_first, attn_second)
    (down_new,), sums = adam(
        ("down",),
        (0,),
        ((down_own_weight, down_reduced, down_firsts, down_seconds),),
        jnp.zeros((1, LANES), F32),
        inverse_scale,
    )
    (up_new, out_new, attn_new), sums = adam(
        ("up", "out", "attn"),
        (local_width, 0, 0),
        (
            (up_weight, wide_reduced, up_first, up_second),
            (out_own_weight, wide_reduced, out_firsts, out_seconds),
            (attn_parts, attn_reduced, attn_firsts, attn_seconds),
        ),
        sums,
        inverse_scale,
    )
    hidden_args = [array.reshape(1, -1) for array in (hidden_bias, hidden_first, hidden_second)]
    gathered = everyones(jnp.concatenate([sums, small_sums], axis=0))
    gathered, grad_tokens = together(gathered, grad_tokens)
    (
        new_attn,
        new_out,
        new_up,
        new_down,
        new_gains,
        new_gains_first,
        new_gains_second,
        new_shifts,
        new_shifts_first,
        new_shifts_second,
        new_hidden,
        new_hidden_first,
        new_hidden_second,
    ) = apply_updates(
        ("attn", "out", "up", "down"),
        gathered,
        (
            (attn_parts, attn_new[2]),
            (out_own_weight, out_new[2]),
            (up_weight, up_new[2]),
            (down_own_weight, down_new[2]),
        ),
        (gains, gains_first, gains_second, shifts, shifts_first, shifts_second, *hidden_args),
        inverse_scale,
    )
    new_hidden, new_hidden_first, new_hidden_second = (
        array.reshape(-1) for array in (new_hidden, new_hidden_first, new_hidden_second)
    )
    new_attn, attn_new_first, attn_new_second = parts_first(new_attn, attn_new[0], attn_new[1])
    new_out, out_new_first, out_new_second = turned(new_out, out_new[0], out_new[1])
    new_down, down_new_first, down_new_second = turned(new_down, down_new[0], down_new[1])
    up_new_first, up_new_second = up_new[:2]
    return (
        loss_value.reshape(()),
        grad_tokens,
        new_attn,
        attn_new_first,
        attn_new_second,
        new_out,
        out_new_first,
        out_new_second,
        new_up,
        up_new_first,
        up_new_second,
        new_down,
        down_new_first,
        down_new_second,
        new_gains,
        new_gains_first,
        new_gains_second,
        new_shifts,
        new_shifts_first,
        new_shifts_second,
        new_hidden,
        new_hidden_first,
        new_hidden_second,
    )


def solution(mesh):
    row_split = P("dp", None, "tensor")
    column_split = P("tensor", "dp")
    matrix_split = P("dp", "tensor")
    return jax.shard_map(
        shards,
        mesh=mesh,
        in_specs=(
            P("dp", "tensor", None),
            P(None, "dp", "tensor", None, None),
            P(None, None, "dp", "tensor", None),
        )
        + (row_split,) * 3
        + (column_split,) * 3
        + (matrix_split,) * 3
        + (column_split,) * 3
        + (P(),) * 9,
        out_specs=(P(), P("dp", "tensor", None))
        + (row_split,) * 3
        + (column_split,) * 3
        + (matrix_split,) * 3
        + (column_split,) * 3
        + (P(),) * 9,
        check_vma=False,
    )
```
